32 devices in a mesh: row: 8 (over y, x, core), col: 4 (over z).
Axes of the slice: x: 2, y: 2, z: 4, core: 2. Of those that a mesh axis runs over, the one named last changes fastest.
Arguments:
- tokens: bfloat16 [32768, 768], P(('row', 'col')), may hold values from -6 to 6
- segment: int32 [32, 1024], replicated, may hold values from 0 to 63, never falling along the last dimension, each value on 1 to 512 neighbouring positions
- w_qkv: bfloat16 [768, 2304], P('row', 'col'), may hold values from -0.21875 to 0.21875
- w_out: bfloat16 [768, 768], P('row', 'col'), may hold values from -0.875 to 0.875
- w_up: bfloat16 [768, 3072], P('row', 'col'), may hold values from -0.21875 to 0.21875
- w_down: bfloat16 [3072, 768], P('row', 'col'), may hold values from -0.109375 to 0.109375
- bias_query: float32 [768], replicated, may hold values from -3 to 3
- bias_value: float32 [768], replicated, may hold values from -3 to 3
- bias_out: float32 [768], replicated, may hold values from -3 to 3
- gain_attn: float32 [768], replicated, may hold values from 0.25 to 1.75
- shift_attn: float32 [768], replicated, may hold values from -3 to 3
- bias_up: float32 [3072], replicated, may hold values from -3 to 3
- bias_down: float32 [768], replicated, may hold values from -3 to 3
- gain_ffn: float32 [768], replicated, may hold values from 0.25 to 1.75
- shift_ffn: float32 [768], replicated, may hold values from -3 to 3
- cotangent: bfloat16 [32768, 768], P(('row', 'col')), may hold values from -6 to 6
Outputs:
- layer_out: bfloat16 [32768, 768], P(('row', 'col'))
- grad_tokens: float32 [32768, 768], P(('row', 'col'))
- grad_qkv: float32 [768, 2304], P('row', 'col')
- grad_out: float32 [768, 768], P('row', 'col')
- grad_up: float32 [768, 3072], P('row', 'col')
- grad_down: float32 [3072, 768], P('row', 'col')
- grad_bias_query: float32 [768], replicated
- grad_bias_value: float32 [768], replicated
- grad_bias_out: float32 [768], replicated
- grad_gain_attn: float32 [768], replicated
- grad_shift_attn: float32 [768], replicated
- grad_bias_up: float32 [3072], replicated
- grad_bias_down: float32 [768], replicated
- grad_gain_ffn: float32 [768], replicated
- grad_shift_ffn: float32 [768], replicated
The draws below stay inside these ranges and needn't reach their ends.
Inputs may be any that keep to these rules, and one draw needn't show every extreme that they name: `segment`: within each packed sequence the document numbers never fall; a document is a run of equal numbers, and some document has 512 tokens.
All inputs are finite; a program needn't handle non-finite values.
Results may differ from the reference program's by a relative error of at most 0.019.
Values may be sent and summed in bfloat16 or wider, within the bound.
A program may use at most 192 MiB of HBM per device.

```python
import math
import jax
import jax.numpy as jnp
import numpy as np
from jax import lax

D = 768
HEADS = 12
HEAD_DIM = 64
FF = 3072
LEN = 1024
NSEQ = 32
TOKENS = 32768


def level_of(rng, shape, pieces, smallest, high):
    factor_of, own = 1.0, jax.random.fold_in(rng, 6)
    for position, shards_of in pieces:
        steps = jnp.exp(jax.random.uniform(jax.random.fold_in(own, position), (shards_of,), jnp.float32, smallest / len(pieces), high / len(pieces)))
        factor_of = factor_of * jnp.repeat(steps, shape[position] // shards_of).reshape([-1 if axis == position else 1 for axis in range(len(shape))])
    return factor_of


def profile(count, total, limit, lean):
    weights = [(1 << 20) // math.isqrt(grade ** lean) + 1 for grade in range(2, count + 1)]
    rest, given = total - limit - (count - 1), [1] * (count - 1)
    while rest > 0:
        candidates = [i for i in range(count - 1) if given[i] < limit]
        whole, remaining = sum([weights[i] for i in candidates]), rest
        for i in candidates:
            more = min(limit - given[i], max(1, remaining * weights[i] // whole), rest)
            given[i] = given[i] + more
            rest = rest - more
    return np.array([limit] + given)


def ragged_sizes(key, amount, total, most, skew):
    if amount == 2:
        one = jax.random.randint(key, (), max(1, total - most), min(most, total - 1) + 1)
        return jnp.stack([one, total - one])
    sizes = jnp.asarray(profile(amount, total, most, skew), jnp.int32)
    twos = (amount - 1) // 2
    donor, taker = sizes[1:1 + 2 * twos:2], sizes[2:2 + 2 * twos:2]
    slack = jnp.minimum(donor - 1, most - taker)
    shifted = jax.random.randint(jax.random.fold_in(key, 1), (twos,), 0, 1 << 20) % (slack + 1)
    sizes = sizes.at[1:1 + 2 * twos:2].set(donor - shifted).at[2:2 + 2 * twos:2].set(taker + shifted)
    return sizes[jax.random.permutation(jax.random.fold_in(key, 2), amount)]


def centred(own_key, extent, scale, most, shards=(), dtype=jnp.bfloat16):
    values = scale * jax.random.normal(own_key, extent, jnp.float32)
    if shards:
        values = values * level_of(own_key, extent, shards, -0.22, 0.18)
    return jnp.clip(values, -most, most).astype(dtype)


def setup_inputs(seed: int = 0) -> dict:
    splits = jax.random.split(jax.random.key(seed), 17)
    return {
        "tokens": centred(splits[0], (TOKENS, D), 1.0, 6.0, ((0, 32),)),
        "segment": jax.vmap(lambda own: jnp.searchsorted(jnp.cumsum(ragged_sizes(own, LEN // 16, LEN, LEN // 2, 2)), jnp.arange(LEN), side="right"))(jax.random.split(splits[1], NSEQ)).reshape((NSEQ, LEN)).astype(jnp.int32),
        "w_qkv": centred(splits[2], (D, 3 * D), D ** -0.5, 0.21875, ((0, 8), (1, 4))),
        "w_out": centred(splits[3], (D, D), (D // 16) ** -0.5, 0.875, ((0, 8), (1, 4))),
        "w_up": centred(splits[4], (D, FF), D ** -0.5, 0.21875, ((0, 8), (1, 4))),
        "w_down": centred(splits[5], (FF, D), FF ** -0.5, 0.109375, ((0, 8), (1, 4))),
        "bias_query": centred(splits[6], (D,), 0.5, 3.0, (), jnp.float32),
        "bias_value": centred(splits[7], (D,), 0.5, 3.0, (), jnp.float32),
        "bias_out": centred(splits[8], (D,), 0.5, 3.0, (), jnp.float32),
        "gain_attn": jnp.clip(1.0 + 0.15 * jax.random.normal(splits[9], (D,), jnp.float32), 0.25, 1.75),
        "shift_attn": centred(splits[10], (D,), 0.5, 3.0, (), jnp.float32),
        "bias_up": centred(splits[11], (FF,), 0.5, 3.0, (), jnp.float32),
        "bias_down": centred(splits[12], (D,), 0.5, 3.0, (), jnp.float32),
        "gain_ffn": jnp.clip(1.0 + 0.15 * jax.random.normal(splits[13], (D,), jnp.float32), 0.25, 1.75),
        "shift_ffn": centred(splits[14], (D,), 0.5, 3.0, (), jnp.float32),
        "cotangent": centred(splits[15], (TOKENS, D), 1.0, 6.0, ((0, 32),)),
    }


@jax.custom_vjp
def low(v):
    return lax.optimization_barrier(v.astype(jnp.bfloat16)).astype(jnp.float32)

@jax.custom_vjp
def low_back(v):
    return v

def low_keep(v):
    return (low(v), None)

def low_pass(kept, grad):
    return (grad,)

def back_keep(v):
    return (v, None)

def back_low(kept, grad):
    return (low(grad),)
low.defvjp(low_keep, low_pass)
low_back.defvjp(back_keep, back_low)
highest = lax.Precision.HIGHEST
norm_eps = 1e-05
masked_score = -1e+30

def norm_rows(resid, gain, shift):
    centre = resid - lax.optimization_barrier(jnp.mean(resid, axis=-1, keepdims=True))
    spread = lax.optimization_barrier(jnp.mean(centre * centre, axis=-1, keepdims=True))
    return centre * lax.rsqrt(spread + norm_eps) * gain + shift

def pair_attend(items):
    query_part, key_part, value_part, segrow = items
    query_heads = query_part.reshape(LEN, 2, HEAD_DIM)
    key_heads = key_part.reshape(LEN, 2, HEAD_DIM)
    value_heads = value_part.reshape(LEN, 2, HEAD_DIM)
    raw = low_back(jnp.einsum('qhd,khd->hqk', query_heads, key_heads, precision=highest))
    same = segrow[:, None] == segrow[None, :]
    scores = jnp.where(same[None], raw * HEAD_DIM ** (-0.5), masked_score)
    peak = lax.optimization_barrier(jnp.max(scores, axis=-1, keepdims=True))
    expo = jnp.exp(scores - peak)
    prob = expo / lax.optimization_barrier(jnp.sum(expo, axis=-1, keepdims=True))
    result = jnp.einsum('hqk,khd->qhd', low(prob), value_heads, precision=highest)
    return result.reshape(LEN, 2 * HEAD_DIM)

def layer(tokens_f, segs, w_qkv, w_out, w_up, w_down, bias_query, bias_value, bias_out, gain_attn, shift_attn, bias_up, bias_down, gain_ffn, shift_ffn):
    rows = tokens_f.shape[0]
    nseqs = rows // LEN
    pairs = HEADS // 2
    width = 2 * HEAD_DIM
    projected = low_back(jnp.dot(tokens_f, w_qkv, precision=highest))
    queries = low(projected[:, :D] + bias_query)
    keys_all = low(projected[:, D:2 * D])
    values = low(projected[:, 2 * D:] + bias_value)

    def split_pairs(field):
        return field.reshape(nseqs, LEN, pairs, width).transpose(0, 2, 1, 3).reshape(nseqs * pairs, LEN, width)
    seg_items = jnp.repeat(segs, pairs, axis=0)
    context = lax.map(jax.checkpoint(pair_attend), (split_pairs(queries), split_pairs(keys_all), split_pairs(values), seg_items))
    context = context.reshape(nseqs, pairs, LEN, width).transpose(0, 2, 1, 3).reshape(rows, D)
    context = low(low_back(context))
    attended = low_back(jnp.dot(context, w_out, precision=highest)) + bias_out
    hidden = norm_rows(tokens_f + attended, gain_attn, shift_attn)
    upward = low_back(jnp.dot(low(hidden), w_up, precision=highest)) + bias_up
    active = low(jax.nn.gelu(upward, approximate=False))
    ffn_out = low_back(jnp.dot(active, w_down, precision=highest)) + bias_down
    return norm_rows(hidden + ffn_out, gain_ffn, shift_ffn)

def reference(tokens, segment, w_qkv, w_out, w_up, w_down, bias_query, bias_value, bias_out, gain_attn, shift_attn, bias_up, bias_down, gain_ffn, shift_ffn, cotangent):
    params = tuple((item.astype(jnp.float32) for item in (w_qkv, w_out, w_up, w_down, bias_query, bias_value, bias_out, gain_attn, shift_attn, bias_up, bias_down, gain_ffn, shift_ffn)))
    per_group = 4
    groups = NSEQ // per_group
    tok_groups = tokens.astype(jnp.float32).reshape(groups, per_group * LEN, D)
    cot_groups = cotangent.astype(jnp.float32).reshape(groups, per_group * LEN, D)
    seg_groups = segment.reshape(groups, per_group, LEN)

    def group_step(summed, inputs_now):
        tok_now, cot_now, seg_now = inputs_now

        def forward_now(tok_value, *weights):
            return layer(tok_value, seg_now, *weights)
        result, pullback = jax.vjp(forward_now, tok_now, *params)
        grads = pullback(cot_now)
        summed = tuple((left + right for left, right in zip(summed, grads[1:])))
        return (summed, (result.astype(jnp.bfloat16), grads[0]))
    zeros = tuple((jnp.zeros_like(item) for item in params))
    summed, (outputs, grad_toks) = lax.scan(group_step, zeros, (tok_groups, cot_groups, seg_groups))
    return (outputs.reshape(TOKENS, D), grad_toks.reshape(TOKENS, D), summed[0], summed[1], summed[2], summed[3], summed[4], summed[5], summed[6], summed[7], summed[8], summed[9], summed[10], summed[11], summed[12])
```

```python
import jax
import jax.numpy as jnp
from jax import lax
from jax.experimental import pallas as pl
from jax.experimental.pallas import tpu as pltpu
from jax.sharding import PartitionSpec as P

HEADS = 12
HEAD_DIM = 64
LEN = 1024


norm_eps = 1e-05
masked_score = -1e30


def gather_block(blocks):
    widened = (
        lax.all_gather(blocks[0], "col", axis=1, tiled=True),
        lax.all_gather(blocks[1], "col", axis=1, tiled=True),
    )
    return (
        lax.all_gather(widened[0], "row", axis=0, tiled=True),
        lax.all_gather(widened[1], "row", axis=0, tiled=True),
    )


def reduce_grads(grads):
    def one(grad):
        narrowed = lax.psum_scatter(
            grad.astype(jnp.bfloat16), "row", scatter_dimension=0, tiled=True
        )
        return lax.psum_scatter(narrowed, "col", scatter_dimension=1, tiled=True).astype(jnp.float32)

    return tuple(one(grad) for grad in grads)


def dot_rows(left, right):
    return lax.dot_general(
        left, right, (((0,), (0,)), ((), ())), preferred_element_type=jnp.float32
    )


def dot_back(left, right):
    return lax.dot_general(
        left, right, (((1,), (1,)), ((), ())), preferred_element_type=jnp.float32
    )


def norm_rows(resid, gain, shift):
    centre = resid - jnp.mean(resid, axis=1, keepdims=True)
    factor = lax.rsqrt(jnp.mean(centre * centre, axis=1, keepdims=True) + norm_eps)
    normed = centre * factor
    return (normed * gain + shift, normed, factor)


def norm_back(grad_result, normed, factor, gain):
    grad_normed = grad_result * gain
    grad_resid = factor * (
        grad_normed
        - jnp.mean(grad_normed, axis=1, keepdims=True)
        - normed * jnp.mean(grad_normed * normed, axis=1, keepdims=True)
    )
    return (grad_resid, jnp.sum(grad_result * normed, axis=0), jnp.sum(grad_result, axis=0))


def gelu_exact(value):
    return jax.nn.gelu(value, approximate=False)


BLOCK = 512


def contract(left, right, left_dim, right_dim):
    return lax.dot_general(
        left, right, (((left_dim,), (right_dim,)), ((), ())), preferred_element_type=jnp.float32
    )


def keep_head(field, head):
    lane = lax.broadcasted_iota(jnp.int32, field.shape, 1)
    keep = (lane < HEAD_DIM) if head == 0 else (lane >= HEAD_DIM)
    return jnp.where(keep, field, jnp.zeros_like(field))


def attend_kernel(q, k, v, seg_row, seg_col, context, logsum, bias):
    bias[...] = jnp.where(seg_col[BLOCK:, :] == seg_row[0:1, BLOCK:], 0.0, masked_score)
    for block in range(2):
        rows = slice(block * BLOCK, (block + 1) * BLOCK)

        def pair_step(pair, _, rows=rows, block=block):
            cols = pl.ds(pl.multiple_of(pair * 128, 128), 128)
            qp, kp, vp = q[rows, cols], k[rows, cols], v[rows, cols]
            total = 0.0
            for head in range(2):
                scores = contract(keep_head(qp, head), kp, 1, 1)
                if block:
                    scores = scores + bias[...]
                peak = jnp.max(scores, axis=1, keepdims=True)
                expo = jnp.exp(scores - peak)
                norm = jnp.sum(expo, axis=1, keepdims=True)
                lse = jnp.broadcast_to(peak + jnp.log(norm), (BLOCK, 128)).T
                logsum[pl.ds(pair * 2 + head, 1), rows] = lse[0:1]
                part = contract(expo.astype(jnp.bfloat16), keep_head(vp, head), 1, 0)
                total = total + part * (1.0 / norm)
            context[rows, cols] = total.astype(jnp.bfloat16)
            return 0

        lax.fori_loop(0, HEADS // 2, pair_step, 0)


def attend_back_kernel(q, k, v, grad, context, logsum, seg_row, seg_col, dq, dk, dv, bias):
    bias[...] = jnp.where(seg_col[BLOCK:, :] == seg_row[0:1, BLOCK:], 0.0, masked_score)
    for block in range(2):
        rows = slice(block * BLOCK, (block + 1) * BLOCK)

        def pair_step(pair, _, rows=rows, block=block):
            cols = pl.ds(pl.multiple_of(pair * 128, 128), 128)
            qp, kp, vp, gp = q[rows, cols], k[rows, cols], v[rows, cols], grad[rows, cols]
            prod = (gp.astype(jnp.float32) * context[rows, cols].astype(jnp.float32)).T
            sum_q = sum_k = sum_v = 0.0
            for head in range(2):
                inner = jnp.sum(prod[head * HEAD_DIM : (head + 1) * HEAD_DIM], axis=0, keepdims=True)
                qh, gh, kh = keep_head(qp, head), keep_head(gp, head), keep_head(kp, head)
                scores = contract(kp, qh, 1, 1)
                if block:
                    scores = scores + bias[...]
                prob = jnp.exp(scores - logsum[pl.ds(pair * 2 + head, 1), rows])
                raw = (prob * (contract(vp, gh, 1, 1) - inner)).astype(jnp.bfloat16)
                sum_v = sum_v + contract(prob.astype(jnp.bfloat16), gh, 1, 0)
                sum_k = sum_k + contract(raw, qh, 1, 0)
                sum_q = sum_q + contract(raw, kh, 0, 0)
            dq[rows, cols] = sum_q * HEAD_DIM ** (-0.5)
            dk[rows, cols] = sum_k
            dv[rows, cols] = sum_v
            return 0

        lax.fori_loop(0, HEADS // 2, pair_step, 0)


VMEM = pl.BlockSpec(memory_space=pltpu.VMEM)


def local_call(kernel, outs, name, *args):
    return pl.pallas_call(
        kernel,
        out_shape=outs,
        in_specs=[VMEM] * len(args),
        out_specs=[VMEM] * len(outs),
        scratch_shapes=[pltpu.VMEM((BLOCK, BLOCK), jnp.float32)],
        compiler_params=pltpu.CompilerParams(vmem_limit_bytes=48 << 20),
        name=name,
    )(*args)


def roll_rows(field, start):
    return lax.dynamic_slice_in_dim(jnp.concatenate([field, field]), start, field.shape[0], 0)


def per_device(
    tokens,
    segment,
    w_qkv,
    w_out,
    w_up,
    w_down,
    bias_query,
    bias_value,
    bias_out,
    gain_attn,
    shift_attn,
    bias_up,
    bias_down,
    gain_ffn,
    shift_ffn,
    cotangent,
):
    model = tokens.shape[1]
    tok_rows = tokens.shape[0]
    device_at = lax.axis_index("row") * lax.axis_size("col") + lax.axis_index("col")
    segrow = lax.dynamic_index_in_dim(segment, device_at * tok_rows // LEN, 0, keepdims=False)
    start = jnp.argmax(segrow[: LEN - BLOCK + 1] == segrow[BLOCK - 1 :]).astype(jnp.int32)
    back = (LEN - start).astype(jnp.int32)
    segrow = roll_rows(segrow, start)
    tokens = roll_rows(tokens, start)
    cotangent = roll_rows(cotangent, start)
    seg_row, seg_col = segrow[None, :], segrow[:, None]
    attn_qkv, attn_out = gather_block((w_qkv, w_out))
    ffn_up, ffn_down = gather_block((w_up, w_down))
    projected = jnp.dot(tokens, attn_qkv, preferred_element_type=jnp.float32)
    queries = (projected[:, :model] + bias_query).astype(jnp.bfloat16) * jnp.bfloat16(HEAD_DIM ** (-0.5))
    keys = projected[:, model : 2 * model].astype(jnp.bfloat16)
    values = (projected[:, 2 * model :] + bias_value).astype(jnp.bfloat16)
    wide = jax.ShapeDtypeStruct((tok_rows, model), jnp.bfloat16)
    context, logsum = local_call(
        attend_kernel,
        [wide, jax.ShapeDtypeStruct((HEADS, tok_rows), jnp.float32)],
        "attend",
        queries, keys, values, seg_row, seg_col,
    )
    attended = jnp.dot(context, attn_out, preferred_element_type=jnp.float32) + bias_out
    hidden, normed_one, factor_one = norm_rows(
        tokens.astype(jnp.float32) + attended, gain_attn, shift_attn
    )
    hidden_low = hidden.astype(jnp.bfloat16)
    upward = jnp.dot(hidden_low, ffn_up, preferred_element_type=jnp.float32) + bias_up
    active_low = gelu_exact(upward).astype(jnp.bfloat16)
    ffn_result = jnp.dot(active_low, ffn_down, preferred_element_type=jnp.float32) + bias_down
    output, normed_two, factor_two = norm_rows(hidden + ffn_result, gain_ffn, shift_ffn)
    grad_two, grad_gain_ffn, grad_shift_ffn = norm_back(
        cotangent.astype(jnp.float32), normed_two, factor_two, gain_ffn
    )
    grad_bias_down = jnp.sum(grad_two, axis=0)
    grad_two_low = grad_two.astype(jnp.bfloat16)
    grad_down_full = dot_rows(active_low, grad_two_low)
    grad_active = dot_back(grad_two_low, ffn_down)
    grad_upward = jax.vjp(gelu_exact, upward)[1](grad_active)[0]
    grad_bias_up = jnp.sum(grad_upward, axis=0)
    grad_up_low = grad_upward.astype(jnp.bfloat16)
    grad_up_full = dot_rows(hidden_low, grad_up_low)
    grad_hidden = grad_two + dot_back(grad_up_low, ffn_up)
    block_up, block_down = reduce_grads((grad_up_full, grad_down_full))
    grad_one, grad_gain_attn, grad_shift_attn = norm_back(
        grad_hidden, normed_one, factor_one, gain_attn
    )
    grad_bias_out = jnp.sum(grad_one, axis=0)
    grad_one_low = grad_one.astype(jnp.bfloat16)
    grad_out_full = dot_rows(context, grad_one_low)
    grad_context = dot_back(grad_one_low, attn_out).astype(jnp.bfloat16)

    full = jax.ShapeDtypeStruct((tok_rows, model), jnp.float32)
    grad_queries, grad_keys, grad_values = local_call(
        attend_back_kernel,
        [full, full, full],
        "attend_back",
        queries, keys, values, grad_context, context, logsum, seg_row, seg_col,
    )
    grad_bias_query = jnp.sum(grad_queries, axis=0)
    grad_bias_value = jnp.sum(grad_values, axis=0)
    grad_proj_low = jnp.concatenate([grad_queries, grad_keys, grad_values], axis=1).astype(jnp.bfloat16)
    grad_qkv_full = dot_rows(tokens, grad_proj_low)
    grad_tokens = grad_one + dot_back(grad_proj_low, attn_qkv)
    block_qkv, block_out = reduce_grads((grad_qkv_full, grad_out_full))
    (
        sum_query,
        sum_value,
        sum_out,
        sum_gain_attn,
        sum_shift_attn,
        sum_up,
        sum_down,
        sum_gain_ffn,
        sum_shift_ffn,
    ) = lax.psum(
        (
            grad_bias_query,
            grad_bias_value,
            grad_bias_out,
            grad_gain_attn,
            grad_shift_attn,
            grad_bias_up,
            grad_bias_down,
            grad_gain_ffn,
            grad_shift_ffn,
        ),
        ("row", "col"),
    )
    return (
        roll_rows(output.astype(jnp.bfloat16), back),
        roll_rows(grad_tokens, back),
        block_qkv,
        block_out,
        block_up,
        block_down,
        sum_query,
        sum_value,
        sum_out,
        sum_gain_attn,
        sum_shift_attn,
        sum_up,
        sum_down,
        sum_gain_ffn,
        sum_shift_ffn,
    )


def solution(mesh):
    return jax.shard_map(
        per_device,
        mesh=mesh,
        in_specs=(
            P(("row", "col"), None),
            P(),
            P("row", "col"),
            P("row", "col"),
            P("row", "col"),
            P("row", "col"),
            P(),
            P(),
            P(),
            P(),
            P(),
            P(),
            P(),
            P(),
            P(),
            P(("row", "col"), None),
        ),
        out_specs=(
            P(("row", "col"), None),
            P(("row", "col"), None),
            P("row", "col"),
            P("row", "col"),
            P("row", "col"),
            P("row", "col"),
            P(),
            P(),
            P(),
            P(),
            P(),
            P(),
            P(),
            P(),
            P(),
        ),
        check_vma=False,
    )
```

```python
import functools

import jax
import jax.numpy as jnp
from jax import lax
from jax.experimental import pallas as pl
from jax.experimental.pallas import tpu as pltpu
from jax.sharding import PartitionSpec as P

HEADS = 12
HEAD_DIM = 64
LEN = 1024


norm_eps = 1e-05
masked_score = -1e30


def reduce_grads(grads):
    def one(grad):
        narrowed = lax.psum_scatter(
            grad.astype(jnp.bfloat16), "row", scatter_dimension=0, tiled=True
        )
        return lax.psum_scatter(narrowed, "col", scatter_dimension=1, tiled=True).astype(jnp.float32)

    return tuple(one(grad) for grad in grads)


def dot_rows(left, right):
    return lax.dot_general(
        left, right, (((0,), (0,)), ((), ())), preferred_element_type=jnp.float32
    )


def dot_back(left, right):
    return lax.dot_general(
        left, right, (((1,), (1,)), ((), ())), preferred_element_type=jnp.float32
    )


def norm_back(grad_result, normed, factor, gain):
    grad_normed = grad_result * gain
    grad_resid = factor * (
        grad_normed
        - jnp.mean(grad_normed, axis=1, keepdims=True)
        - normed * jnp.mean(grad_normed * normed, axis=1, keepdims=True)
    )
    return (grad_resid, jnp.sum(grad_result * normed, axis=0), jnp.sum(grad_result, axis=0))


BLOCK = 512


def contract(left, right, left_dim, right_dim):
    return lax.dot_general(
        left, right, (((left_dim,), (right_dim,)), ((), ())), preferred_element_type=jnp.float32
    )


def keep_head(field, head):
    lane = lax.broadcasted_iota(jnp.int32, field.shape, 1)
    keep = (lane < HEAD_DIM) if head == 0 else (lane >= HEAD_DIM)
    return jnp.where(keep, field, jnp.zeros_like(field))


MESH = pl.DeviceIdType.MESH
ANY = pl.BlockSpec(memory_space=pl.ANY)
CHUNK = 256


class Place:
    def __init__(self, chips, depth):
        self.chips, self.depth, self.hops = chips, depth, chips // 2
        self.row, self.z = lax.axis_index("row"), lax.axis_index("col")
        self.chip, self.core = self.row // 2, self.row % 2
        across = self.chip % 2
        self.pos = self.chip // 2 + across * (chips - 1 - 2 * (self.chip // 2))

    def chip_at(self, pos):
        pos = (pos + self.chips) % self.chips
        far = pos // (self.chips // 2)
        return 2 * (pos + far * (self.chips - 1 - 2 * pos)) + far

    def right(self):
        return (2 * self.chip_at(self.pos + 1) + self.core, self.z)

    def left(self):
        return (2 * self.chip_at(self.pos - 1) + self.core, self.z)

    def mate(self):
        return (self.row + 1 - 2 * self.core, self.z)

    def up(self):
        return (self.row, self.z + 1)

    def down(self):
        return (self.row, self.z - 1)

    def meet(self):
        barrier = pltpu.get_barrier_semaphore()
        for device in (self.right(), self.left(), self.mate()):
            pl.semaphore_signal(barrier, inc=1, device_id=device, device_id_type=MESH)

        @pl.when(self.z < self.depth - 1)
        def _():
            pl.semaphore_signal(barrier, inc=1, device_id=self.up(), device_id_type=MESH)

        @pl.when(self.z > 0)
        def _():
            pl.semaphore_signal(barrier, inc=1, device_id=self.down(), device_id_type=MESH)

        ends = jnp.where(self.z == 0, 1, 0) + jnp.where(self.z == self.depth - 1, 1, 0)
        pl.semaphore_wait(barrier, 5 - ends)


class Gather:
    def __init__(self, place, index, staged, full, sems):
        self.p, self.i, self.staged, self.full = place, index, staged, full
        self.z_send, self.z_recv, self.ring_sent, self.ring_recv, self.core_sent, self.core_recv = sems
        self.rows, self.half = staged.shape[1], full.shape[1] // 2

    def line(self, source, way, step):
        block = self.staged.at[source]
        return pltpu.make_async_remote_copy(
            block, block, self.z_send.at[self.i, way, step], self.z_recv.at[self.i, source],
            device_id=self.p.down() if way else self.p.up(), device_id_type=MESH,
        )

    def open(self):
        p = self.p

        @pl.when(p.z < p.depth - 1)
        def _():
            self.line(p.z, 0, 0).start()

        @pl.when(p.z > 0)
        def _():
            self.line(p.z, 1, 0).start()

    def relay(self):
        p = self.p
        for step in range(1, p.depth):

            @pl.when(p.z - step >= 0)
            def _(step=step):
                self.line(p.z - step, 0, step).wait_recv()

                @pl.when(p.z < p.depth - 1)
                def _():
                    self.line(p.z - step, 0, step).start()

            @pl.when(p.z + step < p.depth)
            def _(step=step):
                self.line(p.z + step, 1, step).wait_recv()

                @pl.when(p.z > 0)
                def _():
                    self.line(p.z + step, 1, step).start()

        rows = pl.ds(pl.multiple_of(p.row * self.rows, self.rows), self.rows)
        self.full[rows, :] = jnp.concatenate([self.staged[z] for z in range(p.depth)], axis=1)

    def line_sent(self):
        p = self.p
        for step in range(p.depth):

            @pl.when((p.z - step >= 0) & (p.z < p.depth - 1))
            def _(step=step):
                self.line(p.z - step, 0, step).wait_send()

            @pl.when((p.z + step < p.depth) & (p.z > 0))
            def _(step=step):
                self.line(p.z + step, 1, step).wait_send()

    def piece(self, hop, way, core):
        p = self.p
        pos = p.pos + hop if way else p.pos - hop
        row = 2 * p.chip_at(pos) + core
        rows = pl.ds(pl.multiple_of(row * self.rows, self.rows), self.rows)
        if hop == p.hops:
            return self.full.at[rows, pl.ds(way * self.half, self.half)]
        return self.full.at[rows, :]

    def ring(self, hop, way):
        p = self.p
        pos = p.pos + hop - 1 if way else p.pos - hop + 1
        row = 2 * p.chip_at(pos) + p.core
        rows = pl.ds(pl.multiple_of(row * self.rows, self.rows), self.rows)
        cols = pl.ds(way * self.half, self.half) if hop == p.hops else slice(None)
        block = self.full.at[rows, cols]
        return pltpu.make_async_remote_copy(
            block, block, self.ring_sent.at[self.i, way, hop - 1], self.ring_recv.at[self.i, way, hop - 1],
            device_id=p.left() if way else p.right(), device_id_type=MESH,
        )

    def landed(self, hop, way):
        block = self.piece(hop, way, self.p.core)
        return pltpu.make_async_remote_copy(
            block, block, self.ring_sent.at[self.i, way, hop - 1], self.ring_recv.at[self.i, way, hop - 1],
            device_id=self.p.left() if way else self.p.right(), device_id_type=MESH,
        )

    def pair(self, hop, way, core):
        block = self.piece(hop, way, core)
        slot = 0 if hop == 0 else 2 * hop - 1 + way
        return pltpu.make_async_remote_copy(
            block, block, self.core_sent.at[self.i, slot], self.core_recv.at[self.i, slot],
            device_id=self.p.mate(), device_id_type=MESH,
        )

    def start_ring(self):
        self.ring(1, 0).start()
        self.ring(1, 1).start()
        self.pair(0, 0, self.p.core).start()

    def advance(self, hop):
        for way in range(2):
            self.landed(hop, way).wait_recv()
            if hop < self.p.hops:
                self.ring(hop + 1, way).start()
            self.pair(hop, way, self.p.core).start()

    def mate_has(self, hop):
        for way in range(1 if hop == 0 else 2):
            self.pair(hop, way, 1 - self.p.core).wait_recv()

    def finish(self):
        self.line_sent()
        self.pair(0, 0, self.p.core).wait_send()
        for hop in range(1, self.p.hops + 1):
            for way in range(2):
                self.ring(hop, way).wait_send()
                self.pair(hop, way, self.p.core).wait_send()


def gelu_parts(value):
    part = 1.0 / (1.0 + jnp.abs(value) * (0.3275911 * 0.5**0.5))
    bell = jnp.exp(value * value * -0.5)
    tail = part * (0.127414796 + part * (-0.142248368 + part * (0.7107068705 + part * (-0.7265760135 + part * 0.5307027145))))
    tail = tail * bell
    below = jnp.where(value >= 0, 1.0 - tail, tail)
    return value * below, below + value * bell * 0.3989422804014327


def row_mean(field):
    return jnp.mean(field, axis=1, keepdims=True)


def fill_bias(seg_row, bias):
    seg_key = seg_row[0:1, BLOCK:]
    seg_query = jnp.broadcast_to(seg_key, (128, BLOCK)).T[:, 0:1]
    bias[...] = jnp.where(seg_query == seg_key, 0.0, masked_score)


def attend_pair(qkv, bias, context, logsum, model, block, pair):
    rows = slice(block * BLOCK, (block + 1) * BLOCK)
    cols = [pl.ds(pl.multiple_of(part * model + pair * 128, 128), 128) for part in range(3)]
    qp, kp, vp = (qkv[rows, col] for col in cols)
    total = 0.0
    for head in range(2):
        scores = contract(keep_head(qp, head), kp, 1, 1)
        if block:
            scores = scores + bias[...]
        peak = jnp.max(scores, axis=1, keepdims=True)
        expo = jnp.exp(scores - peak)
        norm = jnp.sum(expo, axis=1, keepdims=True)
        lse = jnp.broadcast_to(peak + jnp.log(norm), (BLOCK, 128)).T
        logsum[pl.ds(pair * 2 + head, 1), rows] = lse[0:1]
        part = contract(expo.astype(jnp.bfloat16), keep_head(vp, head), 1, 0)
        total = total + part * (1.0 / norm)
    context[rows, cols[0]] = total.astype(jnp.bfloat16)


def forward_kernel(
    chips, depth,
    tokens_in, cot_in, qkv_in, out_in, up_in, down_in, seg_row, vecs,
    output_o, two_o, two_low_o, qkv_o, context_o, normed_o, hidden_low_o, active_o, slope_o,
    wqkv_o, wout_o, wup_o, wdown_o, logsum, factor, sums,
    tokens, cot, s_qkv, s_out, s_up, s_down, w_qkv, w_out, w_up, w_down,
    qkv, context, bias, hidden, hidden_low, normed, active, slope, two_low, output,
    load, store, z_send, z_recv, ring_sent, ring_recv, core_sent, core_recv,
):
    p = Place(chips, depth)
    rows, model = tokens.shape
    pairs = HEADS // 2
    loads = [
        pltpu.make_async_copy(src, dst, load.at[i])
        for i, (src, dst) in enumerate(
            ((qkv_in, s_qkv.at[p.z]), (out_in, s_out.at[p.z]), (up_in, s_up.at[p.z]), (down_in, s_down.at[p.z]), (tokens_in, tokens), (cot_in, cot))
        )
    ]
    for item in loads:
        item.start()
    sems = (z_send, z_recv, ring_sent, ring_recv, core_sent, core_recv)
    g_qkv, g_out, g_up, g_down = (
        Gather(p, i, staged, full, sems)
        for i, (staged, full) in enumerate(((s_qkv, w_qkv), (s_out, w_out), (s_up, w_up), (s_down, w_down)))
    )
    stores = []

    def put(src, dst):
        copy = pltpu.make_async_copy(src, dst, store.at[len(stores)])
        copy.start()
        stores.append(copy)

    p.meet()
    for item, gather in zip(loads, (g_qkv, g_out, g_up, g_down)):
        item.wait()
        gather.open()
    g_qkv.relay()
    g_qkv.start_ring()
    g_out.relay()
    fill_bias(seg_row, bias)
    for hop in range(1, p.hops):
        g_qkv.advance(hop)
    g_out.start_ring()
    g_up.relay()
    g_qkv.advance(p.hops)
    g_up.start_ring()
    loads[4].wait()
    loads[5].wait()
    for hop in range(p.hops + 1):
        g_qkv.mate_has(hop)
    put(w_qkv, wqkv_o)

    def project(step, _):
        tile, at = step % 3, pl.ds(pl.multiple_of(step // 3 * CHUNK, CHUNK), CHUNK)
        cols = pl.ds(pl.multiple_of(tile * model, model), model)
        got = contract(tokens[at, :], w_qkv[:, cols], 1, 0) + vecs[pl.ds(tile, 1), :]
        got = got * jnp.where(tile == 0, HEAD_DIM ** (-0.5), 1.0)
        qkv[at, cols] = got.astype(jnp.bfloat16)
        return 0

    lax.fori_loop(0, 3 * (rows // CHUNK), project, 0)
    put(qkv, qkv_o)
    for hop in range(1, p.hops):
        g_out.advance(hop)

    def attend_first(pair, _):
        attend_pair(qkv, bias, context, logsum, model, 0, pair)
        return 0

    lax.fori_loop(0, pairs, attend_first, 0)
    g_down.relay()

    def attend_second(pair, _):
        attend_pair(qkv, bias, context, logsum, model, 1, pair)

        @pl.when(pair == pairs // 2 - 1)
        def _():
            for hop in range(1, p.hops):
                g_up.advance(hop)
            g_down.start_ring()

        return 0

    lax.fori_loop(0, pairs, attend_second, 0)
    g_out.advance(p.hops)
    put(context, context_o)
    for hop in range(p.hops + 1):
        g_out.mate_has(hop)
    put(w_out, wout_o)

    def first_norm(step, _):
        at = pl.ds(pl.multiple_of(step * CHUNK, CHUNK), CHUNK)
        resid = contract(context[at, :], w_out[...], 1, 0) + vecs[3:4, :] + tokens[at, :].astype(jnp.float32)
        centre = resid - row_mean(resid)
        scale = lax.rsqrt(row_mean(centre * centre) + norm_eps)
        unit = centre * scale
        normed[at, :] = unit
        factor[at, :] = jnp.broadcast_to(scale, (CHUNK, 128))
        value = unit * vecs[4:5, :] + vecs[5:6, :]
        hidden[at, :] = value + vecs[6:7, :]
        hidden_low[at, :] = value.astype(jnp.bfloat16)
        return 0

    lax.fori_loop(0, rows // CHUNK, first_norm, 0)
    put(normed, normed_o)
    put(hidden_low, hidden_low_o)
    g_up.advance(p.hops)
    for hop in range(p.hops + 1):
        g_up.mate_has(hop)
    put(w_up, wup_o)
    tiles = active.shape[1] // model
    steps = tiles * (rows // CHUNK)

    def widen(step, _):
        tile, at = step % tiles, pl.ds(pl.multiple_of(step // tiles * CHUNK, CHUNK), CHUNK)
        cols = pl.ds(pl.multiple_of(tile * model, model), model)
        value = contract(hidden_low[at, :], w_up[:, cols], 1, 0) + vecs[pl.ds(9 + tile, 1), :]
        act, grade = gelu_parts(value)
        active[at, cols] = act.astype(jnp.bfloat16)
        slope[at, cols] = grade.astype(jnp.bfloat16)

        @pl.when(step == steps * 3 // 4)
        def _():
            for hop in range(1, p.hops):
                g_down.advance(hop)

        return 0

    lax.fori_loop(0, steps, widen, 0)
    put(active, active_o)
    put(slope, slope_o)
    deep = 2 * g_down.rows

    def narrow(chip):
        span = pl.ds(pl.multiple_of(chip * deep, deep), deep)

        def step_rows(step, _):
            at = pl.ds(pl.multiple_of(step * CHUNK, CHUNK), CHUNK)
            hidden[at, :] += contract(active[at, span], w_down[span, :], 1, 0)
            return 0

        lax.fori_loop(0, rows // CHUNK, step_rows, 0)

    for hop in range(p.hops):
        g_down.mate_has(hop)
        if hop == p.hops - 1:
            g_down.advance(p.hops)
        for way in range(1 if hop == 0 else 2):
            narrow(p.chip_at(p.pos + hop if way else p.pos - hop))
    g_down.mate_has(p.hops)
    put(w_down, wdown_o)
    narrow(p.chip_at(p.pos + p.hops))
    sums[...] = jnp.zeros_like(sums)

    def second_norm(step, _):
        at = pl.ds(pl.multiple_of(step * CHUNK, CHUNK), CHUNK)
        resid = hidden[at, :]
        centre = resid - row_mean(resid)
        scale = lax.rsqrt(row_mean(centre * centre) + norm_eps)
        unit = centre * scale
        output[at, :] = (unit * vecs[7:8, :] + vecs[8:9, :]).astype(jnp.bfloat16)
        coming = cot[at, :].astype(jnp.float32)
        inner = coming * vecs[7:8, :]
        both = scale * (inner - row_mean(inner) - unit * row_mean(inner * unit))
        hidden[at, :] = both
        two_low[at, :] = both.astype(jnp.bfloat16)
        sums[0:1, :] += jnp.sum(coming * unit, axis=0, keepdims=True)
        sums[1:2, :] += jnp.sum(coming, axis=0, keepdims=True)
        sums[2:3, :] += jnp.sum(both, axis=0, keepdims=True)
        return 0

    lax.fori_loop(0, rows // CHUNK, second_norm, 0)
    put(output, output_o)
    put(hidden, two_o)
    put(two_low, two_low_o)
    for gather in (g_qkv, g_out, g_up, g_down):
        gather.finish()
    for copy in stores:
        copy.wait()


def forward(chips, depth, tokens, cotangent, w_qkv, w_out, w_up, w_down, seg_row, vecs):
    rows, model = tokens.shape
    low, full = jnp.bfloat16, jnp.float32
    weights = (w_qkv, w_out, w_up, w_down)
    whole = [(2 * chips * w.shape[0], depth * w.shape[1]) for w in weights]
    wide = whole[2][1]
    shape = jax.ShapeDtypeStruct
    outs = [
        shape((rows, model), low), shape((rows, model), full), shape((rows, model), low),
        shape((rows, 3 * model), low), shape((rows, model), low), shape((rows, model), full),
        shape((rows, model), low), shape((rows, wide), low), shape((rows, wide), low),
        *(shape(size, low) for size in whole),
        shape((HEADS, rows), full), shape((rows, 128), full), shape((8, model), full),
    ]
    hops = chips // 2
    return pl.pallas_call(
        functools.partial(forward_kernel, chips, depth),
        out_shape=outs,
        in_specs=[ANY] * 6 + [VMEM] * 2,
        out_specs=[ANY] * 13 + [VMEM] * 3,
        scratch_shapes=[
            pltpu.VMEM((rows, model), low), pltpu.VMEM((rows, model), low),
            *(pltpu.VMEM((depth, *w.shape), low) for w in weights),
            *(pltpu.VMEM(size, low) for size in whole),
            pltpu.VMEM((rows, 3 * model), low), pltpu.VMEM((rows, model), low), pltpu.VMEM((BLOCK, BLOCK), full),
            pltpu.VMEM((rows, model), full), pltpu.VMEM((rows, model), low), pltpu.VMEM((rows, model), full),
            pltpu.VMEM((rows, wide), low), pltpu.VMEM((rows, wide), low),
            pltpu.VMEM((rows, model), low), pltpu.VMEM((rows, model), low),
            pltpu.SemaphoreType.DMA((6,)), pltpu.SemaphoreType.DMA((13,)),
            pltpu.SemaphoreType.DMA((4, 2, depth)), pltpu.SemaphoreType.DMA((4, depth)),
            pltpu.SemaphoreType.DMA((4, 2, hops)), pltpu.SemaphoreType.DMA((4, 2, hops)),
            pltpu.SemaphoreType.DMA((4, 2 * hops + 1)), pltpu.SemaphoreType.DMA((4, 2 * hops + 1)),
        ],
        compiler_params=pltpu.CompilerParams(collective_id=0, has_side_effects=True, vmem_limit_bytes=67043328),
        name="forward",
    )(tokens, cotangent, *weights, seg_row, vecs)


def attend_back_kernel(q, k, v, grad, context, logsum, seg_row, seg_col, dq, dk, dv, bias):
    bias[...] = jnp.where(seg_col[BLOCK:, :] == seg_row[0:1, BLOCK:], 0.0, masked_score)
    for block in range(2):
        rows = slice(block * BLOCK, (block + 1) * BLOCK)

        def pair_step(pair, _, rows=rows, block=block):
            cols = pl.ds(pl.multiple_of(pair * 128, 128), 128)
            qp, kp, vp, gp = q[rows, cols], k[rows, cols], v[rows, cols], grad[rows, cols]
            prod = (gp.astype(jnp.float32) * context[rows, cols].astype(jnp.float32)).T
            sum_q = sum_k = sum_v = 0.0
            for head in range(2):
                inner = jnp.sum(prod[head * HEAD_DIM : (head + 1) * HEAD_DIM], axis=0, keepdims=True)
                qh, gh, kh = keep_head(qp, head), keep_head(gp, head), keep_head(kp, head)
                scores = contract(kp, qh, 1, 1)
                if block:
                    scores = scores + bias[...]
                prob = jnp.exp(scores - logsum[pl.ds(pair * 2 + head, 1), rows])
                raw = (prob * (contract(vp, gh, 1, 1) - inner)).astype(jnp.bfloat16)
                sum_v = sum_v + contract(prob.astype(jnp.bfloat16), gh, 1, 0)
                sum_k = sum_k + contract(raw, qh, 1, 0)
                sum_q = sum_q + contract(raw, kh, 0, 0)
            dq[rows, cols] = sum_q * HEAD_DIM ** (-0.5)
            dk[rows, cols] = sum_k
            dv[rows, cols] = sum_v
            return 0

        lax.fori_loop(0, HEADS // 2, pair_step, 0)


VMEM = pl.BlockSpec(memory_space=pltpu.VMEM)


def local_call(kernel, outs, name, *args):
    return pl.pallas_call(
        kernel,
        out_shape=outs,
        in_specs=[VMEM] * len(args),
        out_specs=[VMEM] * len(outs),
        scratch_shapes=[pltpu.VMEM((BLOCK, BLOCK), jnp.float32)],
        compiler_params=pltpu.CompilerParams(vmem_limit_bytes=48 << 20),
        name=name,
    )(*args)


def roll_rows(field, start):
    return lax.dynamic_slice_in_dim(jnp.concatenate([field, field]), start, field.shape[0], 0)


def per_device(
    tokens,
    segment,
    w_qkv,
    w_out,
    w_up,
    w_down,
    bias_query,
    bias_value,
    bias_out,
    gain_attn,
    shift_attn,
    bias_up,
    bias_down,
    gain_ffn,
    shift_ffn,
    cotangent,
):
    model = tokens.shape[1]
    tok_rows = tokens.shape[0]
    device_at = lax.axis_index("row") * lax.axis_size("col") + lax.axis_index("col")
    segrow = lax.dynamic_index_in_dim(segment, device_at * tok_rows // LEN, 0, keepdims=False)
    start = jnp.argmax(segrow[: LEN - BLOCK + 1] == segrow[BLOCK - 1 :]).astype(jnp.int32)
    back = (LEN - start).astype(jnp.int32)
    segrow = roll_rows(segrow, start)
    tokens = roll_rows(tokens, start)
    cotangent = roll_rows(cotangent, start)
    seg_row, seg_col = segrow[None, :], segrow[:, None]
    vecs = jnp.concatenate(
        [
            jnp.stack([bias_query, jnp.zeros_like(bias_query), bias_value, bias_out, gain_attn, shift_attn, bias_down, gain_ffn, shift_ffn]),
            bias_up.reshape(-1, model),
        ]
    )
    chips, depth = lax.axis_size("row") // 2, lax.axis_size("col")
    (
        output, grad_two, grad_two_low, projected, context, normed_one, hidden_low, active_low, slope,
        attn_qkv, attn_out, ffn_up, ffn_down, logsum, factor_one, sums,
    ) = forward(chips, depth, tokens, cotangent, w_qkv, w_out, w_up, w_down, seg_row, vecs)
    factor_one = factor_one[:, :1]
    queries, keys, values = (projected[:, i * model : (i + 1) * model] for i in range(3))
    grad_gain_ffn, grad_shift_ffn, grad_bias_down = sums[0], sums[1], sums[2]
    grad_down_full = dot_rows(active_low, grad_two_low)
    grad_active = dot_back(grad_two_low, ffn_down)
    grad_upward = grad_active * slope.astype(jnp.float32)
    grad_bias_up = jnp.sum(grad_upward, axis=0)
    grad_up_low = grad_upward.astype(jnp.bfloat16)
    grad_up_full = dot_rows(hidden_low, grad_up_low)
    grad_hidden = grad_two + dot_back(grad_up_low, ffn_up)
    block_up, block_down = reduce_grads((grad_up_full, grad_down_full))
    grad_one, grad_gain_attn, grad_shift_attn = norm_back(
        grad_hidden, normed_one, factor_one, gain_attn
    )
    grad_bias_out = jnp.sum(grad_one, axis=0)
    grad_one_low = grad_one.astype(jnp.bfloat16)
    grad_out_full = dot_rows(context, grad_one_low)
    grad_context = dot_back(grad_one_low, attn_out).astype(jnp.bfloat16)

    full = jax.ShapeDtypeStruct((tok_rows, model), jnp.float32)
    grad_queries, grad_keys, grad_values = local_call(
        attend_back_kernel,
        [full, full, full],
        "attend_back",
        queries, keys, values, grad_context, context, logsum, seg_row, seg_col,
    )
    grad_bias_query = jnp.sum(grad_queries, axis=0)
    grad_bias_value = jnp.sum(grad_values, axis=0)
    grad_proj_low = jnp.concatenate([grad_queries, grad_keys, grad_values], axis=1).astype(jnp.bfloat16)
    grad_qkv_full = dot_rows(tokens, grad_proj_low)
    grad_tokens = grad_one + dot_back(grad_proj_low, attn_qkv)
    block_qkv, block_out = reduce_grads((grad_qkv_full, grad_out_full))
    (
        sum_query,
        sum_value,
        sum_out,
        sum_gain_attn,
        sum_shift_attn,
        sum_up,
        sum_down,
        sum_gain_ffn,
        sum_shift_ffn,
    ) = lax.psum(
        (
            grad_bias_query,
            grad_bias_value,
            grad_bias_out,
            grad_gain_attn,
            grad_shift_attn,
            grad_bias_up,
            grad_bias_down,
            grad_gain_ffn,
            grad_shift_ffn,
        ),
        ("row", "col"),
    )
    return (
        roll_rows(output.astype(jnp.bfloat16), back),
        roll_rows(grad_tokens, back),
        block_qkv,
        block_out,
        block_up,
        block_down,
        sum_query,
        sum_value,
        sum_out,
        sum_gain_attn,
        sum_shift_attn,
        sum_up,
        sum_down,
        sum_gain_ffn,
        sum_shift_ffn,
    )


def solution(mesh):
    return jax.shard_map(
        per_device,
        mesh=mesh,
        in_specs=(
            P(("row", "col"), None),
            P(),
            P("row", "col"),
            P("row", "col"),
            P("row", "col"),
            P("row", "col"),
            P(),
            P(),
            P(),
            P(),
            P(),
            P(),
            P(),
            P(),
            P(),
            P(("row", "col"), None),
        ),
        out_specs=(
            P(("row", "col"), None),
            P(("row", "col"), None),
            P("row", "col"),
            P("row", "col"),
            P("row", "col"),
            P("row", "col"),
            P(),
            P(),
            P(),
            P(),
            P(),
            P(),
            P(),
            P(),
            P(),
        ),
        check_vma=False,
    )
```

```python
import functools

import jax
import jax.numpy as jnp
from jax import lax
from jax.experimental import pallas as pl
from jax.experimental.pallas import tpu as pltpu
from jax.sharding import PartitionSpec as P

HEADS = 12
HEAD_DIM = 64
LEN = 1024


norm_eps = 1e-05
masked_score = -1e30


BLOCK = 512


def contract(left, right, left_dim, right_dim):
    return lax.dot_general(
        left, right, (((left_dim,), (right_dim,)), ((), ())), preferred_element_type=jnp.float32
    )


def keep_head(field, head):
    lane = lax.broadcasted_iota(jnp.int32, field.shape, 1)
    keep = (lane < HEAD_DIM) if head == 0 else (lane >= HEAD_DIM)
    return jnp.where(keep, field, jnp.zeros_like(field))


MESH = pl.DeviceIdType.MESH
ANY = pl.BlockSpec(memory_space=pl.ANY)
CHUNK = 256


class Place:
    def __init__(self, chips, depth):
        self.chips, self.depth, self.hops = chips, depth, chips // 2
        self.row, self.z = lax.axis_index("row"), lax.axis_index("col")
        self.chip, self.core = self.row // 2, self.row % 2
        across = self.chip % 2
        self.pos = self.chip // 2 + across * (chips - 1 - 2 * (self.chip // 2))

    def chip_at(self, pos):
        pos = (pos + self.chips) % self.chips
        far = pos // (self.chips // 2)
        return 2 * (pos + far * (self.chips - 1 - 2 * pos)) + far

    def right(self):
        return (2 * self.chip_at(self.pos + 1) + self.core, self.z)

    def left(self):
        return (2 * self.chip_at(self.pos - 1) + self.core, self.z)

    def mate(self):
        return (self.row + 1 - 2 * self.core, self.z)

    def up(self):
        return (self.row, self.z + 1)

    def down(self):
        return (self.row, self.z - 1)

    def meet(self):
        barrier = pltpu.get_barrier_semaphore()
        for device in (self.right(), self.left(), self.mate()):
            pl.semaphore_signal(barrier, inc=1, device_id=device, device_id_type=MESH)

        @pl.when(self.z < self.depth - 1)
        def _():
            pl.semaphore_signal(barrier, inc=1, device_id=self.up(), device_id_type=MESH)

        @pl.when(self.z > 0)
        def _():
            pl.semaphore_signal(barrier, inc=1, device_id=self.down(), device_id_type=MESH)

        ends = jnp.where(self.z == 0, 1, 0) + jnp.where(self.z == self.depth - 1, 1, 0)
        pl.semaphore_wait(barrier, 5 - ends)

    def meet_all(self):
        barrier = pltpu.get_barrier_semaphore()
        others = [(2 * self.chip_at(self.pos + apart) + self.core, self.z) for apart in range(1, self.chips)]
        others += [(self.row, (self.z + apart) % self.depth) for apart in range(1, self.depth)]
        for device in [*others, self.mate()]:
            pl.semaphore_signal(barrier, inc=1, device_id=device, device_id_type=MESH)
        pl.semaphore_wait(barrier, self.chips + self.depth - 1)


class Gather:
    def __init__(self, place, index, staged, full, sems):
        self.p, self.i, self.staged, self.full = place, index, staged, full
        self.z_send, self.z_recv, self.ring_sent, self.ring_recv, self.core_sent, self.core_recv = sems
        self.rows, self.half = staged.shape[1], full.shape[1] // 2

    def line(self, source, way, step):
        block = self.staged.at[source]
        return pltpu.make_async_remote_copy(
            block, block, self.z_send.at[self.i, way, step], self.z_recv.at[self.i, source],
            device_id=self.p.down() if way else self.p.up(), device_id_type=MESH,
        )

    def open(self):
        p = self.p

        @pl.when(p.z < p.depth - 1)
        def _():
            self.line(p.z, 0, 0).start()

        @pl.when(p.z > 0)
        def _():
            self.line(p.z, 1, 0).start()

    def relay(self):
        p = self.p
        for step in range(1, p.depth):

            @pl.when(p.z - step >= 0)
            def _(step=step):
                self.line(p.z - step, 0, step).wait_recv()

                @pl.when(p.z < p.depth - 1)
                def _():
                    self.line(p.z - step, 0, step).start()

            @pl.when(p.z + step < p.depth)
            def _(step=step):
                self.line(p.z + step, 1, step).wait_recv()

                @pl.when(p.z > 0)
                def _():
                    self.line(p.z + step, 1, step).start()

        rows = pl.ds(pl.multiple_of(p.row * self.rows, self.rows), self.rows)
        self.full[rows, :] = jnp.concatenate([self.staged[z] for z in range(p.depth)], axis=1)

    def line_sent(self):
        p = self.p
        for step in range(p.depth):

            @pl.when((p.z - step >= 0) & (p.z < p.depth - 1))
            def _(step=step):
                self.line(p.z - step, 0, step).wait_send()

            @pl.when((p.z + step < p.depth) & (p.z > 0))
            def _(step=step):
                self.line(p.z + step, 1, step).wait_send()

    def piece(self, hop, way, core):
        p = self.p
        pos = p.pos + hop if way else p.pos - hop
        row = 2 * p.chip_at(pos) + core
        rows = pl.ds(pl.multiple_of(row * self.rows, self.rows), self.rows)
        if hop == p.hops:
            return self.full.at[rows, pl.ds(way * self.half, self.half)]
        return self.full.at[rows, :]

    def ring(self, hop, way):
        p = self.p
        pos = p.pos + hop - 1 if way else p.pos - hop + 1
        row = 2 * p.chip_at(pos) + p.core
        rows = pl.ds(pl.multiple_of(row * self.rows, self.rows), self.rows)
        cols = pl.ds(way * self.half, self.half) if hop == p.hops else slice(None)
        block = self.full.at[rows, cols]
        return pltpu.make_async_remote_copy(
            block, block, self.ring_sent.at[self.i, way, hop - 1], self.ring_recv.at[self.i, way, hop - 1],
            device_id=p.left() if way else p.right(), device_id_type=MESH,
        )

    def landed(self, hop, way):
        block = self.piece(hop, way, self.p.core)
        return pltpu.make_async_remote_copy(
            block, block, self.ring_sent.at[self.i, way, hop - 1], self.ring_recv.at[self.i, way, hop - 1],
            device_id=self.p.left() if way else self.p.right(), device_id_type=MESH,
        )

    def pair(self, hop, way, core):
        block = self.piece(hop, way, core)
        slot = 0 if hop == 0 else 2 * hop - 1 + way
        return pltpu.make_async_remote_copy(
            block, block, self.core_sent.at[self.i, slot], self.core_recv.at[self.i, slot],
            device_id=self.p.mate(), device_id_type=MESH,
        )

    def start_ring(self):
        self.ring(1, 0).start()
        self.ring(1, 1).start()
        self.pair(0, 0, self.p.core).start()

    def advance(self, hop):
        for way in range(2):
            self.landed(hop, way).wait_recv()
            if hop < self.p.hops:
                self.ring(hop + 1, way).start()
            self.pair(hop, way, self.p.core).start()

    def mate_has(self, hop):
        for way in range(1 if hop == 0 else 2):
            self.pair(hop, way, 1 - self.p.core).wait_recv()

    def finish(self):
        self.line_sent()
        self.pair(0, 0, self.p.core).wait_send()
        for hop in range(1, self.p.hops + 1):
            for way in range(2):
                self.ring(hop, way).wait_send()
                self.pair(hop, way, self.p.core).wait_send()


def gelu_parts(value):
    part = 1.0 / (1.0 + jnp.abs(value) * (0.3275911 * 0.5**0.5))
    bell = jnp.exp(value * value * -0.5)
    tail = part * (0.127414796 + part * (-0.142248368 + part * (0.7107068705 + part * (-0.7265760135 + part * 0.5307027145))))
    tail = tail * bell
    below = jnp.where(value >= 0, 1.0 - tail, tail)
    return value * below, below + value * bell * 0.3989422804014327


def row_mean(field):
    return jnp.mean(field, axis=1, keepdims=True)


def fill_bias(seg_row, bias):
    seg_key = seg_row[0:1, BLOCK:]
    seg_query = jnp.broadcast_to(seg_key, (128, BLOCK)).T[:, 0:1]
    bias[...] = jnp.where(seg_query == seg_key, 0.0, masked_score)


def attend_pair(qkv, bias, context, logsum, model, block, pair):
    rows = slice(block * BLOCK, (block + 1) * BLOCK)
    cols = [pl.ds(pl.multiple_of(part * model + pair * 128, 128), 128) for part in range(3)]
    qp, kp, vp = (qkv[rows, col] for col in cols)
    total = 0.0
    for head in range(2):
        scores = contract(keep_head(qp, head), kp, 1, 1)
        if block:
            scores = scores + bias[...]
        peak = jnp.max(scores, axis=1, keepdims=True)
        expo = jnp.exp(scores - peak)
        norm = jnp.sum(expo, axis=1, keepdims=True)
        lse = jnp.broadcast_to(peak + jnp.log(norm), (BLOCK, 128)).T
        logsum[pl.ds(pair * 2 + head, 1), rows] = lse[0:1]
        part = contract(expo.astype(jnp.bfloat16), keep_head(vp, head), 1, 0)
        total = total + part * (1.0 / norm)
    context[rows, cols[0]] = total.astype(jnp.bfloat16)


def forward_kernel(
    chips, depth,
    tokens_in, cot_in, qkv_in, out_in, up_in, down_in, seg_row, vecs,
    output_o, two_o, two_low_o, qkv_o, context_o, normed_o, hidden_low_o, active_o, slope_o,
    wqkv_o, wout_o, wup_o, wdown_o, logsum, factor, sums,
    tokens, cot, s_qkv, s_out, s_up, s_down, w_qkv, w_out, w_up, w_down,
    qkv, context, bias, hidden, hidden_low, normed, active, slope, two_low, output,
    load, store, z_send, z_recv, ring_sent, ring_recv, core_sent, core_recv,
):
    p = Place(chips, depth)
    rows, model = tokens.shape
    pairs = HEADS // 2
    loads = [
        pltpu.make_async_copy(src, dst, load.at[i])
        for i, (src, dst) in enumerate(
            ((qkv_in, s_qkv.at[p.z]), (out_in, s_out.at[p.z]), (up_in, s_up.at[p.z]), (down_in, s_down.at[p.z]), (tokens_in, tokens), (cot_in, cot))
        )
    ]
    for item in loads:
        item.start()
    sems = (z_send, z_recv, ring_sent, ring_recv, core_sent, core_recv)
    g_qkv, g_out, g_up, g_down = (
        Gather(p, i, staged, full, sems)
        for i, (staged, full) in enumerate(((s_qkv, w_qkv), (s_out, w_out), (s_up, w_up), (s_down, w_down)))
    )
    stores = []

    def put(src, dst):
        copy = pltpu.make_async_copy(src, dst, store.at[len(stores)])
        copy.start()
        stores.append(copy)

    p.meet()
    for item, gather in zip(loads, (g_qkv, g_out, g_up, g_down)):
        item.wait()
        gather.open()
    g_qkv.relay()
    g_qkv.start_ring()
    g_out.relay()
    fill_bias(seg_row, bias)
    for hop in range(1, p.hops):
        g_qkv.advance(hop)
    g_out.start_ring()
    g_up.relay()
    g_qkv.advance(p.hops)
    g_up.start_ring()
    loads[4].wait()
    loads[5].wait()
    for hop in range(p.hops + 1):
        g_qkv.mate_has(hop)
    put(w_qkv, wqkv_o)

    def project(step, _):
        tile, at = step % 3, pl.ds(pl.multiple_of(step // 3 * CHUNK, CHUNK), CHUNK)
        cols = pl.ds(pl.multiple_of(tile * model, model), model)
        got = contract(tokens[at, :], w_qkv[:, cols], 1, 0) + vecs[pl.ds(tile, 1), :]
        got = got * jnp.where(tile == 0, HEAD_DIM ** (-0.5), 1.0)
        qkv[at, cols] = got.astype(jnp.bfloat16)
        return 0

    lax.fori_loop(0, 3 * (rows // CHUNK), project, 0)
    put(qkv, qkv_o)
    for hop in range(1, p.hops):
        g_out.advance(hop)

    def attend_first(pair, _):
        attend_pair(qkv, bias, context, logsum, model, 0, pair)
        return 0

    lax.fori_loop(0, pairs, attend_first, 0)
    g_down.relay()

    def attend_second(pair, _):
        attend_pair(qkv, bias, context, logsum, model, 1, pair)

        @pl.when(pair == pairs // 2 - 1)
        def _():
            for hop in range(1, p.hops):
                g_up.advance(hop)
            g_down.start_ring()

        return 0

    lax.fori_loop(0, pairs, attend_second, 0)
    g_out.advance(p.hops)
    put(context, context_o)
    for hop in range(p.hops + 1):
        g_out.mate_has(hop)
    put(w_out, wout_o)

    def first_norm(step, _):
        at = pl.ds(pl.multiple_of(step * CHUNK, CHUNK), CHUNK)
        resid = contract(context[at, :], w_out[...], 1, 0) + vecs[3:4, :] + tokens[at, :].astype(jnp.float32)
        centre = resid - row_mean(resid)
        scale = lax.rsqrt(row_mean(centre * centre) + norm_eps)
        unit = centre * scale
        normed[at, :] = unit.astype(jnp.bfloat16)
        factor[at, :] = jnp.broadcast_to(scale, (CHUNK, 128))
        value = unit * vecs[4:5, :] + vecs[5:6, :]
        hidden[at, :] = value + vecs[6:7, :]
        hidden_low[at, :] = value.astype(jnp.bfloat16)
        return 0

    lax.fori_loop(0, rows // CHUNK, first_norm, 0)
    put(normed, normed_o)
    put(hidden_low, hidden_low_o)
    g_up.advance(p.hops)
    for hop in range(p.hops + 1):
        g_up.mate_has(hop)
    put(w_up, wup_o)
    tiles = active.shape[1] // model
    steps = tiles * (rows // CHUNK)

    def widen(step, _):
        tile, at = step % tiles, pl.ds(pl.multiple_of(step // tiles * CHUNK, CHUNK), CHUNK)
        cols = pl.ds(pl.multiple_of(tile * model, model), model)
        value = contract(hidden_low[at, :], w_up[:, cols], 1, 0) + vecs[pl.ds(9 + tile, 1), :]
        act, grade = gelu_parts(value)
        active[at, cols] = act.astype(jnp.bfloat16)
        slope[at, cols] = grade.astype(jnp.bfloat16)

        @pl.when(step == steps * 3 // 4)
        def _():
            for hop in range(1, p.hops):
                g_down.advance(hop)

        return 0

    lax.fori_loop(0, steps, widen, 0)
    put(active, active_o)
    put(slope, slope_o)
    deep = 2 * g_down.rows

    def narrow(chip):
        span = pl.ds(pl.multiple_of(chip * deep, deep), deep)

        def step_rows(step, _):
            at = pl.ds(pl.multiple_of(step * CHUNK, CHUNK), CHUNK)
            hidden[at, :] += contract(active[at, span], w_down[span, :], 1, 0)
            return 0

        lax.fori_loop(0, rows // CHUNK, step_rows, 0)

    for hop in range(p.hops):
        g_down.mate_has(hop)
        if hop == p.hops - 1:
            g_down.advance(p.hops)
        for way in range(1 if hop == 0 else 2):
            narrow(p.chip_at(p.pos + hop if way else p.pos - hop))
    g_down.mate_has(p.hops)
    put(w_down, wdown_o)
    narrow(p.chip_at(p.pos + p.hops))
    sums[...] = jnp.zeros_like(sums)

    def second_norm(step, _):
        at = pl.ds(pl.multiple_of(step * CHUNK, CHUNK), CHUNK)
        resid = hidden[at, :]
        centre = resid - row_mean(resid)
        scale = lax.rsqrt(row_mean(centre * centre) + norm_eps)
        unit = centre * scale
        output[at, :] = (unit * vecs[7:8, :] + vecs[8:9, :]).astype(jnp.bfloat16)
        coming = cot[at, :].astype(jnp.float32)
        inner = coming * vecs[7:8, :]
        both = scale * (inner - row_mean(inner) - unit * row_mean(inner * unit))
        hidden[at, :] = both
        two_low[at, :] = both.astype(jnp.bfloat16)
        sums[0:1, :] += jnp.sum(coming * unit, axis=0, keepdims=True)
        sums[1:2, :] += jnp.sum(coming, axis=0, keepdims=True)
        sums[2:3, :] += jnp.sum(both, axis=0, keepdims=True)
        return 0

    lax.fori_loop(0, rows // CHUNK, second_norm, 0)
    put(output, output_o)
    put(hidden, two_o)
    put(two_low, two_low_o)
    for gather in (g_qkv, g_out, g_up, g_down):
        gather.finish()
    for copy in stores:
        copy.wait()


def forward(chips, depth, tokens, cotangent, w_qkv, w_out, w_up, w_down, seg_row, vecs):
    rows, model = tokens.shape
    low, full = jnp.bfloat16, jnp.float32
    weights = (w_qkv, w_out, w_up, w_down)
    whole = [(2 * chips * w.shape[0], depth * w.shape[1]) for w in weights]
    wide = whole[2][1]
    shape = jax.ShapeDtypeStruct
    outs = [
        shape((rows, model), low), shape((rows, model), full), shape((rows, model), low),
        shape((rows, 3 * model), low), shape((rows, model), low), shape((rows, model), low),
        shape((rows, model), low), shape((rows, wide), low), shape((rows, wide), low),
        *(shape(size, low) for size in whole),
        shape((HEADS, rows), full), shape((rows, 128), full), shape((8, model), full),
    ]
    hops = chips // 2
    return pl.pallas_call(
        functools.partial(forward_kernel, chips, depth),
        out_shape=outs,
        in_specs=[ANY] * 6 + [VMEM] * 2,
        out_specs=[ANY] * 13 + [VMEM] * 3,
        scratch_shapes=[
            pltpu.VMEM((rows, model), low), pltpu.VMEM((rows, model), low),
            *(pltpu.VMEM((depth, *w.shape), low) for w in weights),
            *(pltpu.VMEM(size, low) for size in whole),
            pltpu.VMEM((rows, 3 * model), low), pltpu.VMEM((rows, model), low), pltpu.VMEM((BLOCK, BLOCK), full),
            pltpu.VMEM((rows, model), full), pltpu.VMEM((rows, model), low), pltpu.VMEM((rows, model), low),
            pltpu.VMEM((rows, wide), low), pltpu.VMEM((rows, wide), low),
            pltpu.VMEM((rows, model), low), pltpu.VMEM((rows, model), low),
            pltpu.SemaphoreType.DMA((6,)), pltpu.SemaphoreType.DMA((13,)),
            pltpu.SemaphoreType.DMA((4, 2, depth)), pltpu.SemaphoreType.DMA((4, depth)),
            pltpu.SemaphoreType.DMA((4, 2, hops)), pltpu.SemaphoreType.DMA((4, 2, hops)),
            pltpu.SemaphoreType.DMA((4, 2 * hops + 1)), pltpu.SemaphoreType.DMA((4, 2 * hops + 1)),
        ],
        compiler_params=pltpu.CompilerParams(collective_id=0, has_side_effects=True, vmem_limit_bytes=67043328),
        name="forward",
    )(tokens, cotangent, *weights, seg_row, vecs)


VMEM = pl.BlockSpec(memory_space=pltpu.VMEM)


class Reduce:
    def __init__(self, place, index, bufs, result, sems):
        self.p, self.i, self.result = place, index, result
        self.grad, self.other, self.halves, self.fulls, self.parts, self.came, self.total = bufs
        self.core_sent, self.core_recv, self.ring_sent, self.ring_recv, self.z_sent, self.z_recv, self.res_sem = sems
        self.half = self.grad.shape[3] // 2

    def pair(self):
        return pltpu.make_async_remote_copy(
            self.grad.at[:, 1 - self.p.core], self.other, self.core_sent.at[self.i], self.core_recv.at[self.i],
            device_id=self.p.mate(), device_id_type=MESH,
        )

    def swap(self):
        self.pair().start()

    def absorb(self):
        self.pair().wait_recv()

        def step(chip, _):
            both = self.grad[chip, self.p.core].astype(jnp.float32) + self.other[chip].astype(jnp.float32)
            self.grad[chip, self.p.core] = both.astype(jnp.bfloat16)
            return 0

        lax.fori_loop(0, self.p.chips, step, 0)

    def span(self, hop, way):
        return pl.ds((1 - way) * self.half, self.half) if hop == 1 else slice(None)

    def ring(self, hop, way):
        p = self.p
        dest = p.pos - p.hops + hop - 1 if way else p.pos + p.hops - hop + 1
        return pltpu.make_async_remote_copy(
            self.grad.at[p.chip_at(dest), p.core, :, self.span(hop, way)],
            self.halves.at[way] if hop == 1 else self.fulls.at[way, hop - 2],
            self.ring_sent.at[self.i, way, hop - 1], self.ring_recv.at[self.i, way, hop - 1],
            device_id=p.left() if way else p.right(), device_id_type=MESH,
        )

    def go(self, hop):
        self.ring(hop, 0).start()
        self.ring(hop, 1).start()

    def take(self, hop):
        p = self.p
        for way in range(2):
            self.ring(hop, way).wait_recv()
            chip = p.chip_at(p.pos - p.hops + hop if way else p.pos + p.hops - hop)
            got = self.halves[way] if hop == 1 else self.fulls[way, hop - 2]
            cols = self.span(hop, way)
            both = self.grad[chip, p.core, :, cols].astype(jnp.float32) + got.astype(jnp.float32)
            self.grad[chip, p.core, :, cols] = both.astype(jnp.bfloat16)

    def split(self):
        p = self.p
        self.ring(p.hops, 0).wait_recv()
        self.ring(p.hops, 1).wait_recv()
        last = p.hops - 2
        low = (
            self.grad[p.chip, p.core].astype(jnp.float32)
            + self.fulls[0, last].astype(jnp.float32)
            + self.fulls[1, last].astype(jnp.float32)
        ).astype(jnp.bfloat16)
        wide = self.parts.shape[2]
        for z in range(p.depth):
            self.parts[z] = low[:, z * wide : (z + 1) * wide]

    def line(self, block, way):
        return pltpu.make_async_remote_copy(
            self.parts.at[block], self.came.at[block + 1 - way],
            self.z_sent.at[self.i, way, block], self.z_recv.at[self.i, way, block],
            device_id=self.p.down() if way else self.p.up(), device_id_type=MESH,
        )

    def round(self, turn):
        p = self.p
        for way in range(2):
            far = p.depth - 1 - p.z if way else p.z
            block = turn - far if way else p.depth - 1 - turn + far

            @pl.when(far <= turn)
            def _(far=far, block=block, way=way):
                @pl.when(far > 0)
                def _():
                    self.line(block, way).wait_recv()
                    both = self.parts[block].astype(jnp.float32) + self.came[block + 1 - way].astype(jnp.float32)
                    self.parts[block] = both.astype(jnp.bfloat16)

                self.line(block, way).start()

    def write(self):
        return pltpu.make_async_copy(self.total, self.result, self.res_sem.at[self.i])

    def land(self):
        p = self.p
        self.total[...] = self.parts[p.z].astype(jnp.float32)

        @pl.when(p.z > 0)
        def _():
            self.line(p.z, 0).wait_recv()
            self.total[...] += self.came[p.z + 1].astype(jnp.float32)

        @pl.when(p.z < p.depth - 1)
        def _():
            self.line(p.z, 1).wait_recv()
            self.total[...] += self.came[p.z].astype(jnp.float32)

        self.write().start()

    def finish(self):
        p = self.p
        self.pair().wait_send()
        for hop in range(1, p.hops + 1):
            for way in range(2):
                self.ring(hop, way).wait_send()
        for turn in range(p.depth - 1):
            for way in range(2):
                far = p.depth - 1 - p.z if way else p.z
                block = turn - far if way else p.depth - 1 - turn + far

                @pl.when(far <= turn)
                def _(block=block, way=way):
                    self.line(block, way).wait_send()

        self.write().wait()

    def stages(self):
        def first():
            self.absorb()
            self.go(1)

        def along(hop):
            self.take(hop)
            self.go(hop + 1)

        def begin():
            self.split()
            self.round(0)

        p = self.p
        return [
            [first, *(functools.partial(along, hop) for hop in range(1, p.hops)), begin],
            [*(functools.partial(self.round, turn) for turn in range(1, p.depth - 1)), self.land],
        ]


class Sums:
    def __init__(self, place, sums, mine, pair, plane, line, sems):
        self.p, self.sums, self.mine, self.other, self.plane, self.col = place, sums, mine, pair, plane, line
        self.pair_sent, self.pair_recv, self.plane_sent, self.plane_recv, self.col_sent, self.col_recv = sems

    def pair(self):
        return pltpu.make_async_remote_copy(
            self.mine, self.other, self.pair_sent, self.pair_recv, device_id=self.p.mate(), device_id_type=MESH
        )

    def chip(self, apart, source):
        target = (2 * self.p.chip_at(self.p.pos + apart) + self.p.core, self.p.z)
        return pltpu.make_async_remote_copy(
            self.plane.at[source], self.plane.at[source], self.plane_sent.at[apart], self.plane_recv.at[source],
            device_id=target, device_id_type=MESH,
        )

    def level(self, apart, source):
        target = (self.p.row, (self.p.z + apart) % self.p.depth)
        return pltpu.make_async_remote_copy(
            self.col.at[source], self.col.at[source], self.col_sent.at[apart], self.col_recv.at[source],
            device_id=target, device_id_type=MESH,
        )

    def start(self):
        self.mine[...] = self.sums[...]
        self.pair().start()

    def across(self):
        p = self.p
        self.pair().wait_recv()
        self.plane[p.chip] = self.mine[...] + self.other[...]
        for apart in range(1, p.chips):
            self.chip(apart, p.chip).start()

    def along(self):
        p = self.p
        for apart in range(1, p.chips):
            self.chip(apart, p.chip_at(p.pos + apart)).wait_recv()
        total = self.plane[0]
        for chip in range(1, p.chips):
            total = total + self.plane[chip]
        self.col[p.z] = total
        for apart in range(1, p.depth):
            self.level(apart, p.z).start()

    def land(self, result):
        p = self.p
        for apart in range(1, p.depth):
            self.level(apart, (p.z + apart) % p.depth).wait_recv()
        total = self.col[0]
        for z in range(1, p.depth):
            total = total + self.col[z]
        result[...] = total

    def finish(self):
        p = self.p
        self.pair().wait_send()
        for apart in range(1, p.chips):
            self.chip(apart, p.chip).wait_send()
        for apart in range(1, p.depth):
            self.level(apart, p.z).wait_send()


def backward_kernel(
    chips, depth,
    two_low_in, active_in, wdown_in, slope_in, hidden_low_in, wup_in, two_in, normed_in, factor_in, wout_in, context_in,
    qkv_in, tokens_in, wqkv_in, seg_row, vecs, logsum, sums_in,
    tokens_o, qkv_o, out_o, up_o, down_o, sums_o,
    two_low, active, slope, hidden_low, tiles, acc, normed, factor, w_out, bias, sums,
    *rest,
):
    p = Place(chips, depth)
    groups = [rest[7 * i : 7 * i + 7] for i in range(4)]
    mine, other, plane, col = rest[28:32]
    load, store, core_sent, core_recv, ring_sent, ring_recv, z_sent, z_recv, res_sem = rest[32:41]
    sum_sems = rest[41:47]
    rows, model = two_low.shape
    wide = active.shape[1]
    count = wide // model
    pairs = HEADS // 2
    sems = (core_sent, core_recv, ring_sent, ring_recv, z_sent, z_recv, res_sem)
    r_qkv, r_out, r_up, r_down = (
        Reduce(p, i, bufs, result, sems) for i, (bufs, result) in enumerate(zip(groups, (qkv_o, out_o, up_o, down_o)))
    )
    used = []

    def fetch(src, dst):
        copy = pltpu.make_async_copy(src, dst, load.at[len(used)])
        copy.start()
        used.append(copy)
        return copy

    def col_tile(ref, tile):
        return ref.at[:, pl.ds(tile * model, model)]

    got_two_low = fetch(two_low_in, two_low)
    got_active = [fetch(col_tile(active_in, t), col_tile(active, t)) for t in range(count)]
    got_down = [fetch(wdown_in.at[pl.ds(t * model, model), :], tiles.at[t]) for t in range(count)]
    got_slope = [fetch(col_tile(slope_in, t), col_tile(slope, t)) for t in range(count)]
    got_rest = [
        fetch(src, dst)
        for src, dst in ((hidden_low_in, hidden_low), (two_in, acc), (normed_in, normed), (factor_in, factor), (wout_in, w_out))
    ]
    p.meet_all()

    def weight_grad(reduce, left, right, left_at, tile, skip=0):
        piece = 384
        cols = pl.ds(pl.multiple_of(tile * model, model), model)
        got = contract(left[:, pl.ds(pl.multiple_of(skip + left_at * piece, 128), piece)], right[:, cols], 0, 0)
        high = reduce.grad.shape[2]
        for s in range(piece // high):
            row = left_at * (piece // high) + s
            reduce.grad[row // 2, row % 2, :, cols] = got[s * high : (s + 1) * high].astype(jnp.bfloat16)

    got_two_low.wait()
    for t in range(count):
        got_active[t].wait()

        def down_grad(step, _, t=t):
            weight_grad(r_down, active, two_low, t * (model // 384) + step, 0)
            return 0

        lax.fori_loop(0, model // 384, down_grad, 0)
    r_down.swap()
    got_qkv = fetch(qkv_in, active.at[:, pl.ds(0, 3 * model)])
    sums[...] = jnp.zeros_like(sums)
    sums[9:10, :] = sums_in[2:3, :]
    sums[10:12, :] = sums_in[0:2, :]
    got_up = []
    for t in range(count):
        got_down[t].wait()
        got_slope[t].wait()
        cols = pl.ds(t * model, model)

        def upward_grad(step, _, t=t, cols=cols):
            at = pl.ds(pl.multiple_of(step * CHUNK, CHUNK), CHUNK)
            got = contract(two_low[at, :], tiles[t], 1, 1) * slope[at, cols].astype(jnp.float32)
            slope[at, cols] = got.astype(jnp.bfloat16)
            sums[5 + t : 6 + t, :] += jnp.sum(got, axis=0, keepdims=True)
            return 0

        lax.fori_loop(0, rows // CHUNK, upward_grad, 0)
        got_up.append(fetch(col_tile(wup_in, t), tiles.at[t]))
    down_one, down_two = r_down.stages()
    down_one[0]()
    got_rest[0].wait()

    def up_grad(step, _):
        weight_grad(r_up, hidden_low, slope, step // count, step % count)
        return 0

    lax.fori_loop(0, count * (model // 384), up_grad, 0)
    r_up.swap()
    got_tokens = fetch(tokens_in, hidden_low)
    for stage in down_one[1:-1]:
        stage()
    for item in got_rest[1:] + got_up:
        item.wait()

    def first_norm(step, _):
        at = pl.ds(pl.multiple_of(step * CHUNK, CHUNK), CHUNK)
        whole = acc[at, :]
        for t in range(count):
            whole = whole + contract(slope[at, t * model : (t + 1) * model], tiles[t], 1, 1)
        unit, scale = normed[at, :].astype(jnp.float32), factor[at, 0:1]
        inner = whole * vecs[4:5, :]
        both = scale * (inner - row_mean(inner) - unit * row_mean(inner * unit))
        acc[at, :] = both
        low = both.astype(jnp.bfloat16)
        two_low[at, :] = low
        sums[2:3, :] += jnp.sum(both, axis=0, keepdims=True)
        sums[3:4, :] += jnp.sum(whole * unit, axis=0, keepdims=True)
        sums[4:5, :] += jnp.sum(whole, axis=0, keepdims=True)
        active[at, pl.ds(3 * model, model)] = contract(low, w_out[...], 1, 1).astype(jnp.bfloat16)
        return 0

    lax.fori_loop(0, rows // CHUNK, first_norm, 0)
    got_context = fetch(context_in, slope.at[:, pl.ds(3 * model, model)])
    got_wqkv = [fetch(col_tile(wqkv_in, t), tiles.at[t]) for t in range(3)]
    up_one, up_two = r_up.stages()
    up_one[0]()

    got_context.wait()

    def out_grad(step, _):
        weight_grad(r_out, slope, two_low, step, 0, 3 * model)
        return 0

    lax.fori_loop(0, model // 384, out_grad, 0)
    r_out.swap()
    fill_bias(seg_row, bias)
    got_qkv.wait()
    out_one, out_two = r_out.stages()

    def pair_back(pair, block):
        at = slice(block * BLOCK, (block + 1) * BLOCK)
        cols = [pl.ds(pl.multiple_of(part * model + pair * 128, 128), 128) for part in range(4)]
        qp, kp, vp, gp = (active[at, col] for col in cols)
        prod = (gp.astype(jnp.float32) * slope[at, cols[3]].astype(jnp.float32)).T
        sum_q = sum_k = sum_v = 0.0
        for head in range(2):
            inner = jnp.sum(prod[head * HEAD_DIM : (head + 1) * HEAD_DIM], axis=0, keepdims=True)
            qh, gh, kh = keep_head(qp, head), keep_head(gp, head), keep_head(kp, head)
            scores = contract(kp, qh, 1, 1)
            if block:
                scores = scores + bias[...]
            prob = jnp.exp(scores - logsum[pl.ds(pair * 2 + head, 1), at])
            raw = (prob * (contract(vp, gh, 1, 1) - inner)).astype(jnp.bfloat16)
            sum_v = sum_v + contract(prob.astype(jnp.bfloat16), gh, 1, 0)
            sum_k = sum_k + contract(raw, qh, 1, 0)
            sum_q = sum_q + contract(raw, kh, 0, 0)
        sum_q = sum_q * HEAD_DIM ** (-0.5)
        for col, got in zip(cols, (sum_q, sum_k, sum_v)):
            slope[at, col] = got.astype(jnp.bfloat16)
        sums[0:1, cols[0]] += jnp.sum(sum_q, axis=0, keepdims=True)
        sums[1:2, cols[0]] += jnp.sum(sum_v, axis=0, keepdims=True)

    hooks = {
        (0, 0): [out_one[0]],
        (0, 1): [down_one[-1]],
        (1, 1): down_two[:1],
        (2, 0): up_one[1:-1],
        (2, 1): down_two[1:-1],
        (3, 0): out_one[1:-1],
        (3, 1): down_two[-1:],
    }

    def attend_back(pair, _):
        for block in range(2):
            pair_back(pair, block)
            for (when, part), todo in hooks.items():
                if part == block:

                    @pl.when(pair == when)
                    def _(todo=todo):
                        for stage in todo:
                            stage()

        return 0

    lax.fori_loop(0, pairs, attend_back, 0)
    got_tokens.wait()
    for item in got_wqkv:
        item.wait()

    def qkv_grad(step, _):
        weight_grad(r_qkv, hidden_low, slope, step // 3, step % 3)
        return 0

    lax.fori_loop(0, 3 * (model // 384), qkv_grad, 0)
    r_qkv.swap()
    small = Sums(p, sums, mine, other, plane, col, sum_sems)
    small.start()
    up_one[-1]()

    def token_grad(step, _):
        at = pl.ds(pl.multiple_of(step * CHUNK, CHUNK), CHUNK)
        whole = acc[at, :]
        for t in range(3):
            whole = whole + contract(slope[at, t * model : (t + 1) * model], tiles[t], 1, 1)
        acc[at, :] = whole
        return 0

    half = rows // CHUNK // 2
    lax.fori_loop(0, half, token_grad, 0)
    qkv_one, qkv_two = r_qkv.stages()
    qkv_one[0]()
    small.across()
    out_one[-1]()
    lax.fori_loop(half, rows // CHUNK, token_grad, 0)
    tokens_out = pltpu.make_async_copy(acc, tokens_o, store.at[0])
    tokens_out.start()
    small.along()
    up_two[0]()
    for stage in qkv_one[1:-1]:
        stage()
    out_two[0]()
    small.land(sums_o)
    for stage in up_two[1:] + out_two[1:]:
        stage()
    qkv_one[-1]()
    for stage in qkv_two:
        stage()
    small.finish()
    for reduce in (r_down, r_up, r_out, r_qkv):
        reduce.finish()
    tokens_out.wait()


def backward(chips, depth, blocks, ins, vmem_ins):
    rows, model = ins[0].shape
    wide = ins[1].shape[1]
    hops = chips // 2
    low, full = jnp.bfloat16, jnp.float32
    shape, dma = jax.ShapeDtypeStruct, pltpu.SemaphoreType.DMA
    bufs = []
    for high, across in blocks:
        whole = depth * across
        bufs += [
            pltpu.VMEM((chips, 2, high, whole), low), pltpu.VMEM((chips, high, whole), low),
            pltpu.VMEM((2, high, whole // 2), low), pltpu.VMEM((2, hops - 1, high, whole), low),
            pltpu.VMEM((depth, high, across), low), pltpu.VMEM((depth + 1, high, across), low),
            pltpu.VMEM((high, across), full),
        ]
    return pl.pallas_call(
        functools.partial(backward_kernel, chips, depth),
        out_shape=[shape((rows, model), full), *(shape(size, full) for size in blocks), shape((16, model), full)],
        in_specs=[ANY] * len(ins) + [VMEM] * len(vmem_ins),
        out_specs=[ANY] * 5 + [VMEM],
        scratch_shapes=[
            pltpu.VMEM((rows, model), low), pltpu.VMEM((rows, wide), low), pltpu.VMEM((rows, wide), low),
            pltpu.VMEM((rows, model), low), pltpu.VMEM((wide // model, model, model), low), pltpu.VMEM((rows, model), full),
            pltpu.VMEM((rows, model), low), pltpu.VMEM((rows, 128), full), pltpu.VMEM((model, model), low),
            pltpu.VMEM((BLOCK, BLOCK), full), pltpu.VMEM((16, model), full),
            *bufs,
            pltpu.VMEM((16, model), full), pltpu.VMEM((16, model), full),
            pltpu.VMEM((chips, 16, model), full), pltpu.VMEM((depth, 16, model), full),
            dma((32,)), dma((1,)), dma((4,)), dma((4,)), dma((4, 2, hops)), dma((4, 2, hops)), dma((4, 2, depth)), dma((4, 2, depth)), dma((4,)),
            dma, dma, dma((chips,)), dma((chips,)), dma((depth,)), dma((depth,)),
        ],
        compiler_params=pltpu.CompilerParams(collective_id=1, has_side_effects=True, vmem_limit_bytes=67043328),
        name="backward",
    )(*ins, *vmem_ins)


def roll_rows(field, start):
    return lax.dynamic_slice_in_dim(jnp.concatenate([field, field]), start, field.shape[0], 0)


def per_device(
    tokens,
    segment,
    w_qkv,
    w_out,
    w_up,
    w_down,
    bias_query,
    bias_value,
    bias_out,
    gain_attn,
    shift_attn,
    bias_up,
    bias_down,
    gain_ffn,
    shift_ffn,
    cotangent,
):
    model = tokens.shape[1]
    tok_rows = tokens.shape[0]
    device_at = lax.axis_index("row") * lax.axis_size("col") + lax.axis_index("col")
    segrow = lax.dynamic_index_in_dim(segment, device_at * tok_rows // LEN, 0, keepdims=False)
    start = jnp.argmax(segrow[: LEN - BLOCK + 1] == segrow[BLOCK - 1 :]).astype(jnp.int32)
    back = (LEN - start).astype(jnp.int32)
    segrow = roll_rows(segrow, start)
    tokens = roll_rows(tokens, start)
    cotangent = roll_rows(cotangent, start)
    seg_row = segrow[None, :]
    vecs = jnp.concatenate(
        [
            jnp.stack([bias_query, jnp.zeros_like(bias_query), bias_value, bias_out, gain_attn, shift_attn, bias_down, gain_ffn, shift_ffn]),
            bias_up.reshape(-1, model),
        ]
    )
    chips, depth = lax.axis_size("row") // 2, lax.axis_size("col")
    (
        output, grad_two, grad_two_low, projected, context, normed_one, hidden_low, active_low, slope,
        attn_qkv, attn_out, ffn_up, ffn_down, logsum, factor_one, sums,
    ) = forward(chips, depth, tokens, cotangent, w_qkv, w_out, w_up, w_down, seg_row, vecs)
    grad_tokens, block_qkv, block_out, block_up, block_down, sums = backward(
        chips, depth,
        (w_qkv.shape, w_out.shape, w_up.shape, w_down.shape),
        (
            grad_two_low, active_low, ffn_down, slope, hidden_low, ffn_up, grad_two, normed_one, factor_one, attn_out, context,
            projected, tokens, attn_qkv,
        ),
        (seg_row, vecs, logsum, sums),
    )
    wide = bias_up.shape[0] // model
    return (
        roll_rows(output, back),
        roll_rows(grad_tokens, back),
        block_qkv,
        block_out,
        block_up,
        block_down,
        sums[0],
        sums[1],
        sums[2],
        sums[3],
        sums[4],
        sums[5 : 5 + wide].reshape(-1),
        sums[9],
        sums[10],
        sums[11],
    )


def solution(mesh):
    return jax.shard_map(
        per_device,
        mesh=mesh,
        in_specs=(
            P(("row", "col"), None),
            P(),
            P("row", "col"),
            P("row", "col"),
            P("row", "col"),
            P("row", "col"),
            P(),
            P(),
            P(),
            P(),
            P(),
            P(),
            P(),
            P(),
            P(),
            P(("row", "col"), None),
        ),
        out_specs=(
            P(("row", "col"), None),
            P(("row", "col"), None),
            P("row", "col"),
            P("row", "col"),
            P("row", "col"),
            P("row", "col"),
            P(),
            P(),
            P(),
            P(),
            P(),
            P(),
            P(),
            P(),
            P(),
        ),
        check_vma=False,
    )
```

```python
import functools

import jax
import jax.numpy as jnp
from jax import lax
from jax.experimental import pallas as pl
from jax.experimental.pallas import tpu as pltpu
from jax.sharding import PartitionSpec as P

HEADS = 12
HEAD_DIM = 64
LEN = 1024


norm_eps = 1e-05
masked_score = -1e30


BLOCK = 512


def contract(left, right, left_dim, right_dim):
    return lax.dot_general(
        left, right, (((left_dim,), (right_dim,)), ((), ())), preferred_element_type=jnp.float32
    )


def keep_head(field, head):
    lane = lax.broadcasted_iota(jnp.int32, field.shape, 1)
    keep = (lane < HEAD_DIM) if head == 0 else (lane >= HEAD_DIM)
    return jnp.where(keep, field, jnp.zeros_like(field))


MESH = pl.DeviceIdType.MESH
ANY = pl.BlockSpec(memory_space=pl.ANY)
CHUNK = 256


class Place:
    def __init__(self, chips, depth):
        self.chips, self.depth, self.hops = chips, depth, chips // 2
        self.row, self.z = lax.axis_index("row"), lax.axis_index("col")
        self.chip, self.core = self.row // 2, self.row % 2
        across = self.chip % 2
        self.pos = self.chip // 2 + across * (chips - 1 - 2 * (self.chip // 2))

    def chip_at(self, pos):
        pos = (pos + self.chips) % self.chips
        far = pos // (self.chips // 2)
        return 2 * (pos + far * (self.chips - 1 - 2 * pos)) + far

    def right(self):
        return (2 * self.chip_at(self.pos + 1) + self.core, self.z)

    def left(self):
        return (2 * self.chip_at(self.pos - 1) + self.core, self.z)

    def mate(self):
        return (self.row + 1 - 2 * self.core, self.z)

    def up(self):
        return (self.row, self.z + 1)

    def down(self):
        return (self.row, self.z - 1)

    def meet(self):
        barrier = pltpu.get_barrier_semaphore()
        for device in (self.right(), self.left(), self.mate()):
            pl.semaphore_signal(barrier, inc=1, device_id=device, device_id_type=MESH)

        @pl.when(self.z < self.depth - 1)
        def _():
            pl.semaphore_signal(barrier, inc=1, device_id=self.up(), device_id_type=MESH)

        @pl.when(self.z > 0)
        def _():
            pl.semaphore_signal(barrier, inc=1, device_id=self.down(), device_id_type=MESH)

        ends = jnp.where(self.z == 0, 1, 0) + jnp.where(self.z == self.depth - 1, 1, 0)
        pl.semaphore_wait(barrier, 5 - ends)

    def meet_all(self):
        barrier = pltpu.get_barrier_semaphore()
        others = [(2 * self.chip_at(self.pos + apart) + self.core, self.z) for apart in range(1, self.chips)]
        others += [(self.row, (self.z + apart) % self.depth) for apart in range(1, self.depth)]
        for device in [*others, self.mate()]:
            pl.semaphore_signal(barrier, inc=1, device_id=device, device_id_type=MESH)
        pl.semaphore_wait(barrier, self.chips + self.depth - 1)


class Gather:
    def __init__(self, place, index, staged, full, sems):
        self.p, self.i, self.staged, self.full = place, index, staged, full
        self.z_send, self.z_recv, self.ring_sent, self.ring_recv, self.core_sent, self.core_recv = sems
        self.rows, self.half = staged.shape[1], full.shape[1] // 2

    def line(self, source, way, step):
        block = self.staged.at[source]
        return pltpu.make_async_remote_copy(
            block, block, self.z_send.at[self.i, way, step], self.z_recv.at[self.i, source],
            device_id=self.p.down() if way else self.p.up(), device_id_type=MESH,
        )

    def open(self):
        p = self.p

        @pl.when(p.z < p.depth - 1)
        def _():
            self.line(p.z, 0, 0).start()

        @pl.when(p.z > 0)
        def _():
            self.line(p.z, 1, 0).start()

    def relay(self):
        p = self.p
        for step in range(1, p.depth):

            @pl.when(p.z - step >= 0)
            def _(step=step):
                self.line(p.z - step, 0, step).wait_recv()

                @pl.when(p.z < p.depth - 1)
                def _():
                    self.line(p.z - step, 0, step).start()

            @pl.when(p.z + step < p.depth)
            def _(step=step):
                self.line(p.z + step, 1, step).wait_recv()

                @pl.when(p.z > 0)
                def _():
                    self.line(p.z + step, 1, step).start()

        rows = pl.ds(pl.multiple_of(p.row * self.rows, self.rows), self.rows)
        self.full[rows, :] = jnp.concatenate([self.staged[z] for z in range(p.depth)], axis=1)

    def line_sent(self):
        p = self.p
        for step in range(p.depth):

            @pl.when((p.z - step >= 0) & (p.z < p.depth - 1))
            def _(step=step):
                self.line(p.z - step, 0, step).wait_send()

            @pl.when((p.z + step < p.depth) & (p.z > 0))
            def _(step=step):
                self.line(p.z + step, 1, step).wait_send()

    def piece(self, hop, way, core):
        p = self.p
        pos = p.pos + hop if way else p.pos - hop
        row = 2 * p.chip_at(pos) + core
        rows = pl.ds(pl.multiple_of(row * self.rows, self.rows), self.rows)
        if hop == p.hops:
            return self.full.at[rows, pl.ds(way * self.half, self.half)]
        return self.full.at[rows, :]

    def ring(self, hop, way):
        p = self.p
        pos = p.pos + hop - 1 if way else p.pos - hop + 1
        row = 2 * p.chip_at(pos) + p.core
        rows = pl.ds(pl.multiple_of(row * self.rows, self.rows), self.rows)
        cols = pl.ds(way * self.half, self.half) if hop == p.hops else slice(None)
        block = self.full.at[rows, cols]
        return pltpu.make_async_remote_copy(
            block, block, self.ring_sent.at[self.i, way, hop - 1], self.ring_recv.at[self.i, way, hop - 1],
            device_id=p.left() if way else p.right(), device_id_type=MESH,
        )

    def landed(self, hop, way):
        block = self.piece(hop, way, self.p.core)
        return pltpu.make_async_remote_copy(
            block, block, self.ring_sent.at[self.i, way, hop - 1], self.ring_recv.at[self.i, way, hop - 1],
            device_id=self.p.left() if way else self.p.right(), device_id_type=MESH,
        )

    def pair(self, hop, way, core):
        block = self.piece(hop, way, core)
        slot = 0 if hop == 0 else 2 * hop - 1 + way
        return pltpu.make_async_remote_copy(
            block, block, self.core_sent.at[self.i, slot], self.core_recv.at[self.i, slot],
            device_id=self.p.mate(), device_id_type=MESH,
        )

    def start_ring(self):
        self.ring(1, 0).start()
        self.ring(1, 1).start()
        self.pair(0, 0, self.p.core).start()

    def advance(self, hop):
        for way in range(2):
            self.landed(hop, way).wait_recv()
            if hop < self.p.hops:
                self.ring(hop + 1, way).start()
            self.pair(hop, way, self.p.core).start()

    def mate_has(self, hop):
        for way in range(1 if hop == 0 else 2):
            self.pair(hop, way, 1 - self.p.core).wait_recv()

    def finish(self):
        self.line_sent()
        self.pair(0, 0, self.p.core).wait_send()
        for hop in range(1, self.p.hops + 1):
            for way in range(2):
                self.ring(hop, way).wait_send()
                self.pair(hop, way, self.p.core).wait_send()


def gelu_parts(value):
    part = 1.0 / (1.0 + jnp.abs(value) * (0.3275911 * 0.5**0.5))
    bell = jnp.exp(value * value * -0.5)
    tail = part * (0.127414796 + part * (-0.142248368 + part * (0.7107068705 + part * (-0.7265760135 + part * 0.5307027145))))
    tail = tail * bell
    below = jnp.where(value >= 0, 1.0 - tail, tail)
    return value * below, below + value * bell * 0.3989422804014327


def row_mean(field):
    return jnp.mean(field, axis=1, keepdims=True)


def fill_bias(seg_row, bias):
    seg_key = seg_row[0:1, BLOCK:]
    seg_query = jnp.broadcast_to(seg_key, (128, BLOCK)).T[:, 0:1]
    bias[...] = jnp.where(seg_query == seg_key, 0.0, masked_score)


def attend_pair(qkv, bias, context, logsum, model, block, pair):
    rows = slice(block * BLOCK, (block + 1) * BLOCK)
    cols = [pl.ds(pl.multiple_of(part * model + pair * 128, 128), 128) for part in range(3)]
    qp, kp, vp = (qkv[rows, col] for col in cols)
    total = 0.0
    for head in range(2):
        scores = contract(keep_head(qp, head), kp, 1, 1)
        if block:
            scores = scores + bias[...]
        peak = jnp.max(scores, axis=1, keepdims=True)
        expo = jnp.exp(scores - peak)
        norm = jnp.sum(expo, axis=1, keepdims=True)
        lse = jnp.broadcast_to(peak + jnp.log(norm), (BLOCK, 128)).T
        logsum[pl.ds(pair * 2 + head, 1), rows] = lse[0:1]
        part = contract(expo.astype(jnp.bfloat16), keep_head(vp, head), 1, 0)
        total = total + part * (1.0 / norm)
    context[rows, cols[0]] = total.astype(jnp.bfloat16)


def find_rows(p, segment, turn, seg_row, start_o):
    own = jnp.broadcast_to(segment[pl.ds(p.row * p.depth + p.z, 1), :].astype(jnp.float32), (16, LEN))
    lane = lax.broadcasted_iota(jnp.int32, (16, LEN), 1)
    ahead = pltpu.roll(own, LEN - BLOCK + 1, 1)
    found = (own == ahead) & (lane <= LEN - BLOCK)
    start = jnp.min(jnp.where(found, lane.astype(jnp.float32), 2.0 * LEN), axis=1, keepdims=True)
    start_o[...] = jnp.broadcast_to(start[:8].astype(jnp.int32), start_o.shape)

    def step(i, _):
        at = pl.ds(pl.multiple_of(i * CHUNK, CHUNK), CHUNK)
        apart = lax.broadcasted_iota(jnp.int32, (CHUNK, LEN), 1) - lax.broadcasted_iota(jnp.int32, (CHUNK, LEN), 0) - i * CHUNK
        apart = apart.astype(jnp.float32) - start[0:1, 0:1]
        turn[at, 0:LEN] = jnp.where((apart == 0.0) | (apart == -1.0 * LEN), 1.0, 0.0).astype(jnp.bfloat16)
        return 0

    lax.fori_loop(0, LEN // CHUNK, step, 0)
    seg_row[...] = contract(own.astype(jnp.bfloat16), turn[:, 0:LEN], 1, 1)


def turn_rows(turn, source, result):
    def step(i, _):
        at = pl.ds(pl.multiple_of(i * CHUNK, CHUNK), CHUNK)
        result[at, :] = contract(turn[at, 0:LEN], source[...], 1, 0).astype(jnp.bfloat16)
        return 0

    lax.fori_loop(0, LEN // CHUNK, step, 0)


def forward_kernel(
    chips, depth,
    tokens_in, cot_in, qkv_in, out_in, up_in, down_in, segment,
    bias_query, bias_value, bias_out, gain_attn, shift_attn, bias_down, gain_ffn, shift_ffn, bias_up,
    output_o, two_o, two_low_o, qkv_o, context_o, normed_o, hidden_low_o, active_o, slope_o,
    wqkv_o, wout_o, wup_o, wdown_o, tokens_o, logsum, factor, sums, seg_row, vecs, start_o,
    tokens, cot, s_qkv, s_out, s_up, s_down, w_qkv, w_out, w_up, w_down,
    qkv, context, bias, hidden, hidden_low, normed, active, slope, two_low, output, down_flat,
    load, store, z_send, z_recv, ring_sent, ring_recv, core_sent, core_recv,
):
    p = Place(chips, depth)
    rows, model = tokens.shape
    pairs = HEADS // 2
    loads = [
        pltpu.make_async_copy(src, dst, load.at[i])
        for i, (src, dst) in enumerate(
            ((qkv_in, s_qkv.at[p.z]), (out_in, s_out.at[p.z]), (up_in, s_up.at[p.z]), (down_in, down_flat), (tokens_in, two_low), (cot_in, output))
        )
    ]
    for item in loads:
        item.start()
    sems = (z_send, z_recv, ring_sent, ring_recv, core_sent, core_recv)
    g_qkv, g_out, g_up, g_down = (
        Gather(p, i, staged, full, sems)
        for i, (staged, full) in enumerate(((s_qkv, w_qkv), (s_out, w_out), (s_up, w_up), (s_down, w_down)))
    )
    stores = []

    def put(src, dst):
        copy = pltpu.make_async_copy(src, dst, store.at[len(stores)])
        copy.start()
        stores.append(copy)

    p.meet()
    loads[0].wait()
    g_qkv.open()
    find_rows(p, segment, active, seg_row, start_o)
    loads[4].wait()
    turn_rows(active, two_low, tokens)
    put(tokens, tokens_o)
    for i in (1, 2, 3, 5):
        loads[i].wait()
    g_qkv.relay()
    g_qkv.start_ring()
    g_out.open()
    g_up.open()
    s_down[p.z] = down_flat[...].astype(jnp.float32).T.astype(jnp.bfloat16)
    turn_rows(active, output, cot)
    for i, vector in enumerate((bias_query, None, bias_value, bias_out, gain_attn, shift_attn, bias_down, gain_ffn, shift_ffn)):
        vecs[i : i + 1, :] = jnp.zeros((1, model), jnp.float32) if vector is None else vector[...].reshape(1, model)
    for i in range(active.shape[1] // model):
        vecs[9 + i : 10 + i, :] = bias_up[i * model : (i + 1) * model].reshape(1, model)
    fill_bias(seg_row, bias)
    g_out.relay()
    for hop in range(1, p.hops):
        g_qkv.advance(hop)
    g_down.open()
    g_out.start_ring()
    g_up.relay()
    g_up.start_ring()
    g_qkv.advance(p.hops)
    for hop in range(p.hops + 1):
        g_qkv.mate_has(hop)
    put(w_qkv, wqkv_o)

    def project(step, _):
        tile, at = step % 3, pl.ds(pl.multiple_of(step // 3 * CHUNK, CHUNK), CHUNK)
        cols = pl.ds(pl.multiple_of(tile * model, model), model)
        got = contract(tokens[at, :], w_qkv[:, cols], 1, 0) + vecs[pl.ds(tile, 1), :]
        got = got * jnp.where(tile == 0, HEAD_DIM ** (-0.5), 1.0)
        qkv[at, cols] = got.astype(jnp.bfloat16)

        @pl.when(step == 2 * (rows // CHUNK))
        def _():
            for hop in range(1, p.hops):
                g_out.advance(hop)

        return 0

    lax.fori_loop(0, 3 * (rows // CHUNK), project, 0)
    put(qkv, qkv_o)

    def attend_first(pair, _):
        attend_pair(qkv, bias, context, logsum, model, 0, pair)

        @pl.when(pair == 0)
        def _():
            g_out.advance(p.hops)

        @pl.when(pair == pairs - 1)
        def _():
            g_down.relay()

        return 0

    lax.fori_loop(0, pairs, attend_first, 0)

    def attend_second(pair, _):
        attend_pair(qkv, bias, context, logsum, model, 1, pair)

        @pl.when(pair == 1)
        def _():
            for hop in range(1, p.hops):
                g_up.advance(hop)
            g_down.start_ring()

        return 0

    lax.fori_loop(0, pairs, attend_second, 0)
    put(context, context_o)
    for hop in range(p.hops + 1):
        g_out.mate_has(hop)
    put(w_out, wout_o)

    def first_norm(step, _):
        at = pl.ds(pl.multiple_of(step * CHUNK, CHUNK), CHUNK)
        resid = contract(context[at, :], w_out[...], 1, 0) + vecs[3:4, :] + tokens[at, :].astype(jnp.float32)
        centre = resid - row_mean(resid)
        scale = lax.rsqrt(row_mean(centre * centre) + norm_eps)
        unit = centre * scale
        normed[at, :] = unit.astype(jnp.bfloat16)
        factor[at, :] = jnp.broadcast_to(scale, (CHUNK, 128))
        value = unit * vecs[4:5, :] + vecs[5:6, :]
        hidden[at, :] = value + vecs[6:7, :]
        hidden_low[at, :] = value.astype(jnp.bfloat16)
        return 0

    lax.fori_loop(0, rows // CHUNK, first_norm, 0)
    put(normed, normed_o)
    put(hidden_low, hidden_low_o)
    g_up.advance(p.hops)
    for hop in range(p.hops + 1):
        g_up.mate_has(hop)
    put(w_up, wup_o)
    tiles = active.shape[1] // model
    steps = tiles * (rows // CHUNK)

    def widen(step, _):
        tile, at = step % tiles, pl.ds(pl.multiple_of(step // tiles * CHUNK, CHUNK), CHUNK)
        cols = pl.ds(pl.multiple_of(tile * model, model), model)
        value = contract(hidden_low[at, :], w_up[:, cols], 1, 0) + vecs[pl.ds(9 + tile, 1), :]
        act, grade = gelu_parts(value)
        active[at, cols] = act.astype(jnp.bfloat16)
        slope[at, cols] = grade.astype(jnp.bfloat16)

        @pl.when(step == steps * 3 // 4)
        def _():
            for hop in range(1, p.hops):
                g_down.advance(hop)

        return 0

    lax.fori_loop(0, steps, widen, 0)
    put(active, active_o)
    put(slope, slope_o)
    deep = 2 * g_down.rows

    def narrow(chip):
        span = pl.ds(pl.multiple_of(chip * deep, deep), deep)

        def step_rows(step, _):
            at = pl.ds(pl.multiple_of(step * CHUNK, CHUNK), CHUNK)
            hidden[at, :] += contract(active[at, span], w_down[span, :], 1, 0)
            return 0

        lax.fori_loop(0, rows // CHUNK, step_rows, 0)

    for hop in range(p.hops):
        g_down.mate_has(hop)
        if hop == p.hops - 1:
            g_down.advance(p.hops)
        for way in range(1 if hop == 0 else 2):
            narrow(p.chip_at(p.pos + hop if way else p.pos - hop))
    g_down.mate_has(p.hops)
    put(w_down, wdown_o)
    narrow(p.chip_at(p.pos + p.hops))
    sums[...] = jnp.zeros_like(sums)

    def second_norm(step, _):
        at = pl.ds(pl.multiple_of(step * CHUNK, CHUNK), CHUNK)
        resid = hidden[at, :]
        centre = resid - row_mean(resid)
        scale = lax.rsqrt(row_mean(centre * centre) + norm_eps)
        unit = centre * scale
        output[at, :] = (unit * vecs[7:8, :] + vecs[8:9, :]).astype(jnp.bfloat16)
        coming = cot[at, :].astype(jnp.float32)
        inner = coming * vecs[7:8, :]
        both = scale * (inner - row_mean(inner) - unit * row_mean(inner * unit))
        hidden[at, :] = both
        two_low[at, :] = both.astype(jnp.bfloat16)
        sums[0:1, :] += jnp.sum(coming * unit, axis=0, keepdims=True)
        sums[1:2, :] += jnp.sum(coming, axis=0, keepdims=True)
        sums[2:3, :] += jnp.sum(both, axis=0, keepdims=True)
        return 0

    lax.fori_loop(0, rows // CHUNK, second_norm, 0)
    put(output, output_o)
    put(hidden, two_o)
    put(two_low, two_low_o)
    for gather in (g_qkv, g_out, g_up, g_down):
        gather.finish()
    for copy in stores:
        copy.wait()


def forward(chips, depth, tokens, cotangent, w_qkv, w_out, w_up, w_down, segment, vectors):
    rows, model = tokens.shape
    low, full = jnp.bfloat16, jnp.float32
    weights = (w_qkv, w_out, w_up, w_down)
    whole = [(2 * chips * w.shape[0], depth * w.shape[1]) for w in weights]
    wide = whole[2][1]
    shape = jax.ShapeDtypeStruct
    outs = [
        shape((rows, model), low), shape((rows, model), full), shape((rows, model), low),
        shape((rows, 3 * model), low), shape((rows, model), low), shape((rows, model), low),
        shape((rows, model), low), shape((rows, wide), low), shape((rows, wide), low),
        *(shape(size, low) for size in whole),
        shape((rows, model), low), shape((HEADS, rows), full), shape((rows, 128), full), shape((8, model), full),
        shape((16, rows), full), shape((16, model), full), shape((8, 128), jnp.int32),
    ]
    hops = chips // 2
    return pl.pallas_call(
        functools.partial(forward_kernel, chips, depth),
        out_shape=outs,
        in_specs=[ANY] * 6 + [VMEM] * (1 + len(vectors)),
        out_specs=[ANY] * 14 + [VMEM] * 6,
        scratch_shapes=[
            pltpu.VMEM((rows, model), low), pltpu.VMEM((rows, model), low),
            *(pltpu.VMEM((depth, *w.shape), low) for w in weights),
            *(pltpu.VMEM(size, low) for size in whole),
            pltpu.VMEM((rows, 3 * model), low), pltpu.VMEM((rows, model), low), pltpu.VMEM((BLOCK, BLOCK), full),
            pltpu.VMEM((rows, model), full), pltpu.VMEM((rows, model), low), pltpu.VMEM((rows, model), low),
            pltpu.VMEM((rows, wide), low), pltpu.VMEM((rows, wide), low),
            pltpu.VMEM((rows, model), low), pltpu.VMEM((rows, model), low), pltpu.VMEM(w_down.shape[::-1], low),
            pltpu.SemaphoreType.DMA((6,)), pltpu.SemaphoreType.DMA((14,)),
            pltpu.SemaphoreType.DMA((4, 2, depth)), pltpu.SemaphoreType.DMA((4, depth)),
            pltpu.SemaphoreType.DMA((4, 2, hops)), pltpu.SemaphoreType.DMA((4, 2, hops)),
            pltpu.SemaphoreType.DMA((4, 2 * hops + 1)), pltpu.SemaphoreType.DMA((4, 2 * hops + 1)),
        ],
        compiler_params=pltpu.CompilerParams(collective_id=0, has_side_effects=True, vmem_limit_bytes=67043328),
        name="forward",
    )(tokens, cotangent, w_qkv, w_out, w_up, w_down.T, segment, *vectors)


VMEM = pl.BlockSpec(memory_space=pltpu.VMEM)


class Reduce:
    def __init__(self, place, index, bufs, result, sems):
        self.p, self.i, self.result = place, index, result
        self.grad, self.other, self.halves, self.fulls, self.parts, self.came, self.total = bufs
        self.core_sent, self.core_recv, self.ring_sent, self.ring_recv, self.z_sent, self.z_recv, self.res_sem = sems
        self.half = self.grad.shape[3] // 2

    def pair(self):
        return pltpu.make_async_remote_copy(
            self.grad.at[:, 1 - self.p.core], self.other, self.core_sent.at[self.i], self.core_recv.at[self.i],
            device_id=self.p.mate(), device_id_type=MESH,
        )

    def swap(self):
        self.pair().start()

    def absorb(self):
        self.pair().wait_recv()

        def step(chip, _):
            both = self.grad[chip, self.p.core].astype(jnp.float32) + self.other[chip].astype(jnp.float32)
            self.grad[chip, self.p.core] = both.astype(jnp.bfloat16)
            return 0

        lax.fori_loop(0, self.p.chips, step, 0)

    def span(self, hop, way):
        return pl.ds((1 - way) * self.half, self.half) if hop == 1 else slice(None)

    def ring(self, hop, way):
        p = self.p
        dest = p.pos - p.hops + hop - 1 if way else p.pos + p.hops - hop + 1
        return pltpu.make_async_remote_copy(
            self.grad.at[p.chip_at(dest), p.core, :, self.span(hop, way)],
            self.halves.at[way] if hop == 1 else self.fulls.at[way, hop - 2],
            self.ring_sent.at[self.i, way, hop - 1], self.ring_recv.at[self.i, way, hop - 1],
            device_id=p.left() if way else p.right(), device_id_type=MESH,
        )

    def go(self, hop):
        self.ring(hop, 0).start()
        self.ring(hop, 1).start()

    def take(self, hop):
        p = self.p
        for way in range(2):
            self.ring(hop, way).wait_recv()
            chip = p.chip_at(p.pos - p.hops + hop if way else p.pos + p.hops - hop)
            got = self.halves[way] if hop == 1 else self.fulls[way, hop - 2]
            cols = self.span(hop, way)
            both = self.grad[chip, p.core, :, cols].astype(jnp.float32) + got.astype(jnp.float32)
            self.grad[chip, p.core, :, cols] = both.astype(jnp.bfloat16)

    def split(self):
        p = self.p
        self.ring(p.hops, 0).wait_recv()
        self.ring(p.hops, 1).wait_recv()
        last = p.hops - 2
        low = (
            self.grad[p.chip, p.core].astype(jnp.float32)
            + self.fulls[0, last].astype(jnp.float32)
            + self.fulls[1, last].astype(jnp.float32)
        ).astype(jnp.bfloat16)
        wide = self.parts.shape[2]
        for z in range(p.depth):
            self.parts[z] = low[:, z * wide : (z + 1) * wide]

    def line(self, block, way):
        return pltpu.make_async_remote_copy(
            self.parts.at[block], self.came.at[block + 1 - way],
            self.z_sent.at[self.i, way, block], self.z_recv.at[self.i, way, block],
            device_id=self.p.down() if way else self.p.up(), device_id_type=MESH,
        )

    def round(self, turn):
        p = self.p
        for way in range(2):
            far = p.depth - 1 - p.z if way else p.z
            block = turn - far if way else p.depth - 1 - turn + far

            @pl.when(far <= turn)
            def _(far=far, block=block, way=way):
                @pl.when(far > 0)
                def _():
                    self.line(block, way).wait_recv()
                    both = self.parts[block].astype(jnp.float32) + self.came[block + 1 - way].astype(jnp.float32)
                    self.parts[block] = both.astype(jnp.bfloat16)

                self.line(block, way).start()

    def write(self):
        return pltpu.make_async_copy(self.total, self.result, self.res_sem.at[self.i])

    def land(self):
        p = self.p
        self.total[...] = self.parts[p.z].astype(jnp.float32)

        @pl.when(p.z > 0)
        def _():
            self.line(p.z, 0).wait_recv()
            self.total[...] += self.came[p.z + 1].astype(jnp.float32)

        @pl.when(p.z < p.depth - 1)
        def _():
            self.line(p.z, 1).wait_recv()
            self.total[...] += self.came[p.z].astype(jnp.float32)

        self.write().start()

    def finish(self):
        p = self.p
        self.pair().wait_send()
        for hop in range(1, p.hops + 1):
            for way in range(2):
                self.ring(hop, way).wait_send()
        for turn in range(p.depth - 1):
            for way in range(2):
                far = p.depth - 1 - p.z if way else p.z
                block = turn - far if way else p.depth - 1 - turn + far

                @pl.when(far <= turn)
                def _(block=block, way=way):
                    self.line(block, way).wait_send()

        self.write().wait()

    def stages(self):
        def first():
            self.absorb()
            self.go(1)

        def along(hop):
            self.take(hop)
            self.go(hop + 1)

        def begin():
            self.split()
            self.round(0)

        p = self.p
        return [
            [first, *(functools.partial(along, hop) for hop in range(1, p.hops)), begin],
            [*(functools.partial(self.round, turn) for turn in range(1, p.depth - 1)), self.land],
        ]


class Sums:
    def __init__(self, place, sums, mine, pair, plane, line, sems):
        self.p, self.sums, self.mine, self.other, self.plane, self.col = place, sums, mine, pair, plane, line
        self.pair_sent, self.pair_recv, self.plane_sent, self.plane_recv, self.col_sent, self.col_recv = sems

    def pair(self):
        return pltpu.make_async_remote_copy(
            self.mine, self.other, self.pair_sent, self.pair_recv, device_id=self.p.mate(), device_id_type=MESH
        )

    def chip(self, apart, source):
        target = (2 * self.p.chip_at(self.p.pos + apart) + self.p.core, self.p.z)
        return pltpu.make_async_remote_copy(
            self.plane.at[source], self.plane.at[source], self.plane_sent.at[apart], self.plane_recv.at[source],
            device_id=target, device_id_type=MESH,
        )

    def level(self, apart, source):
        target = (self.p.row, (self.p.z + apart) % self.p.depth)
        return pltpu.make_async_remote_copy(
            self.col.at[source], self.col.at[source], self.col_sent.at[apart], self.col_recv.at[source],
            device_id=target, device_id_type=MESH,
        )

    def start(self):
        self.mine[...] = self.sums[...]
        self.pair().start()

    def across(self):
        p = self.p
        self.pair().wait_recv()
        self.plane[p.chip] = self.mine[...] + self.other[...]
        for apart in range(1, p.chips):
            self.chip(apart, p.chip).start()

    def along(self):
        p = self.p
        for apart in range(1, p.chips):
            self.chip(apart, p.chip_at(p.pos + apart)).wait_recv()
        total = self.plane[0]
        for chip in range(1, p.chips):
            total = total + self.plane[chip]
        self.col[p.z] = total
        for apart in range(1, p.depth):
            self.level(apart, p.z).start()

    def land(self, result):
        p = self.p
        for apart in range(1, p.depth):
            self.level(apart, (p.z + apart) % p.depth).wait_recv()
        total = self.col[0]
        for z in range(1, p.depth):
            total = total + self.col[z]
        result[...] = total

    def finish(self):
        p = self.p
        self.pair().wait_send()
        for apart in range(1, p.chips):
            self.chip(apart, p.chip).wait_send()
        for apart in range(1, p.depth):
            self.level(apart, p.z).wait_send()


def backward_kernel(
    chips, depth,
    two_low_in, active_in, wdown_in, slope_in, hidden_low_in, wup_in, two_in, normed_in, factor_in, wout_in, context_in,
    qkv_in, tokens_in, wqkv_in, seg_row, vecs, logsum, sums_in,
    tokens_o, qkv_o, out_o, up_o, down_o, sums_o,
    two_low, active, slope, hidden_low, tiles, acc, normed, factor, w_out, bias, sums,
    *rest,
):
    p = Place(chips, depth)
    groups = [rest[7 * i : 7 * i + 7] for i in range(4)]
    mine, other, plane, col = rest[28:32]
    load, store, core_sent, core_recv, ring_sent, ring_recv, z_sent, z_recv, res_sem = rest[32:41]
    sum_sems = rest[41:47]
    rows, model = two_low.shape
    wide = active.shape[1]
    count = wide // model
    pairs = HEADS // 2
    sems = (core_sent, core_recv, ring_sent, ring_recv, z_sent, z_recv, res_sem)
    r_qkv, r_out, r_up, r_down = (
        Reduce(p, i, bufs, result, sems) for i, (bufs, result) in enumerate(zip(groups, (qkv_o, out_o, up_o, down_o)))
    )
    used = []

    def fetch(src, dst):
        copy = pltpu.make_async_copy(src, dst, load.at[len(used)])
        copy.start()
        used.append(copy)
        return copy

    def col_tile(ref, tile):
        return ref.at[:, pl.ds(tile * model, model)]

    got_two_low = fetch(two_low_in, two_low)
    got_active = [fetch(col_tile(active_in, t), col_tile(active, t)) for t in range(count)]
    got_down = [fetch(wdown_in.at[pl.ds(t * model, model), :], tiles.at[t]) for t in range(count)]
    got_slope = [fetch(col_tile(slope_in, t), col_tile(slope, t)) for t in range(count)]
    got_rest = [
        fetch(src, dst)
        for src, dst in ((hidden_low_in, hidden_low), (two_in, acc), (normed_in, normed), (factor_in, factor), (wout_in, w_out))
    ]
    p.meet_all()

    def weight_grad(reduce, left, right, left_at, tile, skip=0):
        piece = 384
        cols = pl.ds(pl.multiple_of(tile * model, model), model)
        got = contract(left[:, pl.ds(pl.multiple_of(skip + left_at * piece, 128), piece)], right[:, cols], 0, 0)
        high = reduce.grad.shape[2]
        for s in range(piece // high):
            row = left_at * (piece // high) + s
            reduce.grad[row // 2, row % 2, :, cols] = got[s * high : (s + 1) * high].astype(jnp.bfloat16)

    got_two_low.wait()
    for t in range(count):
        got_active[t].wait()

        def down_grad(step, _, t=t):
            weight_grad(r_down, active, two_low, t * (model // 384) + step, 0)
            return 0

        lax.fori_loop(0, model // 384, down_grad, 0)
    r_down.swap()
    got_qkv = fetch(qkv_in, active.at[:, pl.ds(0, 3 * model)])
    sums[...] = jnp.zeros_like(sums)
    sums[9:10, :] = sums_in[2:3, :]
    sums[10:12, :] = sums_in[0:2, :]
    got_up = []
    for t in range(count):
        got_down[t].wait()
        got_slope[t].wait()
        cols = pl.ds(t * model, model)

        def upward_grad(step, _, t=t, cols=cols):
            at = pl.ds(pl.multiple_of(step * CHUNK, CHUNK), CHUNK)
            got = contract(two_low[at, :], tiles[t], 1, 1) * slope[at, cols].astype(jnp.float32)
            slope[at, cols] = got.astype(jnp.bfloat16)
            sums[5 + t : 6 + t, :] += jnp.sum(got, axis=0, keepdims=True)
            return 0

        lax.fori_loop(0, rows // CHUNK, upward_grad, 0)
        got_up.append(fetch(col_tile(wup_in, t), tiles.at[t]))
    down_one, down_two = r_down.stages()
    down_one[0]()
    got_rest[0].wait()

    def up_grad(step, _):
        weight_grad(r_up, hidden_low, slope, step // count, step % count)
        return 0

    lax.fori_loop(0, count * (model // 384), up_grad, 0)
    r_up.swap()
    got_tokens = fetch(tokens_in, hidden_low)
    for stage in down_one[1:-1]:
        stage()
    for item in got_rest[1:] + got_up:
        item.wait()

    def first_norm(step, _):
        at = pl.ds(pl.multiple_of(step * CHUNK, CHUNK), CHUNK)
        whole = acc[at, :]
        for t in range(count):
            whole = whole + contract(slope[at, t * model : (t + 1) * model], tiles[t], 1, 1)
        unit, scale = normed[at, :].astype(jnp.float32), factor[at, 0:1]
        inner = whole * vecs[4:5, :]
        both = scale * (inner - row_mean(inner) - unit * row_mean(inner * unit))
        acc[at, :] = both
        low = both.astype(jnp.bfloat16)
        two_low[at, :] = low
        sums[2:3, :] += jnp.sum(both, axis=0, keepdims=True)
        sums[3:4, :] += jnp.sum(whole * unit, axis=0, keepdims=True)
        sums[4:5, :] += jnp.sum(whole, axis=0, keepdims=True)
        active[at, pl.ds(3 * model, model)] = contract(low, w_out[...], 1, 1).astype(jnp.bfloat16)
        return 0

    lax.fori_loop(0, rows // CHUNK, first_norm, 0)
    got_context = fetch(context_in, slope.at[:, pl.ds(3 * model, model)])
    got_wqkv = [fetch(col_tile(wqkv_in, t), tiles.at[t]) for t in range(3)]
    up_one, up_two = r_up.stages()
    up_one[0]()

    got_context.wait()

    def out_grad(step, _):
        weight_grad(r_out, slope, two_low, step, 0, 3 * model)
        return 0

    lax.fori_loop(0, model // 384, out_grad, 0)
    r_out.swap()
    fill_bias(seg_row, bias)
    got_qkv.wait()
    out_one, out_two = r_out.stages()

    def pair_back(pair, block):
        at = slice(block * BLOCK, (block + 1) * BLOCK)
        cols = [pl.ds(pl.multiple_of(part * model + pair * 128, 128), 128) for part in range(4)]
        qp, kp, vp, gp = (active[at, col] for col in cols)
        prod = (gp.astype(jnp.float32) * slope[at, cols[3]].astype(jnp.float32)).T
        sum_q = sum_k = sum_v = 0.0
        for head in range(2):
            inner = jnp.sum(prod[head * HEAD_DIM : (head + 1) * HEAD_DIM], axis=0, keepdims=True)
            qh, gh, kh = keep_head(qp, head), keep_head(gp, head), keep_head(kp, head)
            scores = contract(kp, qh, 1, 1)
            if block:
                scores = scores + bias[...]
            prob = jnp.exp(scores - logsum[pl.ds(pair * 2 + head, 1), at])
            raw = (prob * (contract(vp, gh, 1, 1) - inner)).astype(jnp.bfloat16)
            sum_v = sum_v + contract(prob.astype(jnp.bfloat16), gh, 1, 0)
            sum_k = sum_k + contract(raw, qh, 1, 0)
            sum_q = sum_q + contract(raw, kh, 0, 0)
        sum_q = sum_q * HEAD_DIM ** (-0.5)
        for col, got in zip(cols, (sum_q, sum_k, sum_v)):
            slope[at, col] = got.astype(jnp.bfloat16)
        sums[0:1, cols[0]] += jnp.sum(sum_q, axis=0, keepdims=True)
        sums[1:2, cols[0]] += jnp.sum(sum_v, axis=0, keepdims=True)

    hooks = {
        (0, 0): [out_one[0]],
        (0, 1): [down_one[-1]],
        (1, 1): down_two[:1],
        (2, 0): up_one[1:-1],
        (2, 1): down_two[1:-1],
        (3, 0): out_one[1:-1],
        (3, 1): down_two[-1:],
    }

    def attend_back(pair, _):
        for block in range(2):
            pair_back(pair, block)
            for (when, part), todo in hooks.items():
                if part == block:

                    @pl.when(pair == when)
                    def _(todo=todo):
                        for stage in todo:
                            stage()

        return 0

    lax.fori_loop(0, pairs, attend_back, 0)
    got_tokens.wait()
    for item in got_wqkv:
        item.wait()

    def qkv_grad(step, _):
        weight_grad(r_qkv, hidden_low, slope, step // 3, step % 3)
        return 0

    lax.fori_loop(0, 3 * (model // 384), qkv_grad, 0)
    r_qkv.swap()
    small = Sums(p, sums, mine, other, plane, col, sum_sems)
    small.start()
    up_one[-1]()

    def token_grad(step, _):
        at = pl.ds(pl.multiple_of(step * CHUNK, CHUNK), CHUNK)
        whole = acc[at, :]
        for t in range(3):
            whole = whole + contract(slope[at, t * model : (t + 1) * model], tiles[t], 1, 1)
        acc[at, :] = whole
        return 0

    half = rows // CHUNK // 2
    lax.fori_loop(0, half, token_grad, 0)
    qkv_one, qkv_two = r_qkv.stages()
    qkv_one[0]()
    small.across()
    out_one[-1]()
    lax.fori_loop(half, rows // CHUNK, token_grad, 0)
    tokens_out = pltpu.make_async_copy(acc, tokens_o, store.at[0])
    tokens_out.start()
    small.along()
    up_two[0]()
    for stage in qkv_one[1:-1]:
        stage()
    out_two[0]()
    small.land(sums_o)
    for stage in up_two[1:] + out_two[1:]:
        stage()
    qkv_one[-1]()
    for stage in qkv_two:
        stage()
    small.finish()
    for reduce in (r_down, r_up, r_out, r_qkv):
        reduce.finish()
    tokens_out.wait()


def backward(chips, depth, blocks, ins, vmem_ins):
    rows, model = ins[0].shape
    wide = ins[1].shape[1]
    hops = chips // 2
    low, full = jnp.bfloat16, jnp.float32
    shape, dma = jax.ShapeDtypeStruct, pltpu.SemaphoreType.DMA
    bufs = []
    for high, across in blocks:
        whole = depth * across
        bufs += [
            pltpu.VMEM((chips, 2, high, whole), low), pltpu.VMEM((chips, high, whole), low),
            pltpu.VMEM((2, high, whole // 2), low), pltpu.VMEM((2, hops - 1, high, whole), low),
            pltpu.VMEM((depth, high, across), low), pltpu.VMEM((depth + 1, high, across), low),
            pltpu.VMEM((high, across), full),
        ]
    return pl.pallas_call(
        functools.partial(backward_kernel, chips, depth),
        out_shape=[shape((rows, model), full), *(shape(size, full) for size in blocks), shape((16, model), full)],
        in_specs=[ANY] * len(ins) + [VMEM] * len(vmem_ins),
        out_specs=[ANY] * 5 + [VMEM],
        scratch_shapes=[
            pltpu.VMEM((rows, model), low), pltpu.VMEM((rows, wide), low), pltpu.VMEM((rows, wide), low),
            pltpu.VMEM((rows, model), low), pltpu.VMEM((wide // model, model, model), low), pltpu.VMEM((rows, model), full),
            pltpu.VMEM((rows, model), low), pltpu.VMEM((rows, 128), full), pltpu.VMEM((model, model), low),
            pltpu.VMEM((BLOCK, BLOCK), full), pltpu.VMEM((16, model), full),
            *bufs,
            pltpu.VMEM((16, model), full), pltpu.VMEM((16, model), full),
            pltpu.VMEM((chips, 16, model), full), pltpu.VMEM((depth, 16, model), full),
            dma((32,)), dma((1,)), dma((4,)), dma((4,)), dma((4, 2, hops)), dma((4, 2, hops)), dma((4, 2, depth)), dma((4, 2, depth)), dma((4,)),
            dma, dma, dma((chips,)), dma((chips,)), dma((depth,)), dma((depth,)),
        ],
        compiler_params=pltpu.CompilerParams(collective_id=1, has_side_effects=True, vmem_limit_bytes=67043328),
        name="backward",
    )(*ins, *vmem_ins)


def finish_kernel(
    start_in, output_in, tokens_in, qkv_in, out_in, up_in, down_in, sums,
    output_o, tokens_o, qkv_o, out_o, up_o, down_o, *rest,
):
    vectors, (low, wide, grad, done_low, done, qkv, out, up, down, load, store) = rest[:9], rest[9:]
    rows, model = low.shape
    loads = [
        pltpu.make_async_copy(src, dst, load.at[i])
        for i, (src, dst) in enumerate(
            ((output_in, low), (tokens_in, grad.at[pl.ds(0, rows), :]), (tokens_in.at[pl.ds(0, 32), :], grad.at[pl.ds(rows, 32), :]), (qkv_in, qkv), (out_in, out), (up_in, up), (down_in, down))
        )
    ]
    for item in loads:
        item.start()
    stores = []

    def put(src, dst):
        copy = pltpu.make_async_copy(src, dst, store.at[len(stores)])
        copy.start()
        stores.append(copy)

    for i, vector in enumerate(vectors):
        row = i if i < 6 else i + 3
        for j in range(vector.shape[0] // model):
            vector[j * model : (j + 1) * model] = sums[row + j : row + j + 1, :].reshape(model)
    start = start_in[0, 0]
    loads[0].wait()

    def widen(i, _):
        at = pl.ds(pl.multiple_of(i * 64, 64), 64)
        wide[at, :] = low[at, :].astype(jnp.float32)
        return 0

    lax.fori_loop(0, rows // 64, widen, 0)
    wide[rows:, :] = wide[0:32, :]

    over = lax.rem(rows - start, 8)
    early = lax.broadcasted_iota(jnp.int32, (8, model), 0) < 8 - over

    def turn(source, result, i):
        for j in range(2):
            at = i * 64 + j * 32
            came = pl.multiple_of(lax.rem(at + rows - start - over, rows), 8)
            field = source[pl.ds(came, 40), :]
            parts = [pltpu.roll(field[8 * k : 8 * k + 8], lax.rem(8 - over, 8), 0) for k in range(5)]
            whole = jnp.concatenate([jnp.where(early, parts[k], parts[k + 1]) for k in range(4)])
            result[pl.ds(pl.multiple_of(at, 32), 32), :] = whole.astype(result.dtype)

    for source, result, dst, waits in ((wide, done_low, output_o, ()), (grad, done, tokens_o, (1, 2))):
        for i in waits:
            loads[i].wait()
        for part in range(4):
            deep = rows // 4

            def step(i, _, source=source, result=result):
                turn(source, result, i)
                return 0

            lax.fori_loop(part * (deep // 64), (part + 1) * (deep // 64), step, 0)
            at = pl.ds(part * deep, deep)
            put(result.at[at, :], dst.at[at, :])
        if not waits:
            for i, (src, dst) in enumerate(((qkv, qkv_o), (out, out_o), (up, up_o))):
                loads[3 + i].wait()
                put(src, dst)
    loads[6].wait()
    down_o[...] = down[...].T
    for copy in stores:
        copy.wait()


def finish(start, output, grad_tokens, grads, sums, wide):
    rows, model = output.shape
    low, full = jnp.bfloat16, jnp.float32
    shape = jax.ShapeDtypeStruct
    flipped = grads[3].shape[::-1]
    return pl.pallas_call(
        finish_kernel,
        out_shape=[
            shape((rows, model), low), shape((rows, model), full), *(shape(g.shape, full) for g in grads[:3]), shape(flipped, full),
            *(shape((model,), full) for _ in range(5)), shape((wide,), full), *(shape((model,), full) for _ in range(3)),
        ],
        in_specs=[pl.BlockSpec(memory_space=pltpu.SMEM)] + [ANY] * 6 + [VMEM],
        out_specs=[ANY] * 5 + [VMEM] * 10,
        scratch_shapes=[
            pltpu.VMEM((rows, model), low), pltpu.VMEM((rows + 32, model), full), pltpu.VMEM((rows + 32, model), full),
            pltpu.VMEM((rows, model), low), pltpu.VMEM((rows, model), full), *(pltpu.VMEM(g.shape, full) for g in grads),
            pltpu.SemaphoreType.DMA((7,)), pltpu.SemaphoreType.DMA((11,)),
        ],
        compiler_params=pltpu.CompilerParams(vmem_limit_bytes=67043328),
        name="finish",
    )(start, output, grad_tokens, *grads, sums)


def per_device(
    tokens,
    segment,
    w_qkv,
    w_out,
    w_up,
    w_down,
    bias_query,
    bias_value,
    bias_out,
    gain_attn,
    shift_attn,
    bias_up,
    bias_down,
    gain_ffn,
    shift_ffn,
    cotangent,
):
    chips, depth = lax.axis_size("row") // 2, lax.axis_size("col")
    (
        output, grad_two, grad_two_low, projected, context, normed_one, hidden_low, active_low, slope,
        attn_qkv, attn_out, ffn_up, ffn_down, turned, logsum, factor_one, sums, seg_row, vecs, start,
    ) = forward(
        chips, depth, tokens, cotangent, w_qkv, w_out, w_up, w_down, segment,
        (bias_query, bias_value, bias_out, gain_attn, shift_attn, bias_down, gain_ffn, shift_ffn, bias_up),
    )
    grad_tokens, *grads, sums = backward(
        chips, depth,
        (w_qkv.shape, w_out.shape, w_up.shape, w_down.shape),
        (
            grad_two_low, active_low, ffn_down, slope, hidden_low, ffn_up, grad_two, normed_one, factor_one, attn_out, context,
            projected, turned, attn_qkv,
        ),
        (seg_row, vecs, logsum, sums),
    )
    done = finish(start, output, grad_tokens, grads, sums, bias_up.shape[0])
    return (*done[:5], done[5].T, *done[6:])


def solution(mesh):
    return jax.shard_map(
        per_device,
        mesh=mesh,
        in_specs=(
            P(("row", "col"), None),
            P(),
            P("row", "col"),
            P("row", "col"),
            P("row", "col"),
            P("row", "col"),
            P(),
            P(),
            P(),
            P(),
            P(),
            P(),
            P(),
            P(),
            P(),
            P(("row", "col"), None),
        ),
        out_specs=(
            P(("row", "col"), None),
            P(("row", "col"), None),
            P("row", "col"),
            P("row", "col"),
            P("row", "col"),
            P("row", "col"),
            P(),
            P(),
            P(),
            P(),
            P(),
            P(),
            P(),
            P(),
            P(),
        ),
        check_vma=False,
    )
```

```python
import functools

import jax
import jax.numpy as jnp
from jax import lax
from jax.experimental import pallas as pl
from jax.experimental.pallas import tpu as pltpu
from jax.sharding import PartitionSpec as P

HEADS = 12
HEAD_DIM = 64
LEN = 1024


norm_eps = 1e-05
masked_score = -1e30


BLOCK = 512


def contract(left, right, left_dim, right_dim):
    return lax.dot_general(
        left, right, (((left_dim,), (right_dim,)), ((), ())), preferred_element_type=jnp.float32
    )


def keep_head(field, head):
    lane = lax.broadcasted_iota(jnp.int32, field.shape, 1)
    keep = (lane < HEAD_DIM) if head == 0 else (lane >= HEAD_DIM)
    return jnp.where(keep, field, jnp.zeros_like(field))


MESH = pl.DeviceIdType.MESH
ANY = pl.BlockSpec(memory_space=pl.ANY)
CHUNK = 256
EARLY = 512
UP_AT = 6
DOWN_AT = 12
DT = 2
FN = 0
H_UP = 2
H_OUT = 5


class Place:
    def __init__(self, chips, depth):
        self.chips, self.depth, self.hops = chips, depth, chips // 2
        self.row, self.z = lax.axis_index("row"), lax.axis_index("col")
        self.chip, self.core = self.row // 2, self.row % 2
        across = self.chip % 2
        self.pos = self.chip // 2 + across * (chips - 1 - 2 * (self.chip // 2))

    def chip_at(self, pos):
        pos = (pos + self.chips) % self.chips
        far = pos // (self.chips // 2)
        return 2 * (pos + far * (self.chips - 1 - 2 * pos)) + far

    def order(self):
        apart = [self.hops] + [way * hop for hop in range(self.hops - 1, 0, -1) for way in (1, -1)] + [0]
        return [self.chip_at(self.pos + hop) for hop in apart]

    def right(self):
        return (2 * self.chip_at(self.pos + 1) + self.core, self.z)

    def left(self):
        return (2 * self.chip_at(self.pos - 1) + self.core, self.z)

    def mate(self):
        return (self.row + 1 - 2 * self.core, self.z)

    def up(self):
        return (self.row, self.z + 1)

    def down(self):
        return (self.row, self.z - 1)

    def meet(self):
        barrier = pltpu.get_barrier_semaphore()
        for device in (self.right(), self.left(), self.mate()):
            pl.semaphore_signal(barrier, inc=1, device_id=device, device_id_type=MESH)

        @pl.when(self.z < self.depth - 1)
        def _():
            pl.semaphore_signal(barrier, inc=1, device_id=self.up(), device_id_type=MESH)

        @pl.when(self.z > 0)
        def _():
            pl.semaphore_signal(barrier, inc=1, device_id=self.down(), device_id_type=MESH)

        ends = jnp.where(self.z == 0, 1, 0) + jnp.where(self.z == self.depth - 1, 1, 0)
        pl.semaphore_wait(barrier, 5 - ends)

    def meet_all(self):
        barrier = pltpu.get_barrier_semaphore()
        others = [(2 * self.chip_at(self.pos + apart) + self.core, self.z) for apart in range(1, self.chips)]
        others += [(self.row, (self.z + apart) % self.depth) for apart in range(1, self.depth)]
        for device in [*others, self.mate()]:
            pl.semaphore_signal(barrier, inc=1, device_id=device, device_id_type=MESH)
        pl.semaphore_wait(barrier, self.chips + self.depth - 1)


class Gather:
    def __init__(self, place, index, staged, full, sems):
        self.p, self.i, self.staged, self.full = place, index, staged, full
        self.z_send, self.z_recv, self.ring_sent, self.ring_recv, self.core_sent, self.core_recv = sems
        self.rows, self.half = staged.shape[1], full.shape[1] // 2

    def line(self, source, way, step):
        block = self.staged.at[source]
        return pltpu.make_async_remote_copy(
            block, block, self.z_send.at[self.i, way, step], self.z_recv.at[self.i, source],
            device_id=self.p.down() if way else self.p.up(), device_id_type=MESH,
        )

    def open(self):
        p = self.p

        @pl.when(p.z < p.depth - 1)
        def _():
            self.line(p.z, 0, 0).start()

        @pl.when(p.z > 0)
        def _():
            self.line(p.z, 1, 0).start()

    def relay(self, part):
        p = self.p
        for step in (range(1, 2), range(2, p.depth - 1), range(max(2, p.depth - 1), p.depth))[part]:

            @pl.when(p.z - step >= 0)
            def _(step=step):
                self.line(p.z - step, 0, step).wait_recv()

                @pl.when(p.z < p.depth - 1)
                def _():
                    self.line(p.z - step, 0, step).start()

            @pl.when(p.z + step < p.depth)
            def _(step=step):
                self.line(p.z + step, 1, step).wait_recv()

                @pl.when(p.z > 0)
                def _():
                    self.line(p.z + step, 1, step).start()

        if part == 2:
            rows = pl.ds(pl.multiple_of(p.row * self.rows, self.rows), self.rows)
            self.full[rows, :] = jnp.concatenate([self.staged[z] for z in range(p.depth)], axis=1)

    def line_sent(self):
        p = self.p
        for step in range(p.depth):

            @pl.when((p.z - step >= 0) & (p.z < p.depth - 1))
            def _(step=step):
                self.line(p.z - step, 0, step).wait_send()

            @pl.when((p.z + step < p.depth) & (p.z > 0))
            def _(step=step):
                self.line(p.z + step, 1, step).wait_send()

    def piece(self, hop, way, core):
        p = self.p
        pos = p.pos + hop if way else p.pos - hop
        row = 2 * p.chip_at(pos) + core
        rows = pl.ds(pl.multiple_of(row * self.rows, self.rows), self.rows)
        if hop == p.hops:
            return self.full.at[rows, pl.ds(way * self.half, self.half)]
        return self.full.at[rows, :]

    def ring(self, hop, way):
        p = self.p
        pos = p.pos + hop - 1 if way else p.pos - hop + 1
        row = 2 * p.chip_at(pos) + p.core
        rows = pl.ds(pl.multiple_of(row * self.rows, self.rows), self.rows)
        cols = pl.ds(way * self.half, self.half) if hop == p.hops else slice(None)
        block = self.full.at[rows, cols]
        return pltpu.make_async_remote_copy(
            block, block, self.ring_sent.at[self.i, way, hop - 1], self.ring_recv.at[self.i, way, hop - 1],
            device_id=p.left() if way else p.right(), device_id_type=MESH,
        )

    def landed(self, hop, way):
        block = self.piece(hop, way, self.p.core)
        return pltpu.make_async_remote_copy(
            block, block, self.ring_sent.at[self.i, way, hop - 1], self.ring_recv.at[self.i, way, hop - 1],
            device_id=self.p.left() if way else self.p.right(), device_id_type=MESH,
        )

    def pair(self, hop, way, core):
        block = self.piece(hop, way, core)
        slot = 0 if hop == 0 else 2 * hop - 1 + way
        return pltpu.make_async_remote_copy(
            block, block, self.core_sent.at[self.i, slot], self.core_recv.at[self.i, slot],
            device_id=self.p.mate(), device_id_type=MESH,
        )

    def start_ring(self):
        self.ring(1, 0).start()
        self.ring(1, 1).start()
        self.pair(0, 0, self.p.core).start()

    def advance(self, hop):
        for way in range(2):
            self.landed(hop, way).wait_recv()
            if hop < self.p.hops:
                self.ring(hop + 1, way).start()
            self.pair(hop, way, self.p.core).start()

    def mate_has(self, hop):
        for way in range(1 if hop == 0 else 2):
            self.pair(hop, way, 1 - self.p.core).wait_recv()

    def finish(self):
        self.line_sent()
        self.pair(0, 0, self.p.core).wait_send()
        for hop in range(1, self.p.hops + 1):
            for way in range(2):
                self.ring(hop, way).wait_send()
                self.pair(hop, way, self.p.core).wait_send()


def gelu_parts(value):
    part = 1.0 / (1.0 + jnp.abs(value) * (0.3275911 * 0.5**0.5))
    bell = jnp.exp(value * value * -0.5)
    tail = part * (0.127414796 + part * (-0.142248368 + part * (0.7107068705 + part * (-0.7265760135 + part * 0.5307027145))))
    tail = tail * bell
    below = jnp.where(value >= 0, 1.0 - tail, tail)
    return value * below, below + value * bell * 0.3989422804014327


def row_mean(field):
    return jnp.mean(field, axis=1, keepdims=True)


def fill_bias(seg_row, bias):
    seg_key = seg_row[0:1, BLOCK:]
    seg_query = jnp.broadcast_to(seg_key, (128, BLOCK)).T[:, 0:1]
    bias[...] = jnp.where(seg_query == seg_key, 0.0, masked_score)


def attend_pair(qkv, bias, context, logsum, model, block, pair):
    rows = slice(block * BLOCK, (block + 1) * BLOCK)
    cols = [pl.ds(pl.multiple_of(part * model + pair * 128, 128), 128) for part in range(3)]
    qp, kp, vp = (qkv[rows, col] for col in cols)
    total = 0.0
    for head in range(2):
        scores = contract(keep_head(qp, head), kp, 1, 1)
        if block:
            scores = scores + bias[...]
        peak = jnp.max(scores, axis=1, keepdims=True)
        expo = jnp.exp(scores - peak)
        norm = jnp.sum(expo, axis=1, keepdims=True)
        lse = jnp.broadcast_to(peak + jnp.log(norm), (BLOCK, 128)).T
        logsum[pl.ds(pair * 2 + head, 1), rows] = lse[0:1]
        part = contract(expo.astype(jnp.bfloat16), keep_head(vp, head), 1, 0)
        total = total + part * (1.0 / norm)
    context[rows, cols[0]] = total.astype(jnp.bfloat16)


def find_rows(p, segment, turn, seg_row, start_o):
    own = jnp.broadcast_to(segment[pl.ds(p.row * p.depth + p.z, 1), :].astype(jnp.float32), (16, LEN))
    lane = lax.broadcasted_iota(jnp.int32, (16, LEN), 1)
    ahead = pltpu.roll(own, LEN - BLOCK + 1, 1)
    found = (own == ahead) & (lane <= LEN - BLOCK)
    start = jnp.min(jnp.where(found, lane.astype(jnp.float32), 2.0 * LEN), axis=1, keepdims=True)
    start_o[...] = jnp.broadcast_to(start[:8].astype(jnp.int32), start_o.shape)

    def step(i, _):
        at = pl.ds(pl.multiple_of(i * CHUNK, CHUNK), CHUNK)
        apart = lax.broadcasted_iota(jnp.int32, (CHUNK, LEN), 1) - lax.broadcasted_iota(jnp.int32, (CHUNK, LEN), 0) - i * CHUNK
        apart = apart.astype(jnp.float32) - start[0:1, 0:1]
        turn[at, 0:LEN] = jnp.where((apart == 0.0) | (apart == -1.0 * LEN), 1.0, 0.0).astype(jnp.bfloat16)
        return 0

    lax.fori_loop(0, LEN // CHUNK, step, 0)
    seg_row[...] = contract(own.astype(jnp.bfloat16), turn[:, 0:LEN], 1, 1)


def turn_rows(turn, source, result):
    def step(i, _):
        at = pl.ds(pl.multiple_of(i * CHUNK, CHUNK), CHUNK)
        result[at, :] = contract(turn[at, 0:LEN], source[...], 1, 0).astype(jnp.bfloat16)
        return 0

    lax.fori_loop(0, LEN // CHUNK, step, 0)


def forward_kernel(
    chips, depth,
    tokens_in, cot_in, qkv_in, out_in, up_in, down_in, segment,
    bias_query, bias_value, bias_out, gain_attn, shift_attn, bias_down, gain_ffn, shift_ffn, bias_up,
    output_o, two_o, two_low_o, qkv_o, context_o, normed_o, hidden_low_o, active_o, slope_o,
    wqkv_o, wout_o, wup_o, wdown_o, tokens_o, logsum, factor, sums, seg_row, vecs, start_o,
    tokens, cot, s_qkv, s_out, s_up, s_down, w_qkv, w_out, w_up, w_down,
    qkv, context, bias, hidden, hidden_low, normed, active, slope, two_low, output, down_flat,
    load, store, z_send, z_recv, ring_sent, ring_recv, core_sent, core_recv,
):
    p = Place(chips, depth)
    rows, model = tokens.shape
    pairs = HEADS // 2
    loads = [
        pltpu.make_async_copy(src, dst, load.at[i])
        for i, (src, dst) in enumerate(
            ((qkv_in, s_qkv.at[p.z]), (out_in, s_out.at[p.z]), (up_in, s_up.at[p.z]), (down_in, down_flat), (tokens_in, two_low), (cot_in, output))
        )
    ]
    for item in loads:
        item.start()
    sems = (z_send, z_recv, ring_sent, ring_recv, core_sent, core_recv)
    g_qkv, g_out, g_up, g_down = (
        Gather(p, i, staged, full, sems)
        for i, (staged, full) in enumerate(((s_qkv, w_qkv), (s_out, w_out), (s_up, w_up), (s_down, w_down)))
    )
    stores = []

    def put(src, dst):
        copy = pltpu.make_async_copy(src, dst, store.at[len(stores)])
        copy.start()
        stores.append(copy)

    p.meet()
    loads[0].wait()
    g_qkv.open()
    find_rows(p, segment, active, seg_row, start_o)
    loads[4].wait()
    turn_rows(active, two_low, tokens)
    put(tokens, tokens_o)
    for i in (1, 2, 3, 5):
        loads[i].wait()
    s_down[p.z] = down_flat[...].astype(jnp.float32).T.astype(jnp.bfloat16)
    g_qkv.relay(0)
    g_qkv.relay(1)
    g_out.open()
    g_up.open()
    g_qkv.relay(2)
    g_qkv.start_ring()
    for i in range(active.shape[1] // model):
        vecs[9 + i : 10 + i, :] = bias_up[i * model : (i + 1) * model].reshape(1, model)
    for i, vector in enumerate((bias_query, None, bias_value, bias_out, gain_attn, shift_attn, bias_down, gain_ffn, shift_ffn)):
        vecs[i : i + 1, :] = jnp.zeros((1, model), jnp.float32) if vector is None else vector[...].reshape(1, model)
    g_out.relay(0)
    g_up.relay(0)
    fill_bias(seg_row, bias)
    g_out.relay(1)
    g_up.relay(1)
    g_down.open()
    g_out.relay(2)
    for hop in range(1, p.hops):
        g_qkv.advance(hop)
    g_out.start_ring()
    turn_rows(active, output, cot)
    g_up.relay(2)
    g_up.start_ring()
    g_qkv.advance(p.hops)
    for hop in range(p.hops + 1):
        g_qkv.mate_has(hop)
    put(w_qkv, wqkv_o)

    def project(step, _):
        tile, at = step % 3, pl.ds(pl.multiple_of(step // 3 * CHUNK, CHUNK), CHUNK)
        cols = pl.ds(pl.multiple_of(tile * model, model), model)
        got = contract(tokens[at, :], w_qkv[:, cols], 1, 0) + vecs[pl.ds(tile, 1), :]
        got = got * jnp.where(tile == 0, HEAD_DIM ** (-0.5), 1.0)
        qkv[at, cols] = got.astype(jnp.bfloat16)

        @pl.when(step == 2 * (rows // CHUNK))
        def _():
            for hop in range(1, p.hops):
                g_out.advance(hop)

        return 0

    lax.fori_loop(0, 3 * (rows // CHUNK), project, 0)
    put(qkv, qkv_o)

    def up_next():
        for hop in range(1, p.hops):
            g_up.advance(hop)
        g_down.start_ring()

    def attend_first(pair, _):
        attend_pair(qkv, bias, context, logsum, model, 0, pair)

        for part in range(3):

            @pl.when(pair == part)
            def _(part=part):
                g_down.relay(part)

        if UP_AT < pairs:

            @pl.when(pair == UP_AT)
            def _():
                up_next()

        return 0

    lax.fori_loop(0, pairs, attend_first, 0)

    def attend_second(pair, _):
        attend_pair(qkv, bias, context, logsum, model, 1, pair)

        if UP_AT >= pairs:

            @pl.when(pair == UP_AT - pairs)
            def _():
                up_next()

        return 0

    lax.fori_loop(0, pairs, attend_second, 0)
    put(context, context_o)
    g_out.advance(p.hops)
    for hop in range(p.hops + 1):
        g_out.mate_has(hop)
    put(w_out, wout_o)

    def first_norm(step, _):
        at = pl.ds(pl.multiple_of(step * CHUNK, CHUNK), CHUNK)
        resid = contract(context[at, :], w_out[...], 1, 0) + vecs[3:4, :] + tokens[at, :].astype(jnp.float32)
        centre = resid - row_mean(resid)
        scale = lax.rsqrt(row_mean(centre * centre) + norm_eps)
        unit = centre * scale
        normed[at, :] = unit.astype(jnp.bfloat16)
        factor[at, :] = jnp.broadcast_to(scale, (CHUNK, 128))
        value = unit * vecs[4:5, :] + vecs[5:6, :]
        hidden[at, :] = value + vecs[6:7, :]
        hidden_low[at, :] = value.astype(jnp.bfloat16)
        return 0

    lax.fori_loop(0, rows // CHUNK, first_norm, 0)
    put(normed, normed_o)
    put(hidden_low, hidden_low_o)
    g_up.advance(p.hops)
    for hop in range(p.hops + 1):
        g_up.mate_has(hop)
    put(w_up, wup_o)
    tiles = active.shape[1] // model
    steps = tiles * (rows // CHUNK)

    def widen(step, _):
        tile, at = step % tiles, pl.ds(pl.multiple_of(step // tiles * CHUNK, CHUNK), CHUNK)
        cols = pl.ds(pl.multiple_of(tile * model, model), model)
        value = contract(hidden_low[at, :], w_up[:, cols], 1, 0) + vecs[pl.ds(9 + tile, 1), :]
        act, grade = gelu_parts(value)
        active[at, cols] = act.astype(jnp.bfloat16)
        slope[at, cols] = grade.astype(jnp.bfloat16)

        @pl.when(step == steps * DOWN_AT // 16)
        def _():
            for hop in range(1, p.hops):
                g_down.advance(hop)

        return 0

    lax.fori_loop(0, steps, widen, 0)
    put(active, active_o)
    put(slope, slope_o)
    deep = 2 * g_down.rows

    def narrow(chip):
        span = pl.ds(pl.multiple_of(chip * deep, deep), deep)

        def step_rows(step, _):
            at = pl.ds(pl.multiple_of(step * CHUNK, CHUNK), CHUNK)
            hidden[at, :] += contract(active[at, span], w_down[span, :], 1, 0)
            return 0

        lax.fori_loop(0, rows // CHUNK, step_rows, 0)

    for hop in range(p.hops):
        g_down.mate_has(hop)
        for way in range(1 if hop == 0 else 2):
            if hop == p.hops - 1 and way == 1:
                g_down.advance(p.hops)
            narrow(p.chip_at(p.pos + hop if way else p.pos - hop))
    g_down.mate_has(p.hops)
    put(w_down, wdown_o)
    narrow(p.chip_at(p.pos + p.hops))
    sums[...] = jnp.zeros_like(sums)

    def second_norm(step, _):
        at = pl.ds(pl.multiple_of(step * CHUNK, CHUNK), CHUNK)
        resid = hidden[at, :]
        centre = resid - row_mean(resid)
        scale = lax.rsqrt(row_mean(centre * centre) + norm_eps)
        unit = centre * scale
        output[at, :] = (unit * vecs[7:8, :] + vecs[8:9, :]).astype(jnp.bfloat16)
        coming = cot[at, :].astype(jnp.float32)
        inner = coming * vecs[7:8, :]
        both = scale * (inner - row_mean(inner) - unit * row_mean(inner * unit))
        hidden[at, :] = both
        two_low[at, :] = both.astype(jnp.bfloat16)
        sums[0:1, :] += jnp.sum(coming * unit, axis=0, keepdims=True)
        sums[1:2, :] += jnp.sum(coming, axis=0, keepdims=True)
        sums[2:3, :] += jnp.sum(both, axis=0, keepdims=True)
        return 0

    lax.fori_loop(0, rows // CHUNK, second_norm, 0)
    put(output, output_o)
    put(hidden, two_o)
    put(two_low, two_low_o)
    for gather in (g_qkv, g_out, g_up, g_down):
        gather.finish()
    for copy in stores:
        copy.wait()


def forward(chips, depth, tokens, cotangent, w_qkv, w_out, w_up, w_down, segment, vectors):
    rows, model = tokens.shape
    low, full = jnp.bfloat16, jnp.float32
    weights = (w_qkv, w_out, w_up, w_down)
    whole = [(2 * chips * w.shape[0], depth * w.shape[1]) for w in weights]
    wide = whole[2][1]
    shape = jax.ShapeDtypeStruct
    outs = [
        shape((rows, model), low), shape((rows, model), full), shape((rows, model), low),
        shape((rows, 3 * model), low), shape((rows, model), low), shape((rows, model), low),
        shape((rows, model), low), shape((rows, wide), low), shape((rows, wide), low),
        *(shape(size, low) for size in whole),
        shape((rows, model), low), shape((HEADS, rows), full), shape((rows, 128), full), shape((8, model), full),
        shape((16, rows), full), shape((16, model), full), shape((8, 128), jnp.int32),
    ]
    hops = chips // 2
    return pl.pallas_call(
        functools.partial(forward_kernel, chips, depth),
        out_shape=outs,
        in_specs=[ANY] * 6 + [VMEM] * (1 + len(vectors)),
        out_specs=[ANY] * 14 + [VMEM] * 6,
        scratch_shapes=[
            pltpu.VMEM((rows, model), low), pltpu.VMEM((rows, model), low),
            *(pltpu.VMEM((depth, *w.shape), low) for w in weights),
            *(pltpu.VMEM(size, low) for size in whole),
            pltpu.VMEM((rows, 3 * model), low), pltpu.VMEM((rows, model), low), pltpu.VMEM((BLOCK, BLOCK), full),
            pltpu.VMEM((rows, model), full), pltpu.VMEM((rows, model), low), pltpu.VMEM((rows, model), low),
            pltpu.VMEM((rows, wide), low), pltpu.VMEM((rows, wide), low),
            pltpu.VMEM((rows, model), low), pltpu.VMEM((rows, model), low), pltpu.VMEM(w_down.shape[::-1], low),
            pltpu.SemaphoreType.DMA((6,)), pltpu.SemaphoreType.DMA((14,)),
            pltpu.SemaphoreType.DMA((4, 2, depth)), pltpu.SemaphoreType.DMA((4, depth)),
            pltpu.SemaphoreType.DMA((4, 2, hops)), pltpu.SemaphoreType.DMA((4, 2, hops)),
            pltpu.SemaphoreType.DMA((4, 2 * hops + 1)), pltpu.SemaphoreType.DMA((4, 2 * hops + 1)),
        ],
        compiler_params=pltpu.CompilerParams(collective_id=0, has_side_effects=True, vmem_limit_bytes=67043328),
        name="forward",
    )(tokens, cotangent, w_qkv, w_out, w_up, w_down.T, segment, *vectors)


VMEM = pl.BlockSpec(memory_space=pltpu.VMEM)


class Reduce:
    def __init__(self, place, index, ring_bufs, line_bufs, result, sems, spans=None, last=True):
        self.p, self.i, self.result, self.last = place, index, result, last
        self.grad, self.other, self.halves, self.fulls = ring_bufs
        self.parts, self.came, self.total = line_bufs
        self.spans = spans or [(0, 0, self.grad.shape[3])]
        self.core_sent, self.core_recv, self.ring_sent, self.ring_recv, self.z_sent, self.z_recv, self.res_sem = sems
        self.half = self.grad.shape[3] // 2

    def pair(self, chip):
        return pltpu.make_async_remote_copy(
            self.grad.at[chip, 1 - self.p.core], self.other.at[chip], self.core_sent.at[self.i, chip], self.core_recv.at[self.i, chip],
            device_id=self.p.mate(), device_id_type=MESH,
        )

    def swap(self):
        for chip in self.p.order():
            self.pair(chip).start()

    def absorb(self, chips):
        for chip in chips:
            self.pair(chip).wait_recv()
            both = self.grad[chip, self.p.core].astype(jnp.float32) + self.other[chip].astype(jnp.float32)
            self.grad[chip, self.p.core] = both.astype(jnp.bfloat16)

    def span(self, hop, way):
        return pl.ds((1 - way) * self.half, self.half) if hop == 1 else slice(None)

    def ring(self, hop, way):
        p = self.p
        dest = p.pos - p.hops + hop - 1 if way else p.pos + p.hops - hop + 1
        return pltpu.make_async_remote_copy(
            self.grad.at[p.chip_at(dest), p.core, :, self.span(hop, way)],
            self.halves.at[way] if hop == 1 else self.fulls.at[way, hop - 2],
            self.ring_sent.at[self.i, way, hop - 1], self.ring_recv.at[self.i, way, hop - 1],
            device_id=p.left() if way else p.right(), device_id_type=MESH,
        )

    def go(self, hop):
        self.ring(hop, 0).start()
        self.ring(hop, 1).start()

    def take(self, hop):
        p = self.p
        for way in range(2):
            self.ring(hop, way).wait_recv()
            chip = p.chip_at(p.pos - p.hops + hop if way else p.pos + p.hops - hop)
            got = self.halves[way] if hop == 1 else self.fulls[way, hop - 2]
            cols = self.span(hop, way)
            both = self.grad[chip, p.core, :, cols].astype(jnp.float32) + got.astype(jnp.float32)
            self.grad[chip, p.core, :, cols] = both.astype(jnp.bfloat16)

    def split(self):
        p = self.p
        self.ring(p.hops, 0).wait_recv()
        self.ring(p.hops, 1).wait_recv()
        last = p.hops - 2
        low = (
            self.grad[p.chip, p.core].astype(jnp.float32)
            + self.fulls[0, last].astype(jnp.float32)
            + self.fulls[1, last].astype(jnp.float32)
        ).astype(jnp.bfloat16)
        wide = self.parts.shape[2]
        for z in range(p.depth):
            for at, real, count in self.spans:
                left, right = max(real, z * wide), min(real + count, (z + 1) * wide)
                if left < right:
                    self.parts[z, :, left - z * wide : right - z * wide] = low[:, at + left - real : at + right - real]

    def line(self, block, way):
        return pltpu.make_async_remote_copy(
            self.parts.at[block], self.came.at[block + 1 - way],
            self.z_sent.at[self.i, way, block], self.z_recv.at[self.i, way, block],
            device_id=self.p.down() if way else self.p.up(), device_id_type=MESH,
        )

    def round(self, turn):
        p = self.p
        for way in range(2):
            far = p.depth - 1 - p.z if way else p.z
            block = turn - far if way else p.depth - 1 - turn + far

            @pl.when(far <= turn)
            def _(far=far, block=block, way=way):
                @pl.when(far > 0)
                def _():
                    self.line(block, way).wait_recv()
                    both = self.parts[block].astype(jnp.float32) + self.came[block + 1 - way].astype(jnp.float32)
                    self.parts[block] = both.astype(jnp.bfloat16)

                self.line(block, way).start()

    def write(self):
        return pltpu.make_async_copy(self.total, self.result, self.res_sem.at[self.i])

    def land(self):
        p = self.p
        self.total[...] = self.parts[p.z].astype(jnp.float32)

        @pl.when(p.z > 0)
        def _():
            self.line(p.z, 0).wait_recv()
            self.total[...] += self.came[p.z + 1].astype(jnp.float32)

        @pl.when(p.z < p.depth - 1)
        def _():
            self.line(p.z, 1).wait_recv()
            self.total[...] += self.came[p.z].astype(jnp.float32)

        self.write().start()

    def finish(self):
        p = self.p
        for chip in range(p.chips):
            self.pair(chip).wait_send()
        for hop in range(1, p.hops + 1):
            for way in range(2):
                self.ring(hop, way).wait_send()
        if not self.last:
            return
        for turn in range(p.depth - 1):
            for way in range(2):
                far = p.depth - 1 - p.z if way else p.z
                block = turn - far if way else p.depth - 1 - turn + far

                @pl.when(far <= turn)
                def _(block=block, way=way):
                    self.line(block, way).wait_send()

        self.write().wait()

    def stages(self):
        def first():
            self.absorb(self.p.order()[:1])
            self.go(1)

        def others():
            self.absorb(self.p.order()[1:])

        def along(hop):
            self.take(hop)
            self.go(hop + 1)

        def begin():
            self.split()
            if self.last:
                self.round(0)

        p = self.p
        return [
            [first, others, *(functools.partial(along, hop) for hop in range(1, p.hops)), begin],
            [*(functools.partial(self.round, turn) for turn in range(1, p.depth - 1)), self.land],
        ]


class Sums:
    def __init__(self, place, sums, mine, pair, plane, line, sems):
        self.p, self.sums, self.mine, self.other, self.plane, self.col = place, sums, mine, pair, plane, line
        self.pair_sent, self.pair_recv, self.plane_sent, self.plane_recv, self.col_sent, self.col_recv = sems

    def pair(self):
        return pltpu.make_async_remote_copy(
            self.mine, self.other, self.pair_sent, self.pair_recv, device_id=self.p.mate(), device_id_type=MESH
        )

    def chip(self, apart, source):
        target = (2 * self.p.chip_at(self.p.pos + apart) + self.p.core, self.p.z)
        return pltpu.make_async_remote_copy(
            self.plane.at[source], self.plane.at[source], self.plane_sent.at[apart], self.plane_recv.at[source],
            device_id=target, device_id_type=MESH,
        )

    def level(self, apart, source):
        target = (self.p.row, (self.p.z + apart) % self.p.depth)
        return pltpu.make_async_remote_copy(
            self.col.at[source], self.col.at[source], self.col_sent.at[apart], self.col_recv.at[source],
            device_id=target, device_id_type=MESH,
        )

    def start(self):
        self.mine[...] = self.sums[...]
        self.pair().start()

    def across(self):
        p = self.p
        self.pair().wait_recv()
        self.plane[p.chip] = self.mine[...] + self.other[...]
        for apart in range(1, p.chips):
            self.chip(apart, p.chip).start()

    def along(self):
        p = self.p
        for apart in range(1, p.chips):
            self.chip(apart, p.chip_at(p.pos + apart)).wait_recv()
        total = self.plane[0]
        for chip in range(1, p.chips):
            total = total + self.plane[chip]
        self.col[p.z] = total
        for apart in range(1, p.depth):
            self.level(apart, p.z).start()

    def land(self, result):
        p = self.p
        for apart in range(1, p.depth):
            self.level(apart, (p.z + apart) % p.depth).wait_recv()
        total = self.col[0]
        for z in range(1, p.depth):
            total = total + self.col[z]
        result[...] = total

    def finish(self):
        p = self.p
        self.pair().wait_send()
        for apart in range(1, p.chips):
            self.chip(apart, p.chip).wait_send()
        for apart in range(1, p.depth):
            self.level(apart, p.z).wait_send()


def backward_kernel(
    chips, depth,
    two_low_in, active_in, wdown_in, slope_in, hidden_low_in, wup_in, two_in, normed_in, factor_in, wout_in, context_in,
    qkv_in, tokens_in, wqkv_in, seg_row, vecs, logsum, sums_in,
    tokens_o, qkv_o, out_o, up_o, down_o, sums_o,
    two_low, active, slope, hidden_low, tiles, acc, normed, factor, w_out, bias, sums,
    *rest,
):
    p = Place(chips, depth)
    rings = [rest[4 * i : 4 * i + 4] for i in range(5)]
    lines = [rest[20 + 3 * i : 23 + 3 * i] for i in range(4)]
    mine, other, plane, col = rest[32:36]
    load, store, core_sent, core_recv, ring_sent, ring_recv, z_sent, z_recv, res_sem = rest[36:45]
    sum_sems = rest[45:51]
    rows, model = two_low.shape
    wide = active.shape[1]
    count = wide // model
    pairs = HEADS // 2
    sems = (core_sent, core_recv, ring_sent, ring_recv, z_sent, z_recv, res_sem)
    late = model - EARLY
    r_qkv, r_out, r_up, r_down = (
        Reduce(p, i, rings[i], lines[i], result, sems, [(t * late, t * model + EARLY, late) for t in range(3)] if i == 0 else None)
        for i, result in enumerate((qkv_o, out_o, up_o, down_o))
    )
    r_early = Reduce(p, 4, rings[4], lines[0], qkv_o, sems, [(t * EARLY, t * model, EARLY) for t in range(3)], False)
    used = []

    def fetch(src, dst):
        copy = pltpu.make_async_copy(src, dst, load.at[len(used)])
        copy.start()
        used.append(copy)
        return copy

    def col_tile(ref, tile):
        return ref.at[:, pl.ds(tile * model, model)]

    got_two_low = fetch(two_low_in, two_low)
    order = p.order()
    deep = wide // p.chips
    spans = [pl.ds(pl.multiple_of(chip * deep, 128), deep) for chip in order]
    got_active = [fetch(active_in.at[:, span], active.at[:, span]) for span in spans]
    got_down = [fetch(wdown_in.at[pl.ds(t * model, model), :], tiles.at[t]) for t in range(count)]
    got_slope = [fetch(col_tile(slope_in, t), col_tile(slope, t)) for t in range(count)]
    got_rest = [
        fetch(src, dst)
        for src, dst in ((hidden_low_in, hidden_low), (two_in, acc), (normed_in, normed), (factor_in, factor), (wout_in, w_out))
    ]
    p.meet_all()

    def weight_grad(reduce, left, right, left_at, tile, skip=0, start=0, width=model):
        piece = 384
        cols = pl.ds(pl.multiple_of(tile * model + start, 128), width)
        got = contract(left[:, pl.ds(pl.multiple_of(skip + left_at * piece, 128), piece)], right[:, cols], 0, 0)
        high = reduce.grad.shape[2]
        cols = pl.ds(pl.multiple_of(tile * width, 128), width)
        for s in range(piece // high):
            row = left_at * (piece // high) + s
            reduce.grad[row // 2, row % 2, :, cols] = got[s * high : (s + 1) * high].astype(jnp.bfloat16)

    got_two_low.wait()
    down_one, down_two = r_down.stages()
    for n, chip in enumerate(order):
        got_active[n].wait()

        def down_grad(step, _, chip=chip):
            weight_grad(r_down, active, two_low, chip * (deep // 384) + step, 0)
            return 0

        lax.fori_loop(0, deep // 384, down_grad, 0)
        r_down.pair(chip).start()
        if n == 1:
            down_one[0]()
    got_qkv = fetch(qkv_in, active.at[:, pl.ds(0, 3 * model)])
    sums[...] = jnp.zeros_like(sums)
    sums[9:10, :] = sums_in[2:3, :]
    sums[10:12, :] = sums_in[0:2, :]
    got_up = []
    for t in range(count):
        got_down[t].wait()
        got_slope[t].wait()
        cols = pl.ds(t * model, model)

        def upward_grad(step, _, t=t, cols=cols):
            at = pl.ds(pl.multiple_of(step * CHUNK, CHUNK), CHUNK)
            got = contract(two_low[at, :], tiles[t], 1, 1) * slope[at, cols].astype(jnp.float32)
            slope[at, cols] = got.astype(jnp.bfloat16)
            sums[5 + t : 6 + t, :] += jnp.sum(got, axis=0, keepdims=True)
            return 0

        lax.fori_loop(0, rows // CHUNK, upward_grad, 0)
        got_up.append(fetch(col_tile(wup_in, t), tiles.at[t]))
        if t == 0:
            down_one[1]()
        if t == DT:
            for stage in down_one[2:-1]:
                stage()
    got_rest[0].wait()

    def up_grad(step, _):
        weight_grad(r_up, hidden_low, slope, step // count, step % count)
        return 0

    lax.fori_loop(0, count * (model // 384), up_grad, 0)
    r_up.swap()
    got_tokens = fetch(tokens_in, hidden_low)
    for item in got_rest[1:] + got_up:
        item.wait()

    def first_norm(step, _):
        at = pl.ds(pl.multiple_of(step * CHUNK, CHUNK), CHUNK)
        whole = acc[at, :]
        for t in range(count):
            whole = whole + contract(slope[at, t * model : (t + 1) * model], tiles[t], 1, 1)
        unit, scale = normed[at, :].astype(jnp.float32), factor[at, 0:1]
        inner = whole * vecs[4:5, :]
        both = scale * (inner - row_mean(inner) - unit * row_mean(inner * unit))
        acc[at, :] = both
        low = both.astype(jnp.bfloat16)
        two_low[at, :] = low
        sums[2:3, :] += jnp.sum(both, axis=0, keepdims=True)
        sums[3:4, :] += jnp.sum(whole * unit, axis=0, keepdims=True)
        sums[4:5, :] += jnp.sum(whole, axis=0, keepdims=True)
        active[at, pl.ds(3 * model, model)] = contract(low, w_out[...], 1, 1).astype(jnp.bfloat16)

        @pl.when(step == FN)
        def _():
            r_up.stages()[0][0]()

        @pl.when(step == rows // CHUNK - 1)
        def _():
            r_up.stages()[0][1]()

        return 0

    lax.fori_loop(0, rows // CHUNK, first_norm, 0)
    got_context = fetch(context_in, slope.at[:, pl.ds(3 * model, model)])
    got_wqkv = [fetch(col_tile(wqkv_in, t), tiles.at[t]) for t in range(3)]
    got_context.wait()

    def out_grad(step, _):
        weight_grad(r_out, slope, two_low, step, 0, 3 * model)
        return 0

    lax.fori_loop(0, model // 384, out_grad, 0)
    r_out.swap()
    fill_bias(seg_row, bias)
    got_qkv.wait()
    out_one, out_two = r_out.stages()

    def pair_back(pair, block):
        at = slice(block * BLOCK, (block + 1) * BLOCK)
        cols = [pl.ds(pl.multiple_of(part * model + pair * 128, 128), 128) for part in range(4)]
        qp, kp, vp, gp = (active[at, col] for col in cols)
        prod = (gp.astype(jnp.float32) * slope[at, cols[3]].astype(jnp.float32)).T
        sum_q = sum_k = sum_v = 0.0
        for head in range(2):
            inner = jnp.sum(prod[head * HEAD_DIM : (head + 1) * HEAD_DIM], axis=0, keepdims=True)
            qh, gh, kh = keep_head(qp, head), keep_head(gp, head), keep_head(kp, head)
            scores = contract(kp, qh, 1, 1)
            if block:
                scores = scores + bias[...]
            prob = jnp.exp(scores - logsum[pl.ds(pair * 2 + head, 1), at])
            raw = (prob * (contract(vp, gh, 1, 1) - inner)).astype(jnp.bfloat16)
            sum_v = sum_v + contract(prob.astype(jnp.bfloat16), gh, 1, 0)
            sum_k = sum_k + contract(raw, qh, 1, 0)
            sum_q = sum_q + contract(raw, kh, 0, 0)
        sum_q = sum_q * HEAD_DIM ** (-0.5)
        for col, got in zip(cols, (sum_q, sum_k, sum_v)):
            slope[at, col] = got.astype(jnp.bfloat16)
        sums[0:1, cols[0]] += jnp.sum(sum_q, axis=0, keepdims=True)
        sums[1:2, cols[0]] += jnp.sum(sum_v, axis=0, keepdims=True)

    early_one = r_early.stages()[0]
    qkv_one, qkv_two = r_qkv.stages()
    up_one, up_two = r_up.stages()
    hooks = {
        (0, 0): out_one[:2],
        (0, 1): down_one[-1:],
        (H_UP // 2, H_UP % 2): up_one[2:-1],
        (1, 1): down_two[:1],
        (2, 0): down_two[1:-1],
        (H_OUT // 2, H_OUT % 2): out_one[2:-1],
        (3, 1): down_two[-1:],
        (4, 0): early_one[:2],
        (4, 1): up_one[-1:],
        (5, 0): [*early_one[2:-1], *out_one[-1:]],
        (5, 1): up_two[:1],
    }

    def attend_back(first, stop):
        def step(pair, _):
            for block in range(2):
                pair_back(pair, block)
                for (when, part), todo in hooks.items():
                    if part == block and first <= when < stop:

                        @pl.when(pair == when)
                        def _(todo=todo):
                            for stage in todo:
                                stage()

            return 0

        lax.fori_loop(first, stop, step, 0)

    def early_grad(step, _):
        weight_grad(r_early, hidden_low, slope, step // 3, step % 3, 0, 0, EARLY)
        return 0

    def late_grad(step, _):
        weight_grad(r_qkv, hidden_low, slope, step // 3, step % 3, 0, EARLY, late)
        return 0

    attend_back(0, EARLY // 128)
    got_tokens.wait()
    lax.fori_loop(0, 3 * (model // 384), early_grad, 0)
    r_early.swap()
    attend_back(EARLY // 128, pairs)
    lax.fori_loop(0, 3 * (model // 384), late_grad, 0)
    r_qkv.swap()
    small = Sums(p, sums, mine, other, plane, col, sum_sems)
    small.start()
    for item in got_wqkv:
        item.wait()

    def token_grad(step, _):
        at = pl.ds(pl.multiple_of(step * CHUNK, CHUNK), CHUNK)
        whole = acc[at, :]
        for t in range(3):
            whole = whole + contract(slope[at, t * model : (t + 1) * model], tiles[t], 1, 1)
        acc[at, :] = whole
        return 0

    half = rows // CHUNK // 4
    lax.fori_loop(0, half, token_grad, 0)
    qkv_one[0]()
    qkv_one[1]()
    small.across()
    for stage in out_two[:1] + up_two[1:-1]:
        stage()
    lax.fori_loop(half, 2 * half, token_grad, 0)
    for stage in qkv_one[2:-1]:
        stage()
    early_one[-1]()
    small.along()
    lax.fori_loop(2 * half, rows // CHUNK, token_grad, 0)
    tokens_out = pltpu.make_async_copy(acc, tokens_o, store.at[0])
    tokens_out.start()
    for stage in out_two[1:-1]:
        stage()
    qkv_one[-1]()
    up_two[-1]()
    out_two[-1]()
    small.land(sums_o)
    for stage in qkv_two:
        stage()
    small.finish()
    for reduce in (r_down, r_up, r_out, r_early, r_qkv):
        reduce.finish()
    tokens_out.wait()


def backward(chips, depth, blocks, ins, vmem_ins):
    rows, model = ins[0].shape
    wide = ins[1].shape[1]
    hops = chips // 2
    low, full = jnp.bfloat16, jnp.float32
    shape, dma = jax.ShapeDtypeStruct, pltpu.SemaphoreType.DMA
    bufs = []
    early = 3 * EARLY
    for high, whole in [(high, depth * across - (0 if i else early)) for i, (high, across) in enumerate(blocks)] + [(blocks[0][0], early)]:
        bufs += [
            pltpu.VMEM((chips, 2, high, whole), low), pltpu.VMEM((chips, high, whole), low),
            pltpu.VMEM((2, high, whole // 2), low), pltpu.VMEM((2, hops - 1, high, whole), low),
        ]
    for high, across in blocks:
        bufs += [pltpu.VMEM((depth, high, across), low), pltpu.VMEM((depth + 1, high, across), low), pltpu.VMEM((high, across), full)]
    return pl.pallas_call(
        functools.partial(backward_kernel, chips, depth),
        out_shape=[shape((rows, model), full), *(shape(size, full) for size in blocks), shape((16, model), full)],
        in_specs=[ANY] * len(ins) + [VMEM] * len(vmem_ins),
        out_specs=[ANY] * 5 + [VMEM],
        scratch_shapes=[
            pltpu.VMEM((rows, model), low), pltpu.VMEM((rows, wide), low), pltpu.VMEM((rows, wide), low),
            pltpu.VMEM((rows, model), low), pltpu.VMEM((wide // model, model, model), low), pltpu.VMEM((rows, model), full),
            pltpu.VMEM((rows, model), low), pltpu.VMEM((rows, 128), full), pltpu.VMEM((model, model), low),
            pltpu.VMEM((BLOCK, BLOCK), full), pltpu.VMEM((16, model), full),
            *bufs,
            pltpu.VMEM((16, model), full), pltpu.VMEM((16, model), full),
            pltpu.VMEM((chips, 16, model), full), pltpu.VMEM((depth, 16, model), full),
            dma((32,)), dma((1,)), dma((5, chips)), dma((5, chips)), dma((5, 2, hops)), dma((5, 2, hops)), dma((4, 2, depth)), dma((4, 2, depth)), dma((4,)),
            dma, dma, dma((chips,)), dma((chips,)), dma((depth,)), dma((depth,)),
        ],
        compiler_params=pltpu.CompilerParams(collective_id=1, has_side_effects=True, vmem_limit_bytes=67043328),
        name="backward",
    )(*ins, *vmem_ins)


def finish_kernel(
    start_in, output_in, tokens_in, qkv_in, out_in, up_in, down_in, sums_in,
    output_o, tokens_o, qkv_o, out_o, up_o, down_o, *rest,
):
    vectors, lines = rest[:9], rest[9:18]
    low, wide, grad, done_low, done, qkv, out, up, down, flipped, sums, load, store = rest[18:]
    rows, model = low.shape
    loads = [
        pltpu.make_async_copy(src, dst, load.at[i])
        for i, (src, dst) in enumerate(
            ((output_in, low), (tokens_in, grad.at[pl.ds(0, rows), :]), (tokens_in.at[pl.ds(0, 32), :], grad.at[pl.ds(rows, 32), :]), (qkv_in, qkv), (out_in, out), (up_in, up), (down_in, down), (sums_in, sums))
        )
    ]
    for item in loads:
        item.start()
    stores = []

    def put(src, dst):
        copy = pltpu.make_async_copy(src, dst, store.at[len(stores)])
        copy.start()
        stores.append(copy)

    start = start_in[0, 0]
    loads[0].wait()

    def widen(i, _):
        at = pl.ds(pl.multiple_of(i * 64, 64), 64)
        wide[at, :] = low[at, :].astype(jnp.float32)
        return 0

    lax.fori_loop(0, rows // 64, widen, 0)
    wide[rows:, :] = wide[0:32, :]

    over = lax.rem(rows - start, 8)
    early = lax.broadcasted_iota(jnp.int32, (8, model), 0) < 8 - over

    def turn(source, result, i):
        for j in range(2):
            at = i * 64 + j * 32
            came = pl.multiple_of(lax.rem(at + rows - start - over, rows), 8)
            field = source[pl.ds(came, 40), :]
            parts = [pltpu.roll(field[8 * k : 8 * k + 8], lax.rem(8 - over, 8), 0) for k in range(5)]
            whole = jnp.concatenate([jnp.where(early, parts[k], parts[k + 1]) for k in range(4)])
            result[pl.ds(pl.multiple_of(at, 32), 32), :] = whole.astype(result.dtype)

    for source, result, dst, waits in ((wide, done_low, output_o, ()), (grad, done, tokens_o, (1, 2))):
        for i in waits:
            loads[i].wait()
        for part in range(4):
            deep = rows // 4

            def step(i, _, source=source, result=result):
                turn(source, result, i)
                return 0

            lax.fori_loop(part * (deep // 64), (part + 1) * (deep // 64), step, 0)
            at = pl.ds(part * deep, deep)
            put(result.at[at, :], dst.at[at, :])
        if not waits:
            for i, (src, dst) in enumerate(((qkv, qkv_o), (out, out_o), (up, up_o))):
                loads[3 + i].wait()
                put(src, dst)
            loads[6].wait()
            flipped[...] = down[...].T
            put(flipped, down_o)
            loads[7].wait()
            for i, (line, vector) in enumerate(zip(lines, vectors)):
                row = i if i < 6 else i + 3
                for j in range(vector.shape[0] // model):
                    line[j * model : (j + 1) * model] = sums[row + j : row + j + 1, :].reshape(model)
                put(line, vector)
    for copy in stores:
        copy.wait()


def finish(start, output, grad_tokens, grads, sums, wide):
    rows, model = output.shape
    low, full = jnp.bfloat16, jnp.float32
    shape = jax.ShapeDtypeStruct
    flipped = grads[3].shape[::-1]
    return pl.pallas_call(
        finish_kernel,
        out_shape=[
            shape((rows, model), low), shape((rows, model), full), *(shape(g.shape, full) for g in grads[:3]), shape(flipped, full),
            *(shape((model,), full) for _ in range(5)), shape((wide,), full), *(shape((model,), full) for _ in range(3)),
        ],
        in_specs=[pl.BlockSpec(memory_space=pltpu.SMEM)] + [ANY] * 7,
        out_specs=[ANY] * 15,
        scratch_shapes=[
            *(pltpu.VMEM((wide if i == 5 else model,), full) for i in range(9)),
            pltpu.VMEM((rows, model), low), pltpu.VMEM((rows + 32, model), full), pltpu.VMEM((rows + 32, model), full),
            pltpu.VMEM((rows, model), low), pltpu.VMEM((rows, model), full), *(pltpu.VMEM(g.shape, full) for g in grads),
            pltpu.VMEM(flipped, full), pltpu.VMEM(sums.shape, full), pltpu.SemaphoreType.DMA((8,)), pltpu.SemaphoreType.DMA((21,)),
        ],
        compiler_params=pltpu.CompilerParams(vmem_limit_bytes=67043328),
        name="finish",
    )(start, output, grad_tokens, *grads, sums)


def per_device(
    tokens,
    segment,
    w_qkv,
    w_out,
    w_up,
    w_down,
    bias_query,
    bias_value,
    bias_out,
    gain_attn,
    shift_attn,
    bias_up,
    bias_down,
    gain_ffn,
    shift_ffn,
    cotangent,
):
    chips, depth = lax.axis_size("row") // 2, lax.axis_size("col")
    (
        output, grad_two, grad_two_low, projected, context, normed_one, hidden_low, active_low, slope,
        attn_qkv, attn_out, ffn_up, ffn_down, turned, logsum, factor_one, sums, seg_row, vecs, start,
    ) = forward(
        chips, depth, tokens, cotangent, w_qkv, w_out, w_up, w_down, segment,
        (bias_query, bias_value, bias_out, gain_attn, shift_attn, bias_down, gain_ffn, shift_ffn, bias_up),
    )
    grad_tokens, *grads, sums = backward(
        chips, depth,
        (w_qkv.shape, w_out.shape, w_up.shape, w_down.shape),
        (
            grad_two_low, active_low, ffn_down, slope, hidden_low, ffn_up, grad_two, normed_one, factor_one, attn_out, context,
            projected, turned, attn_qkv,
        ),
        (seg_row, vecs, logsum, sums),
    )
    done = finish(start, output, grad_tokens, grads, sums, bias_up.shape[0])
    return (*done[:5], done[5].T, *done[6:])


def solution(mesh):
    return jax.shard_map(
        per_device,
        mesh=mesh,
        in_specs=(
            P(("row", "col"), None),
            P(),
            P("row", "col"),
            P("row", "col"),
            P("row", "col"),
            P("row", "col"),
            P(),
            P(),
            P(),
            P(),
            P(),
            P(),
            P(),
            P(),
            P(),
            P(("row", "col"), None),
        ),
        out_specs=(
            P(("row", "col"), None),
            P(("row", "col"), None),
            P("row", "col"),
            P("row", "col"),
            P("row", "col"),
            P("row", "col"),
            P(),
            P(),
            P(),
            P(),
            P(),
            P(),
            P(),
            P(),
            P(),
        ),
        check_vma=False,
    )
```

```python
import functools

import jax
import jax.numpy as jnp
from jax import lax
from jax.experimental import pallas as pl
from jax.experimental.pallas import tpu as pltpu
from jax.sharding import PartitionSpec as P

HEADS = 12
HEAD_DIM = 64
LEN = 1024


norm_eps = 1e-05
masked_score = -1e30


BLOCK = 512


def contract(left, right, left_dim, right_dim):
    return lax.dot_general(
        left, right, (((left_dim,), (right_dim,)), ((), ())), preferred_element_type=jnp.float32
    )


def keep_head(field, head):
    lane = lax.broadcasted_iota(jnp.int32, field.shape, 1)
    keep = (lane < HEAD_DIM) if head == 0 else (lane >= HEAD_DIM)
    return jnp.where(keep, field, jnp.zeros_like(field))


MESH = pl.DeviceIdType.MESH
ANY = pl.BlockSpec(memory_space=pl.ANY)
CHUNK = 256
EARLY = 512
UP_AT = 6
UP_START = 2
DOWN_AT = 8
DT = 2
FN = 1
H_UP = 2
H_OUT = 5


class Place:
    def __init__(self, chips, depth):
        self.chips, self.depth, self.hops = chips, depth, chips // 2
        self.row, self.z = lax.axis_index("row"), lax.axis_index("col")
        self.chip, self.core = self.row // 2, self.row % 2
        across = self.chip % 2
        self.pos = self.chip // 2 + across * (chips - 1 - 2 * (self.chip // 2))

    def chip_at(self, pos):
        pos = (pos + self.chips) % self.chips
        far = pos // (self.chips // 2)
        return 2 * (pos + far * (self.chips - 1 - 2 * pos)) + far

    def order(self):
        apart = [self.hops] + [way * hop for hop in range(self.hops - 1, 0, -1) for way in (1, -1)] + [0]
        return [self.chip_at(self.pos + hop) for hop in apart]

    def right(self):
        return (2 * self.chip_at(self.pos + 1) + self.core, self.z)

    def left(self):
        return (2 * self.chip_at(self.pos - 1) + self.core, self.z)

    def mate(self):
        return (self.row + 1 - 2 * self.core, self.z)

    def up(self):
        return (self.row, self.z + 1)

    def down(self):
        return (self.row, self.z - 1)

    def meet(self):
        barrier = pltpu.get_barrier_semaphore()
        for device in (self.right(), self.left(), self.mate()):
            pl.semaphore_signal(barrier, inc=1, device_id=device, device_id_type=MESH)

        @pl.when(self.z < self.depth - 1)
        def _():
            pl.semaphore_signal(barrier, inc=1, device_id=self.up(), device_id_type=MESH)

        @pl.when(self.z > 0)
        def _():
            pl.semaphore_signal(barrier, inc=1, device_id=self.down(), device_id_type=MESH)

        ends = jnp.where(self.z == 0, 1, 0) + jnp.where(self.z == self.depth - 1, 1, 0)
        pl.semaphore_wait(barrier, 5 - ends)

    def meet_all(self):
        barrier = pltpu.get_barrier_semaphore()
        others = [(2 * self.chip_at(self.pos + apart) + self.core, self.z) for apart in range(1, self.chips)]
        others += [(self.row, (self.z + apart) % self.depth) for apart in range(1, self.depth)]
        for device in [*others, self.mate()]:
            pl.semaphore_signal(barrier, inc=1, device_id=device, device_id_type=MESH)
        pl.semaphore_wait(barrier, self.chips + self.depth - 1)


class Gather:
    def __init__(self, place, index, staged, full, sems):
        self.p, self.i, self.staged, self.full = place, index, staged, full
        self.z_send, self.z_recv, self.ring_sent, self.ring_recv, self.core_sent, self.core_recv = sems
        self.rows, self.half = staged.shape[1], full.shape[1] // 2

    def line(self, source, way, step):
        block = self.staged.at[source]
        return pltpu.make_async_remote_copy(
            block, block, self.z_send.at[self.i, way, step], self.z_recv.at[self.i, source],
            device_id=self.p.down() if way else self.p.up(), device_id_type=MESH,
        )

    def open(self):
        p = self.p

        @pl.when(p.z < p.depth - 1)
        def _():
            self.line(p.z, 0, 0).start()

        @pl.when(p.z > 0)
        def _():
            self.line(p.z, 1, 0).start()

    def relay(self, part):
        p = self.p
        for step in (range(1, 2), range(2, p.depth - 1), range(max(2, p.depth - 1), p.depth))[part]:

            @pl.when(p.z - step >= 0)
            def _(step=step):
                self.line(p.z - step, 0, step).wait_recv()

                @pl.when(p.z < p.depth - 1)
                def _():
                    self.line(p.z - step, 0, step).start()

            @pl.when(p.z + step < p.depth)
            def _(step=step):
                self.line(p.z + step, 1, step).wait_recv()

                @pl.when(p.z > 0)
                def _():
                    self.line(p.z + step, 1, step).start()

        if part == 2:
            rows = pl.ds(pl.multiple_of(p.row * self.rows, self.rows), self.rows)
            self.full[rows, :] = jnp.concatenate([self.staged[z] for z in range(p.depth)], axis=1)

    def line_sent(self):
        p = self.p
        for step in range(p.depth):

            @pl.when((p.z - step >= 0) & (p.z < p.depth - 1))
            def _(step=step):
                self.line(p.z - step, 0, step).wait_send()

            @pl.when((p.z + step < p.depth) & (p.z > 0))
            def _(step=step):
                self.line(p.z + step, 1, step).wait_send()

    def piece(self, hop, way, core):
        p = self.p
        pos = p.pos + hop if way else p.pos - hop
        row = 2 * p.chip_at(pos) + core
        rows = pl.ds(pl.multiple_of(row * self.rows, self.rows), self.rows)
        if hop == p.hops:
            return self.full.at[rows, pl.ds(way * self.half, self.half)]
        return self.full.at[rows, :]

    def ring(self, hop, way):
        p = self.p
        pos = p.pos + hop - 1 if way else p.pos - hop + 1
        row = 2 * p.chip_at(pos) + p.core
        rows = pl.ds(pl.multiple_of(row * self.rows, self.rows), self.rows)
        cols = pl.ds(way * self.half, self.half) if hop == p.hops else slice(None)
        block = self.full.at[rows, cols]
        return pltpu.make_async_remote_copy(
            block, block, self.ring_sent.at[self.i, way, hop - 1], self.ring_recv.at[self.i, way, hop - 1],
            device_id=p.left() if way else p.right(), device_id_type=MESH,
        )

    def landed(self, hop, way):
        block = self.piece(hop, way, self.p.core)
        return pltpu.make_async_remote_copy(
            block, block, self.ring_sent.at[self.i, way, hop - 1], self.ring_recv.at[self.i, way, hop - 1],
            device_id=self.p.left() if way else self.p.right(), device_id_type=MESH,
        )

    def pair(self, hop, way, core):
        block = self.piece(hop, way, core)
        slot = 0 if hop == 0 else 2 * hop - 1 + way
        return pltpu.make_async_remote_copy(
            block, block, self.core_sent.at[self.i, slot], self.core_recv.at[self.i, slot],
            device_id=self.p.mate(), device_id_type=MESH,
        )

    def start_ring(self):
        self.ring(1, 0).start()
        self.ring(1, 1).start()
        self.pair(0, 0, self.p.core).start()

    def advance(self, hop):
        for way in range(2):
            self.landed(hop, way).wait_recv()
            if hop < self.p.hops:
                self.ring(hop + 1, way).start()
            self.pair(hop, way, self.p.core).start()

    def mate_has(self, hop):
        for way in range(1 if hop == 0 else 2):
            self.pair(hop, way, 1 - self.p.core).wait_recv()

    def finish(self):
        self.line_sent()
        self.pair(0, 0, self.p.core).wait_send()
        for hop in range(1, self.p.hops + 1):
            for way in range(2):
                self.ring(hop, way).wait_send()
                self.pair(hop, way, self.p.core).wait_send()


def gelu_parts(value):
    part = 1.0 / (1.0 + jnp.abs(value) * (0.3275911 * 0.5**0.5))
    bell = jnp.exp(value * value * -0.5)
    tail = part * (0.127414796 + part * (-0.142248368 + part * (0.7107068705 + part * (-0.7265760135 + part * 0.5307027145))))
    tail = tail * bell
    below = jnp.where(value >= 0, 1.0 - tail, tail)
    return value * below, below + value * bell * 0.3989422804014327


def row_mean(field):
    return jnp.mean(field, axis=1, keepdims=True)


def fill_bias(seg_row, bias):
    seg_key = seg_row[0:1, BLOCK:]
    seg_query = jnp.broadcast_to(seg_key, (128, BLOCK)).T[:, 0:1]
    bias[...] = jnp.where(seg_query == seg_key, 0.0, masked_score)


def attend_pair(qkv, bias, context, logsum, model, block, pair):
    rows = slice(block * BLOCK, (block + 1) * BLOCK)
    cols = [pl.ds(pl.multiple_of(part * model + pair * 128, 128), 128) for part in range(3)]
    qp, kp, vp = (qkv[rows, col] for col in cols)
    total = 0.0
    for head in range(2):
        scores = contract(keep_head(qp, head), kp, 1, 1)
        if block:
            scores = scores + bias[...]
        peak = jnp.max(scores, axis=1, keepdims=True)
        expo = jnp.exp(scores - peak)
        norm = jnp.sum(expo, axis=1, keepdims=True)
        lse = jnp.broadcast_to(peak + jnp.log(norm), (BLOCK, 128)).T
        logsum[pl.ds(pair * 2 + head, 1), rows] = lse[0:1]
        part = contract(expo.astype(jnp.bfloat16), keep_head(vp, head), 1, 0)
        total = total + part * (1.0 / norm)
    context[rows, cols[0]] = total.astype(jnp.bfloat16)


def find_rows(p, segment, turn, seg_row, start_o):
    own = jnp.broadcast_to(segment[pl.ds(p.row * p.depth + p.z, 1), :].astype(jnp.float32), (16, LEN))
    lane = lax.broadcasted_iota(jnp.int32, (16, LEN), 1)
    ahead = pltpu.roll(own, LEN - BLOCK + 1, 1)
    found = (own == ahead) & (lane <= LEN - BLOCK)
    start = jnp.min(jnp.where(found, lane.astype(jnp.float32), 2.0 * LEN), axis=1, keepdims=True)
    start_o[...] = jnp.broadcast_to(start[:8].astype(jnp.int32), start_o.shape)

    def step(i, _):
        at = pl.ds(pl.multiple_of(i * CHUNK, CHUNK), CHUNK)
        apart = lax.broadcasted_iota(jnp.int32, (CHUNK, LEN), 1) - lax.broadcasted_iota(jnp.int32, (CHUNK, LEN), 0) - i * CHUNK
        apart = apart.astype(jnp.float32) - start[0:1, 0:1]
        turn[at, 0:LEN] = jnp.where((apart == 0.0) | (apart == -1.0 * LEN), 1.0, 0.0).astype(jnp.bfloat16)
        return 0

    lax.fori_loop(0, LEN // CHUNK, step, 0)
    seg_row[...] = contract(own.astype(jnp.bfloat16), turn[:, 0:LEN], 1, 1)


def turn_rows(turn, source, result):
    def step(i, _):
        at = pl.ds(pl.multiple_of(i * CHUNK, CHUNK), CHUNK)
        result[at, :] = contract(turn[at, 0:LEN], source[...], 1, 0).astype(jnp.bfloat16)
        return 0

    lax.fori_loop(0, LEN // CHUNK, step, 0)


def forward_kernel(
    chips, depth,
    tokens_in, cot_in, qkv_in, out_in, up_in, down_in, segment,
    bias_query, bias_value, bias_out, gain_attn, shift_attn, bias_down, gain_ffn, shift_ffn, bias_up,
    output_o, two_o, two_low_o, qkv_o, context_o, normed_o, hidden_low_o, active_o, slope_o,
    wqkv_o, wout_o, wup_o, wdown_o, tokens_o, logsum, factor, sums, seg_row, vecs, start_o,
    tokens, cot, s_qkv, s_out, s_up, s_down, w_qkv, w_out, w_up, w_down,
    qkv, context, bias, hidden, hidden_low, normed, active, slope, two_low, output, down_flat,
    load, store, z_send, z_recv, ring_sent, ring_recv, core_sent, core_recv,
):
    p = Place(chips, depth)
    rows, model = tokens.shape
    pairs = HEADS // 2
    loads = [
        pltpu.make_async_copy(src, dst, load.at[i])
        for i, (src, dst) in enumerate(
            ((qkv_in, s_qkv.at[p.z]), (out_in, s_out.at[p.z]), (up_in, s_up.at[p.z]), (down_in, down_flat), (tokens_in, two_low), (cot_in, output))
        )
    ]
    for item in loads:
        item.start()
    sems = (z_send, z_recv, ring_sent, ring_recv, core_sent, core_recv)
    g_qkv, g_out, g_up, g_down = (
        Gather(p, i, staged, full, sems)
        for i, (staged, full) in enumerate(((s_qkv, w_qkv), (s_out, w_out), (s_up, w_up), (s_down, w_down)))
    )
    stores = []

    def put(src, dst):
        copy = pltpu.make_async_copy(src, dst, store.at[len(stores)])
        copy.start()
        stores.append(copy)

    p.meet()
    loads[0].wait()
    g_qkv.open()
    find_rows(p, segment, active, seg_row, start_o)
    loads[4].wait()
    turn_rows(active, two_low, tokens)
    put(tokens, tokens_o)
    for i in (1, 2, 3, 5):
        loads[i].wait()
    s_down[p.z] = down_flat[...].astype(jnp.float32).T.astype(jnp.bfloat16)
    g_qkv.relay(0)
    g_qkv.relay(1)
    g_out.open()
    g_up.open()
    g_qkv.relay(2)
    g_qkv.start_ring()
    for i in range(active.shape[1] // model):
        vecs[9 + i : 10 + i, :] = bias_up[i * model : (i + 1) * model].reshape(1, model)
    for i, vector in enumerate((bias_query, None, bias_value, bias_out, gain_attn, shift_attn, bias_down, gain_ffn, shift_ffn)):
        vecs[i : i + 1, :] = jnp.zeros((1, model), jnp.float32) if vector is None else vector[...].reshape(1, model)
    g_out.relay(0)
    g_up.relay(0)
    turn_rows(active, output, cot)
    fill_bias(seg_row, bias)
    g_out.relay(1)
    for hop in range(1, p.hops):
        g_qkv.advance(hop)
    g_up.relay(1)
    g_out.relay(2)
    g_out.start_ring()
    g_down.open()
    g_qkv.advance(p.hops)
    for hop in range(p.hops + 1):
        g_qkv.mate_has(hop)
    put(w_qkv, wqkv_o)

    def project(step, _):
        tile, at = step % 3, pl.ds(pl.multiple_of(step // 3 * CHUNK, CHUNK), CHUNK)
        cols = pl.ds(pl.multiple_of(tile * model, model), model)
        got = contract(tokens[at, :], w_qkv[:, cols], 1, 0) + vecs[pl.ds(tile, 1), :]
        got = got * jnp.where(tile == 0, HEAD_DIM ** (-0.5), 1.0)
        qkv[at, cols] = got.astype(jnp.bfloat16)

        @pl.when(step == UP_START)
        def _():
            g_up.relay(2)
            g_up.start_ring()

        @pl.when(step == 2 * (rows // CHUNK))
        def _():
            for hop in range(1, p.hops):
                g_out.advance(hop)

        return 0

    lax.fori_loop(0, 3 * (rows // CHUNK), project, 0)
    put(qkv, qkv_o)

    def up_next():
        for hop in range(1, p.hops):
            g_up.advance(hop)
        g_down.start_ring()

    def attend_first(pair, _):
        attend_pair(qkv, bias, context, logsum, model, 0, pair)

        for part in range(3):

            @pl.when(pair == part)
            def _(part=part):
                g_down.relay(part)

        if UP_AT < pairs:

            @pl.when(pair == UP_AT)
            def _():
                up_next()

        return 0

    lax.fori_loop(0, pairs, attend_first, 0)

    def attend_second(pair, _):
        attend_pair(qkv, bias, context, logsum, model, 1, pair)

        if UP_AT >= pairs:

            @pl.when(pair == UP_AT - pairs)
            def _():
                up_next()

        return 0

    lax.fori_loop(0, pairs, attend_second, 0)
    put(context, context_o)
    g_out.advance(p.hops)
    for hop in range(p.hops + 1):
        g_out.mate_has(hop)
    put(w_out, wout_o)

    def first_norm(step, _):
        at = pl.ds(pl.multiple_of(step * CHUNK, CHUNK), CHUNK)
        resid = contract(context[at, :], w_out[...], 1, 0) + vecs[3:4, :] + tokens[at, :].astype(jnp.float32)
        centre = resid - row_mean(resid)
        scale = lax.rsqrt(row_mean(centre * centre) + norm_eps)
        unit = centre * scale
        normed[at, :] = unit.astype(jnp.bfloat16)
        factor[at, :] = jnp.broadcast_to(scale, (CHUNK, 128))
        value = unit * vecs[4:5, :] + vecs[5:6, :]
        hidden[at, :] = value + vecs[6:7, :]
        hidden_low[at, :] = value.astype(jnp.bfloat16)
        return 0

    lax.fori_loop(0, rows // CHUNK, first_norm, 0)
    put(normed, normed_o)
    put(hidden_low, hidden_low_o)
    g_up.advance(p.hops)
    for hop in range(p.hops + 1):
        g_up.mate_has(hop)
    put(w_up, wup_o)
    tiles = active.shape[1] // model
    steps = tiles * (rows // CHUNK)

    def widen(step, _):
        tile, at = step % tiles, pl.ds(pl.multiple_of(step // tiles * CHUNK, CHUNK), CHUNK)
        cols = pl.ds(pl.multiple_of(tile * model, model), model)
        value = contract(hidden_low[at, :], w_up[:, cols], 1, 0) + vecs[pl.ds(9 + tile, 1), :]
        act, grade = gelu_parts(value)
        active[at, cols] = act.astype(jnp.bfloat16)
        slope[at, cols] = grade.astype(jnp.bfloat16)

        @pl.when(step == steps * DOWN_AT // 16)
        def _():
            for hop in range(1, p.hops):
                g_down.advance(hop)

        return 0

    lax.fori_loop(0, steps, widen, 0)
    put(active, active_o)
    put(slope, slope_o)
    deep = 2 * g_down.rows

    def narrow(chip):
        span = pl.ds(pl.multiple_of(chip * deep, deep), deep)

        def step_rows(step, _):
            at = pl.ds(pl.multiple_of(step * CHUNK, CHUNK), CHUNK)
            hidden[at, :] += contract(active[at, span], w_down[span, :], 1, 0)
            return 0

        lax.fori_loop(0, rows // CHUNK, step_rows, 0)

    for hop in range(p.hops):
        g_down.mate_has(hop)
        for way in range(1 if hop == 0 else 2):
            if hop == p.hops - 1 and way == 1:
                g_down.advance(p.hops)
            narrow(p.chip_at(p.pos + hop if way else p.pos - hop))
    g_down.mate_has(p.hops)
    put(w_down, wdown_o)
    narrow(p.chip_at(p.pos + p.hops))
    sums[...] = jnp.zeros_like(sums)

    def second_norm(step, _):
        at = pl.ds(pl.multiple_of(step * CHUNK, CHUNK), CHUNK)
        resid = hidden[at, :]
        centre = resid - row_mean(resid)
        scale = lax.rsqrt(row_mean(centre * centre) + norm_eps)
        unit = centre * scale
        output[at, :] = (unit * vecs[7:8, :] + vecs[8:9, :]).astype(jnp.bfloat16)
        coming = cot[at, :].astype(jnp.float32)
        inner = coming * vecs[7:8, :]
        both = scale * (inner - row_mean(inner) - unit * row_mean(inner * unit))
        hidden[at, :] = both
        two_low[at, :] = both.astype(jnp.bfloat16)
        sums[0:1, :] += jnp.sum(coming * unit, axis=0, keepdims=True)
        sums[1:2, :] += jnp.sum(coming, axis=0, keepdims=True)
        sums[2:3, :] += jnp.sum(both, axis=0, keepdims=True)
        return 0

    lax.fori_loop(0, rows // CHUNK, second_norm, 0)
    put(output, output_o)
    put(hidden, two_o)
    put(two_low, two_low_o)
    for gather in (g_qkv, g_out, g_up, g_down):
        gather.finish()
    for copy in stores:
        copy.wait()


def forward(chips, depth, tokens, cotangent, w_qkv, w_out, w_up, w_down, segment, vectors):
    rows, model = tokens.shape
    low, full = jnp.bfloat16, jnp.float32
    weights = (w_qkv, w_out, w_up, w_down)
    whole = [(2 * chips * w.shape[0], depth * w.shape[1]) for w in weights]
    wide = whole[2][1]
    shape = jax.ShapeDtypeStruct
    outs = [
        shape((rows, model), low), shape((rows, model), full), shape((rows, model), low),
        shape((rows, 3 * model), low), shape((rows, model), low), shape((rows, model), low),
        shape((rows, model), low), shape((rows, wide), low), shape((rows, wide), low),
        *(shape(size, low) for size in whole),
        shape((rows, model), low), shape((HEADS, rows), full), shape((rows, 128), full), shape((8, model), full),
        shape((16, rows), full), shape((16, model), full), shape((8, 128), jnp.int32),
    ]
    hops = chips // 2
    return pl.pallas_call(
        functools.partial(forward_kernel, chips, depth),
        out_shape=outs,
        in_specs=[ANY] * 6 + [VMEM] * (1 + len(vectors)),
        out_specs=[ANY] * 14 + [VMEM] * 6,
        scratch_shapes=[
            pltpu.VMEM((rows, model), low), pltpu.VMEM((rows, model), low),
            *(pltpu.VMEM((depth, *w.shape), low) for w in weights),
            *(pltpu.VMEM(size, low) for size in whole),
            pltpu.VMEM((rows, 3 * model), low), pltpu.VMEM((rows, model), low), pltpu.VMEM((BLOCK, BLOCK), full),
            pltpu.VMEM((rows, model), full), pltpu.VMEM((rows, model), low), pltpu.VMEM((rows, model), low),
            pltpu.VMEM((rows, wide), low), pltpu.VMEM((rows, wide), low),
            pltpu.VMEM((rows, model), low), pltpu.VMEM((rows, model), low), pltpu.VMEM(w_down.shape[::-1], low),
            pltpu.SemaphoreType.DMA((6,)), pltpu.SemaphoreType.DMA((14,)),
            pltpu.SemaphoreType.DMA((4, 2, depth)), pltpu.SemaphoreType.DMA((4, depth)),
            pltpu.SemaphoreType.DMA((4, 2, hops)), pltpu.SemaphoreType.DMA((4, 2, hops)),
            pltpu.SemaphoreType.DMA((4, 2 * hops + 1)), pltpu.SemaphoreType.DMA((4, 2 * hops + 1)),
        ],
        compiler_params=pltpu.CompilerParams(collective_id=0, has_side_effects=True, vmem_limit_bytes=67043328),
        name="forward",
    )(tokens, cotangent, w_qkv, w_out, w_up, w_down.T, segment, *vectors)


VMEM = pl.BlockSpec(memory_space=pltpu.VMEM)


class Reduce:
    def __init__(self, place, index, ring_bufs, line_bufs, result, sems, spans=None, last=True):
        self.p, self.i, self.result, self.last = place, index, result, last
        self.grad, self.other, self.halves, self.fulls = ring_bufs
        self.parts, self.came, self.total = line_bufs
        self.spans = spans or [(0, 0, self.grad.shape[3])]
        self.core_sent, self.core_recv, self.ring_sent, self.ring_recv, self.z_sent, self.z_recv, self.res_sem = sems
        self.half = self.grad.shape[3] // 2

    def pair(self, chip):
        return pltpu.make_async_remote_copy(
            self.grad.at[chip, 1 - self.p.core], self.other.at[chip], self.core_sent.at[self.i, chip], self.core_recv.at[self.i, chip],
            device_id=self.p.mate(), device_id_type=MESH,
        )

    def swap(self):
        for chip in self.p.order():
            self.pair(chip).start()

    def absorb(self, chips):
        for chip in chips:
            self.pair(chip).wait_recv()
            both = self.grad[chip, self.p.core].astype(jnp.float32) + self.other[chip].astype(jnp.float32)
            self.grad[chip, self.p.core] = both.astype(jnp.bfloat16)

    def span(self, hop, way):
        return pl.ds((1 - way) * self.half, self.half) if hop == 1 else slice(None)

    def ring(self, hop, way):
        p = self.p
        dest = p.pos - p.hops + hop - 1 if way else p.pos + p.hops - hop + 1
        return pltpu.make_async_remote_copy(
            self.grad.at[p.chip_at(dest), p.core, :, self.span(hop, way)],
            self.halves.at[way] if hop == 1 else self.fulls.at[way, hop - 2],
            self.ring_sent.at[self.i, way, hop - 1], self.ring_recv.at[self.i, way, hop - 1],
            device_id=p.left() if way else p.right(), device_id_type=MESH,
        )

    def go(self, hop):
        self.ring(hop, 0).start()
        self.ring(hop, 1).start()

    def take(self, hop):
        p = self.p
        for way in range(2):
            self.ring(hop, way).wait_recv()
            chip = p.chip_at(p.pos - p.hops + hop if way else p.pos + p.hops - hop)
            got = self.halves[way] if hop == 1 else self.fulls[way, hop - 2]
            cols = self.span(hop, way)
            both = self.grad[chip, p.core, :, cols].astype(jnp.float32) + got.astype(jnp.float32)
            self.grad[chip, p.core, :, cols] = both.astype(jnp.bfloat16)

    def split(self):
        p = self.p
        self.ring(p.hops, 0).wait_recv()
        self.ring(p.hops, 1).wait_recv()
        last = p.hops - 2
        low = (
            self.grad[p.chip, p.core].astype(jnp.float32)
            + self.fulls[0, last].astype(jnp.float32)
            + self.fulls[1, last].astype(jnp.float32)
        ).astype(jnp.bfloat16)
        wide = self.parts.shape[2]
        for z in range(p.depth):
            for at, real, count in self.spans:
                left, right = max(real, z * wide), min(real + count, (z + 1) * wide)
                if left < right:
                    self.parts[z, :, left - z * wide : right - z * wide] = low[:, at + left - real : at + right - real]

    def line(self, block, way):
        return pltpu.make_async_remote_copy(
            self.parts.at[block], self.came.at[block + 1 - way],
            self.z_sent.at[self.i, way, block], self.z_recv.at[self.i, way, block],
            device_id=self.p.down() if way else self.p.up(), device_id_type=MESH,
        )

    def round(self, turn):
        p = self.p
        for way in range(2):
            far = p.depth - 1 - p.z if way else p.z
            block = turn - far if way else p.depth - 1 - turn + far

            @pl.when(far <= turn)
            def _(far=far, block=block, way=way):
                @pl.when(far > 0)
                def _():
                    self.line(block, way).wait_recv()
                    both = self.parts[block].astype(jnp.float32) + self.came[block + 1 - way].astype(jnp.float32)
                    self.parts[block] = both.astype(jnp.bfloat16)

                self.line(block, way).start()

    def write(self):
        return pltpu.make_async_copy(self.total, self.result, self.res_sem.at[self.i])

    def land(self):
        p = self.p
        self.total[...] = self.parts[p.z].astype(jnp.float32)

        @pl.when(p.z > 0)
        def _():
            self.line(p.z, 0).wait_recv()
            self.total[...] += self.came[p.z + 1].astype(jnp.float32)

        @pl.when(p.z < p.depth - 1)
        def _():
            self.line(p.z, 1).wait_recv()
            self.total[...] += self.came[p.z].astype(jnp.float32)

        self.write().start()

    def finish(self):
        p = self.p
        for chip in range(p.chips):
            self.pair(chip).wait_send()
        for hop in range(1, p.hops + 1):
            for way in range(2):
                self.ring(hop, way).wait_send()
        if not self.last:
            return
        for turn in range(p.depth - 1):
            for way in range(2):
                far = p.depth - 1 - p.z if way else p.z
                block = turn - far if way else p.depth - 1 - turn + far

                @pl.when(far <= turn)
                def _(block=block, way=way):
                    self.line(block, way).wait_send()

        self.write().wait()

    def stages(self):
        def first():
            self.absorb(self.p.order()[:1])
            self.go(1)

        def others():
            self.absorb(self.p.order()[1:])

        def along(hop):
            self.take(hop)
            self.go(hop + 1)

        def begin():
            self.split()
            if self.last:
                self.round(0)

        p = self.p
        return [
            [first, others, *(functools.partial(along, hop) for hop in range(1, p.hops)), begin],
            [*(functools.partial(self.round, turn) for turn in range(1, p.depth - 1)), self.land],
        ]


class Sums:
    def __init__(self, place, sums, mine, pair, plane, line, sems):
        self.p, self.sums, self.mine, self.other, self.plane, self.col = place, sums, mine, pair, plane, line
        self.pair_sent, self.pair_recv, self.plane_sent, self.plane_recv, self.col_sent, self.col_recv = sems

    def pair(self):
        return pltpu.make_async_remote_copy(
            self.mine, self.other, self.pair_sent, self.pair_recv, device_id=self.p.mate(), device_id_type=MESH
        )

    def chip(self, apart, source):
        target = (2 * self.p.chip_at(self.p.pos + apart) + self.p.core, self.p.z)
        return pltpu.make_async_remote_copy(
            self.plane.at[source], self.plane.at[source], self.plane_sent.at[apart], self.plane_recv.at[source],
            device_id=target, device_id_type=MESH,
        )

    def level(self, apart, source):
        target = (self.p.row, (self.p.z + apart) % self.p.depth)
        return pltpu.make_async_remote_copy(
            self.col.at[source], self.col.at[source], self.col_sent.at[apart], self.col_recv.at[source],
            device_id=target, device_id_type=MESH,
        )

    def start(self):
        self.mine[...] = self.sums[...]
        self.pair().start()

    def across(self):
        p = self.p
        self.pair().wait_recv()
        self.plane[p.chip] = self.mine[...] + self.other[...]
        for apart in range(1, p.chips):
            self.chip(apart, p.chip).start()

    def along(self):
        p = self.p
        for apart in range(1, p.chips):
            self.chip(apart, p.chip_at(p.pos + apart)).wait_recv()
        total = self.plane[0]
        for chip in range(1, p.chips):
            total = total + self.plane[chip]
        self.col[p.z] = total
        for apart in range(1, p.depth):
            self.level(apart, p.z).start()

    def land(self, result):
        p = self.p
        for apart in range(1, p.depth):
            self.level(apart, (p.z + apart) % p.depth).wait_recv()
        total = self.col[0]
        for z in range(1, p.depth):
            total = total + self.col[z]
        result[...] = total

    def finish(self):
        p = self.p
        self.pair().wait_send()
        for apart in range(1, p.chips):
            self.chip(apart, p.chip).wait_send()
        for apart in range(1, p.depth):
            self.level(apart, p.z).wait_send()


def backward_kernel(
    chips, depth,
    two_low_in, active_in, wdown_in, slope_in, hidden_low_in, wup_in, two_in, normed_in, factor_in, wout_in, context_in,
    qkv_in, tokens_in, wqkv_in, seg_row, vecs, logsum, sums_in,
    tokens_o, qkv_o, out_o, up_o, down_o, sums_o,
    two_low, active, slope, hidden_low, tiles, acc, normed, factor, w_out, bias, sums,
    *rest,
):
    p = Place(chips, depth)
    rings = [rest[4 * i : 4 * i + 4] for i in range(5)]
    lines = [rest[20 + 3 * i : 23 + 3 * i] for i in range(4)]
    mine, other, plane, col = rest[32:36]
    load, store, core_sent, core_recv, ring_sent, ring_recv, z_sent, z_recv, res_sem = rest[36:45]
    sum_sems = rest[45:51]
    rows, model = two_low.shape
    wide = active.shape[1]
    count = wide // model
    pairs = HEADS // 2
    sems = (core_sent, core_recv, ring_sent, ring_recv, z_sent, z_recv, res_sem)
    late = model - EARLY
    r_qkv, r_out, r_up, r_down = (
        Reduce(p, i, rings[i], lines[i], result, sems, [(t * late, t * model + EARLY, late) for t in range(3)] if i == 0 else None)
        for i, result in enumerate((qkv_o, out_o, up_o, down_o))
    )
    r_early = Reduce(p, 4, rings[4], lines[0], qkv_o, sems, [(t * EARLY, t * model, EARLY) for t in range(3)], False)
    used = []

    def fetch(src, dst):
        copy = pltpu.make_async_copy(src, dst, load.at[len(used)])
        copy.start()
        used.append(copy)
        return copy

    def col_tile(ref, tile):
        return ref.at[:, pl.ds(tile * model, model)]

    got_two_low = fetch(two_low_in, two_low)
    order = p.order()
    deep = wide // p.chips
    spans = [pl.ds(pl.multiple_of(chip * deep, 128), deep) for chip in order]
    got_active = [fetch(active_in.at[:, span], active.at[:, span]) for span in spans]
    got_down = [fetch(wdown_in.at[pl.ds(t * model, model), :], tiles.at[t]) for t in range(count)]
    got_slope = [fetch(col_tile(slope_in, t), col_tile(slope, t)) for t in range(count)]
    got_rest = [
        fetch(src, dst)
        for src, dst in ((hidden_low_in, hidden_low), (two_in, acc), (normed_in, normed), (factor_in, factor), (wout_in, w_out))
    ]
    p.meet_all()

    def weight_grad(reduce, left, right, left_at, tile, skip=0, start=0, width=model):
        piece = 384
        cols = pl.ds(pl.multiple_of(tile * model + start, 128), width)
        got = contract(left[:, pl.ds(pl.multiple_of(skip + left_at * piece, 128), piece)], right[:, cols], 0, 0)
        high = reduce.grad.shape[2]
        cols = pl.ds(pl.multiple_of(tile * width, 128), width)
        for s in range(piece // high):
            row = left_at * (piece // high) + s
            reduce.grad[row // 2, row % 2, :, cols] = got[s * high : (s + 1) * high].astype(jnp.bfloat16)

    got_two_low.wait()
    down_one, down_two = r_down.stages()
    for n, chip in enumerate(order):
        got_active[n].wait()

        def down_grad(step, _, chip=chip):
            weight_grad(r_down, active, two_low, chip * (deep // 384) + step, 0)
            return 0

        lax.fori_loop(0, deep // 384, down_grad, 0)
        r_down.pair(chip).start()
        if n == 1:
            down_one[0]()
    got_qkv = fetch(qkv_in, active.at[:, pl.ds(0, 3 * model)])
    sums[...] = jnp.zeros_like(sums)
    sums[9:10, :] = sums_in[2:3, :]
    sums[10:12, :] = sums_in[0:2, :]
    got_up = []
    for t in range(count):
        got_down[t].wait()
        got_slope[t].wait()
        cols = pl.ds(t * model, model)

        def upward_grad(step, _, t=t, cols=cols):
            at = pl.ds(pl.multiple_of(step * CHUNK, CHUNK), CHUNK)
            got = contract(two_low[at, :], tiles[t], 1, 1) * slope[at, cols].astype(jnp.float32)
            slope[at, cols] = got.astype(jnp.bfloat16)
            sums[5 + t : 6 + t, :] += jnp.sum(got, axis=0, keepdims=True)
            return 0

        lax.fori_loop(0, rows // CHUNK, upward_grad, 0)
        got_up.append(fetch(col_tile(wup_in, t), tiles.at[t]))
        if t == 0:
            down_one[1]()
        if t == DT:
            for stage in down_one[2:-1]:
                stage()
    got_rest[0].wait()

    def up_grad(step, _):
        weight_grad(r_up, hidden_low, slope, step // count, step % count)
        return 0

    lax.fori_loop(0, count * (model // 384), up_grad, 0)
    r_up.swap()
    got_tokens = fetch(tokens_in, hidden_low)
    for item in got_rest[1:] + got_up:
        item.wait()

    def first_norm(step, _):
        at = pl.ds(pl.multiple_of(step * CHUNK, CHUNK), CHUNK)
        whole = acc[at, :]
        for t in range(count):
            whole = whole + contract(slope[at, t * model : (t + 1) * model], tiles[t], 1, 1)
        unit, scale = normed[at, :].astype(jnp.float32), factor[at, 0:1]
        inner = whole * vecs[4:5, :]
        both = scale * (inner - row_mean(inner) - unit * row_mean(inner * unit))
        acc[at, :] = both
        low = both.astype(jnp.bfloat16)
        two_low[at, :] = low
        sums[2:3, :] += jnp.sum(both, axis=0, keepdims=True)
        sums[3:4, :] += jnp.sum(whole * unit, axis=0, keepdims=True)
        sums[4:5, :] += jnp.sum(whole, axis=0, keepdims=True)
        active[at, pl.ds(3 * model, model)] = contract(low, w_out[...], 1, 1).astype(jnp.bfloat16)

        @pl.when(step == FN)
        def _():
            r_up.stages()[0][0]()

        @pl.when(step == rows // CHUNK - 1)
        def _():
            r_up.stages()[0][1]()

        return 0

    lax.fori_loop(0, rows // CHUNK, first_norm, 0)
    got_context = fetch(context_in, slope.at[:, pl.ds(3 * model, model)])
    got_wqkv = [fetch(col_tile(wqkv_in, t), tiles.at[t]) for t in range(3)]
    got_context.wait()

    def out_grad(step, _):
        weight_grad(r_out, slope, two_low, step, 0, 3 * model)
        return 0

    lax.fori_loop(0, model // 384, out_grad, 0)
    r_out.swap()
    fill_bias(seg_row, bias)
    got_qkv.wait()
    out_one, out_two = r_out.stages()

    def pair_back(pair, block):
        at = slice(block * BLOCK, (block + 1) * BLOCK)
        cols = [pl.ds(pl.multiple_of(part * model + pair * 128, 128), 128) for part in range(4)]
        qp, kp, vp, gp = (active[at, col] for col in cols)
        prod = (gp.astype(jnp.float32) * slope[at, cols[3]].astype(jnp.float32)).T
        sum_q = sum_k = sum_v = 0.0
        for head in range(2):
            inner = jnp.sum(prod[head * HEAD_DIM : (head + 1) * HEAD_DIM], axis=0, keepdims=True)
            qh, gh, kh = keep_head(qp, head), keep_head(gp, head), keep_head(kp, head)
            scores = contract(kp, qh, 1, 1)
            if block:
                scores = scores + bias[...]
            prob = jnp.exp(scores - logsum[pl.ds(pair * 2 + head, 1), at])
            raw = (prob * (contract(vp, gh, 1, 1) - inner)).astype(jnp.bfloat16)
            sum_v = sum_v + contract(prob.astype(jnp.bfloat16), gh, 1, 0)
            sum_k = sum_k + contract(raw, qh, 1, 0)
            sum_q = sum_q + contract(raw, kh, 0, 0)
        sum_q = sum_q * HEAD_DIM ** (-0.5)
        for col, got in zip(cols, (sum_q, sum_k, sum_v)):
            slope[at, col] = got.astype(jnp.bfloat16)
        sums[0:1, cols[0]] += jnp.sum(sum_q, axis=0, keepdims=True)
        sums[1:2, cols[0]] += jnp.sum(sum_v, axis=0, keepdims=True)

    early_one = r_early.stages()[0]
    qkv_one, qkv_two = r_qkv.stages()
    up_one, up_two = r_up.stages()
    hooks = [
        (0, out_one[:2]),
        (1, down_one[-1:]),
        (H_UP, up_one[2:-1]),
        (3, down_two[:1]),
        (4, down_two[1:-1]),
        (H_OUT, out_one[2:-1]),
        (7, down_two[-1:]),
        (8, early_one[:2]),
        (9, up_one[-1:]),
        (10, [*early_one[2:-1], *out_one[-1:]]),
        (11, up_two[:1]),
    ]

    def attend_back(first, stop):
        def step(pair, _):
            for block in range(2):
                pair_back(pair, block)
                for when, todo in hooks:
                    if when % 2 == block and first <= when // 2 < stop:

                        @pl.when(pair == when // 2)
                        def _(todo=todo):
                            for stage in todo:
                                stage()

            return 0

        lax.fori_loop(first, stop, step, 0)

    def early_grad(step, _):
        weight_grad(r_early, hidden_low, slope, step // 3, step % 3, 0, 0, EARLY)
        return 0

    def late_grad(step, _):
        weight_grad(r_qkv, hidden_low, slope, step // 3, step % 3, 0, EARLY, late)
        return 0

    attend_back(0, EARLY // 128)
    got_tokens.wait()
    lax.fori_loop(0, 3 * (model // 384), early_grad, 0)
    r_early.swap()
    attend_back(EARLY // 128, pairs)
    lax.fori_loop(0, 3 * (model // 384), late_grad, 0)
    r_qkv.swap()
    small = Sums(p, sums, mine, other, plane, col, sum_sems)
    small.start()
    for item in got_wqkv:
        item.wait()

    def token_grad(step, _):
        at = pl.ds(pl.multiple_of(step * CHUNK, CHUNK), CHUNK)
        whole = acc[at, :]
        for t in range(3):
            whole = whole + contract(slope[at, t * model : (t + 1) * model], tiles[t], 1, 1)
        acc[at, :] = whole
        return 0

    half = rows // CHUNK // 4
    lax.fori_loop(0, half, token_grad, 0)
    qkv_one[0]()
    qkv_one[1]()
    small.across()
    for stage in out_two[:1] + up_two[1:-1]:
        stage()
    lax.fori_loop(half, 2 * half, token_grad, 0)
    for stage in qkv_one[2:-1]:
        stage()
    early_one[-1]()
    small.along()
    lax.fori_loop(2 * half, rows // CHUNK, token_grad, 0)
    tokens_out = pltpu.make_async_copy(acc, tokens_o, store.at[0])
    tokens_out.start()
    for stage in out_two[1:-1]:
        stage()
    qkv_one[-1]()
    up_two[-1]()
    out_two[-1]()
    small.land(sums_o)
    for stage in qkv_two:
        stage()
    small.finish()
    for reduce in (r_down, r_up, r_out, r_early, r_qkv):
        reduce.finish()
    tokens_out.wait()


def backward(chips, depth, blocks, ins, vmem_ins):
    rows, model = ins[0].shape
    wide = ins[1].shape[1]
    hops = chips // 2
    low, full = jnp.bfloat16, jnp.float32
    shape, dma = jax.ShapeDtypeStruct, pltpu.SemaphoreType.DMA
    bufs = []
    early = 3 * EARLY
    for high, whole in [(high, depth * across - (0 if i else early)) for i, (high, across) in enumerate(blocks)] + [(blocks[0][0], early)]:
        bufs += [
            pltpu.VMEM((chips, 2, high, whole), low), pltpu.VMEM((chips, high, whole), low),
            pltpu.VMEM((2, high, whole // 2), low), pltpu.VMEM((2, hops - 1, high, whole), low),
        ]
    for high, across in blocks:
        bufs += [pltpu.VMEM((depth, high, across), low), pltpu.VMEM((depth + 1, high, across), low), pltpu.VMEM((high, across), full)]
    return pl.pallas_call(
        functools.partial(backward_kernel, chips, depth),
        out_shape=[shape((rows, model), full), *(shape(size, full) for size in blocks), shape((16, model), full)],
        in_specs=[ANY] * len(ins) + [VMEM] * len(vmem_ins),
        out_specs=[ANY] * 5 + [VMEM],
        scratch_shapes=[
            pltpu.VMEM((rows, model), low), pltpu.VMEM((rows, wide), low), pltpu.VMEM((rows, wide), low),
            pltpu.VMEM((rows, model), low), pltpu.VMEM((wide // model, model, model), low), pltpu.VMEM((rows, model), full),
            pltpu.VMEM((rows, model), low), pltpu.VMEM((rows, 128), full), pltpu.VMEM((model, model), low),
            pltpu.VMEM((BLOCK, BLOCK), full), pltpu.VMEM((16, model), full),
            *bufs,
            pltpu.VMEM((16, model), full), pltpu.VMEM((16, model), full),
            pltpu.VMEM((chips, 16, model), full), pltpu.VMEM((depth, 16, model), full),
            dma((32,)), dma((1,)), dma((5, chips)), dma((5, chips)), dma((5, 2, hops)), dma((5, 2, hops)), dma((4, 2, depth)), dma((4, 2, depth)), dma((4,)),
            dma, dma, dma((chips,)), dma((chips,)), dma((depth,)), dma((depth,)),
        ],
        compiler_params=pltpu.CompilerParams(collective_id=1, has_side_effects=True, vmem_limit_bytes=67043328),
        name="backward",
    )(*ins, *vmem_ins)


def finish_kernel(
    start_in, output_in, tokens_in, qkv_in, out_in, up_in, down_in, sums_in,
    output_o, tokens_o, qkv_o, out_o, up_o, down_o, *rest,
):
    vectors, lines = rest[:9], rest[9:18]
    low, wide, grad, done_low, done, qkv, out, up, down, flipped, sums, load, store = rest[18:]
    rows, model = low.shape
    loads = [
        pltpu.make_async_copy(src, dst, load.at[i])
        for i, (src, dst) in enumerate(
            ((output_in, low), (tokens_in, grad.at[pl.ds(0, rows), :]), (tokens_in.at[pl.ds(0, 32), :], grad.at[pl.ds(rows, 32), :]), (qkv_in, qkv), (out_in, out), (up_in, up), (down_in, down), (sums_in, sums))
        )
    ]
    for item in loads:
        item.start()
    stores = []

    def put(src, dst):
        copy = pltpu.make_async_copy(src, dst, store.at[len(stores)])
        copy.start()
        stores.append(copy)

    start = start_in[0, 0]
    loads[0].wait()

    def widen(i, _):
        at = pl.ds(pl.multiple_of(i * 64, 64), 64)
        wide[at, :] = low[at, :].astype(jnp.float32)
        return 0

    lax.fori_loop(0, rows // 64, widen, 0)
    wide[rows:, :] = wide[0:32, :]

    over = lax.rem(rows - start, 8)
    early = lax.broadcasted_iota(jnp.int32, (8, model), 0) < 8 - over

    def turn(source, result, i):
        for j in range(2):
            at = i * 64 + j * 32
            came = pl.multiple_of(lax.rem(at + rows - start - over, rows), 8)
            field = source[pl.ds(came, 40), :]
            parts = [pltpu.roll(field[8 * k : 8 * k + 8], lax.rem(8 - over, 8), 0) for k in range(5)]
            whole = jnp.concatenate([jnp.where(early, parts[k], parts[k + 1]) for k in range(4)])
            result[pl.ds(pl.multiple_of(at, 32), 32), :] = whole.astype(result.dtype)

    for source, result, dst, waits in ((wide, done_low, output_o, ()), (grad, done, tokens_o, (1, 2))):
        for i in waits:
            loads[i].wait()
        for part in range(4):
            deep = rows // 4

            def step(i, _, source=source, result=result):
                turn(source, result, i)
                return 0

            lax.fori_loop(part * (deep // 64), (part + 1) * (deep // 64), step, 0)
            at = pl.ds(part * deep, deep)
            put(result.at[at, :], dst.at[at, :])
        if not waits:
            for i, (src, dst) in enumerate(((qkv, qkv_o), (out, out_o), (up, up_o))):
                loads[3 + i].wait()
                put(src, dst)
            loads[6].wait()
            flipped[...] = down[...].T
            put(flipped, down_o)
            loads[7].wait()
            for i, (line, vector) in enumerate(zip(lines, vectors)):
                row = i if i < 6 else i + 3
                for j in range(vector.shape[0] // model):
                    line[j * model : (j + 1) * model] = sums[row + j : row + j + 1, :].reshape(model)
                put(line, vector)
    for copy in stores:
        copy.wait()


def finish(start, output, grad_tokens, grads, sums, wide):
    rows, model = output.shape
    low, full = jnp.bfloat16, jnp.float32
    shape = jax.ShapeDtypeStruct
    flipped = grads[3].shape[::-1]
    return pl.pallas_call(
        finish_kernel,
        out_shape=[
            shape((rows, model), low), shape((rows, model), full), *(shape(g.shape, full) for g in grads[:3]), shape(flipped, full),
            *(shape((model,), full) for _ in range(5)), shape((wide,), full), *(shape((model,), full) for _ in range(3)),
        ],
        in_specs=[pl.BlockSpec(memory_space=pltpu.SMEM)] + [ANY] * 7,
        out_specs=[ANY] * 15,
        scratch_shapes=[
            *(pltpu.VMEM((wide if i == 5 else model,), full) for i in range(9)),
            pltpu.VMEM((rows, model), low), pltpu.VMEM((rows + 32, model), full), pltpu.VMEM((rows + 32, model), full),
            pltpu.VMEM((rows, model), low), pltpu.VMEM((rows, model), full), *(pltpu.VMEM(g.shape, full) for g in grads),
            pltpu.VMEM(flipped, full), pltpu.VMEM(sums.shape, full), pltpu.SemaphoreType.DMA((8,)), pltpu.SemaphoreType.DMA((21,)),
        ],
        compiler_params=pltpu.CompilerParams(vmem_limit_bytes=67043328),
        name="finish",
    )(start, output, grad_tokens, *grads, sums)


def per_device(
    tokens,
    segment,
    w_qkv,
    w_out,
    w_up,
    w_down,
    bias_query,
    bias_value,
    bias_out,
    gain_attn,
    shift_attn,
    bias_up,
    bias_down,
    gain_ffn,
    shift_ffn,
    cotangent,
):
    chips, depth = lax.axis_size("row") // 2, lax.axis_size("col")
    (
        output, grad_two, grad_two_low, projected, context, normed_one, hidden_low, active_low, slope,
        attn_qkv, attn_out, ffn_up, ffn_down, turned, logsum, factor_one, sums, seg_row, vecs, start,
    ) = forward(
        chips, depth, tokens, cotangent, w_qkv, w_out, w_up, w_down, segment,
        (bias_query, bias_value, bias_out, gain_attn, shift_attn, bias_down, gain_ffn, shift_ffn, bias_up),
    )
    grad_tokens, *grads, sums = backward(
        chips, depth,
        (w_qkv.shape, w_out.shape, w_up.shape, w_down.shape),
        (
            grad_two_low, active_low, ffn_down, slope, hidden_low, ffn_up, grad_two, normed_one, factor_one, attn_out, context,
            projected, turned, attn_qkv,
        ),
        (seg_row, vecs, logsum, sums),
    )
    done = finish(start, output, grad_tokens, grads, sums, bias_up.shape[0])
    return (*done[:5], done[5].T, *done[6:])


def solution(mesh):
    return jax.shard_map(
        per_device,
        mesh=mesh,
        in_specs=(
            P(("row", "col"), None),
            P(),
            P("row", "col"),
            P("row", "col"),
            P("row", "col"),
            P("row", "col"),
            P(),
            P(),
            P(),
            P(),
            P(),
            P(),
            P(),
            P(),
            P(),
            P(("row", "col"), None),
        ),
        out_specs=(
            P(("row", "col"), None),
            P(("row", "col"), None),
            P("row", "col"),
            P("row", "col"),
            P("row", "col"),
            P("row", "col"),
            P(),
            P(),
            P(),
            P(),
            P(),
            P(),
            P(),
            P(),
            P(),
        ),
        check_vma=False,
    )
```
